128 devices in a mesh: blk: 8 (over x, core), row: 16 (over z, y).
Axes of the slice: x: 4, y: 4, z: 4, core: 2. Of those that a mesh axis runs over, the one named last changes fastest.
Arguments:
- fibers: bfloat16 [17408, 65536], P(('blk', 'row')), may hold values from -6 to 6
- factor_b: bfloat16 [65536, 256], P('blk'), may hold values from -0.625 to 0.625
- factor_c: bfloat16 [4096, 256], replicated, may hold values from -0.625 to 0.625
- mode2_idx: int32 [17408], P(('blk', 'row')), may hold values from 0 to 8191
- mode3_idx: int32 [17408], P(('blk', 'row')), may hold values from 0 to 4095
- sample_wt: int32 [17408], P(('blk', 'row')), may hold values from 1 to 8
- counts: int32 [128], P(('blk', 'row')), may hold values from 34 to 136, as said below
Outputs:
- factor_new: bfloat16 [65536, 256], P('row')
- leverage: bfloat16 [65536], P('row')
The draws below stay inside these ranges and needn't reach their ends.
Inputs may be any that keep to these rules, and one draw needn't show every extreme that they name: `counts`: slot s of a device holds a sample when s is under that device's count; other slots carry no sample. The busiest device has all 136 slots live. A sample on blk index b has mode-2 coordinate b * 8192 + mode2_idx.
All inputs are finite; a program needn't handle non-finite values.
Results may differ from the reference program's by a relative error of at most 0.0056.
Values may be sent and summed in bfloat16 or wider, within the bound.
A program may use at most 192 MiB of HBM per device.

```python
import jax
import jax.numpy as jnp
from jax import lax

R = 256
J = 65536
K = 4096
CAP = 136
ROWS = 65536
JB = 8192
SLOTS = 17408
N_BLK = 8
N_ROW = 16


def draw_counts(key, part):
    key_rank, key_spread, key_pick = jax.random.split(key, 3)
    order = jax.random.permutation(key_rank, jnp.arange(N_BLK, dtype=jnp.int32))
    level = N_BLK - 1 + 2 * order
    spread = jax.random.randint(key_spread, (N_BLK, N_ROW), 12, 17)
    pick = jax.random.randint(key_pick, (), 0, N_ROW)
    owner_ids = jnp.arange(N_BLK, dtype=jnp.int32)[:, None]
    row_ids = jnp.arange(N_ROW, dtype=jnp.int32)[None, :]
    forced = (owner_ids == jnp.argmax(order)) & (row_ids == pick)
    spread = jnp.where(forced, 16, spread)
    counts = CAP * level[:, None] * spread // (48 * (N_BLK - 1))
    return counts.reshape(-1).astype(jnp.int32)


def with_ends(entries, own_key, smallest, top_value):
    longest = entries.shape.index(max(entries.shape))
    spots = []
    for shift in (0, 1):
        where = [jax.random.randint(jax.random.fold_in(own_key, axis), (), 0, length) for axis, length in enumerate(entries.shape)]
        where[longest] = (where[longest] + shift) % entries.shape[longest]
        spots.append(tuple(where))
    return entries.at[spots[0]].set(smallest).at[spots[1]].set(top_value)


def levels(own_key, extent, shards, least, high):
    def one(dim, blocks):
        heights = jax.random.uniform(jax.random.fold_in(jax.random.fold_in(own_key, 6), dim), (blocks,), jnp.float32, least / len(shards), high / len(shards))
        return jnp.repeat(jnp.exp(heights), extent[dim] // blocks).reshape((-1,) + (1,) * (len(extent) - dim - 1))

    factor_of = one(*shards[0])
    for cut in shards[1:]:
        factor_of = factor_of * one(*cut)
    return factor_of


def gaussian(stream_key, extent, scale, most, cuts=(), kind=jnp.bfloat16):
    result = jax.random.normal(stream_key, extent, jnp.float32) * scale
    if len(cuts) > 0:
        result = levels(stream_key, extent, cuts, -0.22, 0.18) * result
    return jnp.clip(result, min=-most, max=most).astype(kind)


def setup_inputs(seed: int = 0) -> dict:
    splits = jax.random.split(jax.random.key(seed), 8)
    return {
        "fibers": gaussian(splits[0], (SLOTS, ROWS), 1.0, 6.0, ((0, 128),)),
        "factor_b": gaussian(splits[1], (J, R), 0.1, 0.625, ((0, 8),)),
        "factor_c": gaussian(splits[2], (K, R), 0.1, 0.625),
        "mode2_idx": with_ends(jax.random.randint(splits[3], (SLOTS,), 0, JB), jax.random.fold_in(splits[3], 1), 0, JB - 1).astype(jnp.int32),
        "mode3_idx": with_ends(jax.random.randint(splits[4], (SLOTS,), 0, K), jax.random.fold_in(splits[4], 1), 0, K - 1).astype(jnp.int32),
        "sample_wt": with_ends(jax.random.randint(splits[5], (SLOTS,), 1, 9), jax.random.fold_in(splits[5], 1), 1, 8).astype(jnp.int32),
        "counts": draw_counts(jax.random.fold_in(splits[7], 71), 0),
    }


ridge_share = 0.05

def build_rows(factor_b, factor_c, row_b, mode3_idx, sample_wt, live):
    product = factor_b[row_b].astype(jnp.float32) * factor_c[mode3_idx].astype(jnp.float32)
    kr_rows = lax.optimization_barrier(product.astype(jnp.bfloat16))
    scale = jnp.where(live, sample_wt.astype(jnp.float32), jnp.float32(0.0))
    weighted = (scale[:, None] * kr_rows.astype(jnp.float32)).astype(jnp.bfloat16)
    return (kr_rows, weighted)

def contract_rows(left, right):
    return lax.dot_general(left.astype(jnp.float32), right.astype(jnp.float32), (((0,), (0,)), ((), ())), preferred_element_type=jnp.float32)

def inverse_of(matrix, ridge):
    width = matrix.shape[0]
    identity = jnp.eye(width, dtype=jnp.float32)
    shifted = matrix + ridge * (jnp.trace(matrix) / width) * identity
    lower = jnp.linalg.cholesky(shifted)
    return jax.scipy.linalg.cho_solve((lower, True), identity)

def leverage_of(factor, hinverse, scale):
    wide = factor.astype(jnp.float32)
    quad = jnp.sum(jnp.dot(wide, hinverse, precision=lax.Precision.HIGHEST) * wide, axis=1)
    return (scale * quad).astype(jnp.bfloat16)

def reference(fibers, factor_b, factor_c, mode2_idx, mode3_idx, sample_wt, counts):
    slot = jnp.arange(SLOTS, dtype=jnp.int32)
    device = slot // CAP
    owner = slot // (N_ROW * CAP)
    live = slot % CAP < counts[device]
    row_b = (owner * JB + mode2_idx).astype(jnp.int32)
    kr_rows, weighted = build_rows(factor_b, factor_c, row_b, mode3_idx, sample_wt, live)
    gram = contract_rows(weighted, kr_rows)
    gram_inv = inverse_of(gram, ridge_share)
    rhs = contract_rows(fibers, weighted)
    factor = jnp.dot(rhs, gram_inv, precision=lax.Precision.HIGHEST).astype(jnp.bfloat16)
    hmat = contract_rows(factor, factor)
    hinverse = inverse_of(hmat, 0.0)
    leverage = leverage_of(factor, hinverse, ROWS / R)
    return (factor, leverage)
```

```python
import jax
import jax.numpy as jnp
from jax import lax
from jax.experimental import pallas as pl
from jax.experimental.pallas import tpu as pltpu
from jax.sharding import PartitionSpec as P

ridge_share = 0.05
MESH = pl.DeviceIdType.MESH
F32 = jnp.float32
BF16 = jnp.bfloat16

ORDER = ((0, 1, 2), (1, 2, 0), (2, 0, 1))
R0 = (0, 96, 176)
RC = (96, 80, 80)
STEPS = (2, 1, 3, 0)
SUB = 512


def block_order():
    seen, order, marks = set(), [], []

    def add(color, d1, d2):
        for d3 in range(4):
            off = [0, 0, 0]
            off[ORDER[color][0]], off[ORDER[color][1]], off[ORDER[color][2]] = d1, d2, d3
            if tuple(off) not in seen:
                seen.add(tuple(off))
                order.append(tuple(off))

    for d2 in STEPS:
        for group in ((2,), (1, 3), (0,)):
            for d1 in group:
                for color in range(3):
                    add(color, d1, d2)
            marks.append(len(order))
    return order, marks


BLOCKS, MARKS = block_order()
PACK = 5


def block_at(t, me):
    code = jnp.int32(0)
    for g in range(0, 64, PACK):
        word = 0
        for j, (dx, dy, dz) in enumerate(BLOCKS[g:g + PACK]):
            word += (dx + 4 * dy + 16 * dz) << (6 * j)
        code = jnp.where(t // PACK == g // PACK, jnp.int32(word), code)
    code = lax.shift_right_logical(code, 6 * (t % PACK)) % 64
    return ((me[0] + code % 4) % 4, (me[1] + code // 4 % 4) % 4, (me[2] + code // 16) % 4)


def position():
    b, r = lax.axis_index("blk"), lax.axis_index("row")
    return (b // 2, r % 4, r // 4), b % 2


def device(coord, core):
    return {"blk": 2 * coord[0] + core, "row": 4 * coord[2] + coord[1]}


def shifted(me, axis, by):
    out = list(me)
    out[axis] = (me[axis] + by) % 4
    return tuple(out)


def reduce_kernel(fib, wt_own, out, fo, fp, wt_far, part, r1, r2, r3, tot,
                  fo_sem, fs_sem, fr_sem, w_sem, s1, v1, s2, v2, s3, v3):
    me, core = position()
    peers = [device(shifted(me, a, s), core) for a in range(3) for s in (1, 3)]
    partner = device(me, 1 - core)
    barrier = pltpu.get_barrier_semaphore()
    for p in peers + [partner]:
        pl.semaphore_signal(barrier, inc=1, device_id=p, device_id_type=MESH)
    pl.semaphore_wait(barrier, 7)

    def column(t, k):
        x, y, z = block_at(t, me)
        return pl.multiple_of((4 * z + y) * 4096 + (2 * x + k) * SUB, SUB)

    def local_copy(t):
        return pltpu.make_async_copy(fib.at[:, pl.ds(column(t, core), SUB)], fo.at[t], fo_sem.at[t])

    def far_copy(t):
        return pltpu.make_async_remote_copy(
            fib.at[:, pl.ds(column(t, 1 - core), SUB)], fp.at[t], fs_sem.at[t], fr_sem.at[t],
            device_id=partner, device_id_type=MESH)

    wt_copy = pltpu.make_async_remote_copy(
        wt_own, wt_far, w_sem.at[0], w_sem.at[1], device_id=partner, device_id_type=MESH)
    wt_copy.start()

    @pl.loop(0, 64)
    def _(t):
        local_copy(t).start()
        far_copy(t).start()

    wt_copy.wait()

    def compute(lo, hi):
        @pl.loop(lo, hi)
        def _(t):
            local_copy(t).wait()
            far_copy(t).wait_recv()
            x, y, z = block_at(t, me)
            acc = jnp.dot(wt_own[...], fo[t], preferred_element_type=F32)
            acc += jnp.dot(wt_far[...], fp[t], preferred_element_type=F32)
            part[x, y, z] = acc.astype(BF16)

    def rank(c):
        return pl.ds(R0[c], RC[c])

    def place(c, i1, i2, i3):
        at = [None] * 3
        at[ORDER[c][0]], at[ORDER[c][1]], at[ORDER[c][2]] = i1, i2, i3
        return tuple(at)

    def half_of(kind, d):
        return d if kind < 2 else 1 - d

    def dest_step(kind, d):
        return 2 if kind == 0 else (1, 3)[d]

    def slab1(c, d1, e, h):
        i1 = (me[ORDER[c][0]] + d1) % 4
        i2 = (me[ORDER[c][1]] + e) % 4
        return place(c, i1, i2, pl.ds(2 * h, 2)) + (rank(c), slice(None))

    def msg1(kind, d, i, c):
        if kind == 1:
            src = r1.at[0, d, i, :, rank(c)]
        else:
            src = part.at[slab1(c, dest_step(kind, d), STEPS[i], half_of(kind, d))]
        return pltpu.make_async_remote_copy(
            src, r1.at[kind, d, i, :, rank(c)], s1.at[kind, d, i, c], v1.at[kind, d, i, c],
            device_id=device(shifted(me, ORDER[c][0], (1, 3)[d]), core), device_id_type=MESH)

    def slab2(c, e, h):
        return slab1(c, 0, e, h)

    def msg2(kind, d, c):
        if kind == 1:
            src = r2.at[0, d, :, rank(c)]
        else:
            src = part.at[slab2(c, dest_step(kind, d), half_of(kind, d))]
        return pltpu.make_async_remote_copy(
            src, r2.at[kind, d, :, rank(c)], s2.at[kind, d, c], v2.at[kind, d, c],
            device_id=device(shifted(me, ORDER[c][1], (1, 3)[d]), core), device_id_type=MESH)

    def lanes(h):
        return pl.ds(h * (SUB // 2), SUB // 2)

    def msg3(kind, d, c):
        if kind == 1:
            src = r3.at[0, d, rank(c)]
        else:
            f = (me[ORDER[c][2]] + dest_step(kind, d)) % 4
            src = tot.at[f, rank(c), lanes(half_of(kind, d))]
        return pltpu.make_async_remote_copy(
            src, r3.at[kind, d, rank(c)], s3.at[kind, d, c], v3.at[kind, d, c],
            device_id=device(shifted(me, ORDER[c][2], (1, 3)[d]), core), device_id_type=MESH)

    def rows16(c, body):
        @pl.loop(0, RC[c] // 16)
        def _(j):
            body(pl.ds(pl.multiple_of(R0[c] + 16 * j, 16), 16))

    def forward1(d, i, c):
        msg1(0, d, i, c).wait_recv()
        at = slab1(c, (1, 3)[d], STEPS[i], d)

        def body(rows):
            mine = part[at[:3] + (rows, slice(None))].astype(F32)
            r1[0, d, i, :, rows] = (r1[0, d, i, :, rows].astype(F32) + mine).astype(BF16)

        rows16(c, body)
        msg1(1, d, i, c).start()

    def finish1(i, c):
        for d in range(2):
            msg1(2, d, i, c).wait_recv()
        for d in range(2):
            msg1(1, d, i, c).wait_recv()
        for h in range(2):
            at = slab1(c, 0, STEPS[i], h)

            def body(rows):
                total = (r1[1, h, i, :, rows].astype(F32) + r1[2, 1 - h, i, :, rows].astype(F32)
                         + part[at[:3] + (rows, slice(None))].astype(F32))
                if STEPS[i] == 0:
                    tot[pl.ds(2 * h, 2), rows] = total
                else:
                    part[at[:3] + (rows, slice(None))] = total.astype(BF16)

            rows16(c, body)

    def forward2(d, c):
        msg2(0, d, c).wait_recv()
        at = slab2(c, (1, 3)[d], d)

        def body(rows):
            mine = part[at[:3] + (rows, slice(None))].astype(F32)
            r2[0, d, :, rows] = (r2[0, d, :, rows].astype(F32) + mine).astype(BF16)

        rows16(c, body)
        msg2(1, d, c).start()

    compute(0, MARKS[0])
    for c in range(3):
        for d in range(2):
            msg1(0, d, 0, c).start()
    compute(MARKS[0], MARKS[1])
    for c in range(3):
        for d in range(2):
            msg1(2, d, 0, c).start()
    compute(MARKS[1], 64)

    for i in range(4):
        for c in range(3):
            for d in range(2):
                forward1(d, i, c)
        if i < 3:
            for kind in (0, 2):
                for c in range(3):
                    for d in range(2):
                        msg1(kind, d, i + 1, c).start()
        for c in range(3):
            finish1(i, c)
            if i == 0:
                for d in range(2):
                    msg2(0, d, c).start()
            elif i < 3:
                d = i - 1
                msg2(2, d, c).start()
                forward2(d, c)

    for c in range(3):
        for d in range(2):
            msg2(2, d, c).wait_recv()
            msg2(1, d, c).wait_recv()
        for h in range(2):
            def body(rows):
                tot[pl.ds(2 * h, 2), rows] += r2[1, h, :, rows].astype(F32) + r2[2, 1 - h, :, rows].astype(F32)

            rows16(c, body)
        for kind in (0, 2):
            for d in range(2):
                msg3(kind, d, c).start()
    for c in range(3):
        for d in range(2):
            msg3(0, d, c).wait_recv()
            f = (me[ORDER[c][2]] + (1, 3)[d]) % 4

            def body(rows):
                r3[0, d, rows] += tot[f, rows, lanes(d)]

            rows16(c, body)
            msg3(1, d, c).start()
    for c in range(3):
        for d in range(2):
            msg3(2, d, c).wait_recv()
            msg3(1, d, c).wait_recv()
        own = me[ORDER[c][2]]
        for h in range(2):
            def body(rows):
                out[rows, lanes(h)] = tot[own, rows, lanes(h)] + r3[1, h, rows] + r3[2, 1 - h, rows]

            rows16(c, body)

    for c in range(3):
        for kind in range(3):
            for d in range(2):
                for i in range(4):
                    msg1(kind, d, i, c).wait_send()
                msg2(kind, d, c).wait_send()
                msg3(kind, d, c).wait_send()

    @pl.loop(0, 64)
    def _(t):
        far_copy(t).wait_send()


def reduce_rhs(fibers, weighted_t):
    cap = fibers.shape[0]
    dma = pltpu.SemaphoreType.DMA
    vmem = pltpu.VMEM
    return pl.pallas_call(
        reduce_kernel,
        name="reduce_rhs",
        out_shape=jax.ShapeDtypeStruct((256, SUB), F32),
        in_specs=[pl.BlockSpec(memory_space=pl.ANY), pl.BlockSpec(memory_space=pltpu.VMEM)],
        out_specs=pl.BlockSpec(memory_space=pltpu.VMEM),
        scratch_shapes=[
            vmem((64, cap, SUB), BF16), vmem((64, cap, SUB), BF16), vmem((256, cap), BF16),
            vmem((4, 4, 4, 256, SUB), BF16),
            vmem((3, 2, 4, 2, 256, SUB), BF16), vmem((3, 2, 2, 256, SUB), BF16),
            vmem((3, 2, 256, SUB // 2), F32), vmem((4, 256, SUB), F32),
            dma((64,)), dma((64,)), dma((64,)), dma((2,)),
            dma((3, 2, 4, 3)), dma((3, 2, 4, 3)), dma((3, 2, 3)), dma((3, 2, 3)), dma((3, 2, 3)), dma((3, 2, 3)),
        ],
        compiler_params=pltpu.CompilerParams(
            collective_id=0, has_side_effects=True, vmem_limit_bytes=60 * 1024 * 1024),
    )(fibers, weighted_t)


def build_rows(factor_b, factor_c, row_b, mode3_idx, sample_wt, live):
    product = factor_b[row_b].astype(F32) * factor_c[mode3_idx].astype(F32)
    kr_rows = lax.optimization_barrier(product.astype(BF16))
    scale = jnp.where(live, sample_wt.astype(F32), F32(0.0))
    weighted = (scale[:, None] * kr_rows.astype(F32)).astype(BF16)
    return (kr_rows, weighted)


def contract_rows(left, right):
    return lax.dot_general(left, right, (((0,), (0,)), ((), ())), preferred_element_type=F32)


def inverse_of(matrix, ridge):
    width = matrix.shape[0]
    identity = jnp.eye(width, dtype=F32)
    shifted_m = matrix + ridge * (jnp.trace(matrix) / width) * identity
    lower = jnp.linalg.cholesky(shifted_m)
    return jax.scipy.linalg.cho_solve((lower, True), identity)


def local(fibers, factor_b, factor_c, mode2_idx, mode3_idx, sample_wt, counts):
    slot_cap, row_total = fibers.shape
    rank_width = factor_c.shape[1]
    own_live = jnp.arange(slot_cap, dtype=jnp.int32) < counts[0]
    kr_rows, weighted = build_rows(factor_b, factor_c, mode2_idx, mode3_idx, sample_wt, own_live)
    gram = lax.psum(contract_rows(weighted, kr_rows), ("blk", "row"))
    gram_inv = inverse_of(gram, ridge_share)
    rhs_t = reduce_rhs(fibers, weighted.T)
    factor_own = lax.dot_general(
        rhs_t, gram_inv, (((0,), (0,)), ((), ())), precision=lax.Precision.HIGHEST).astype(BF16)
    factor = lax.all_gather(factor_own, "blk", axis=0, tiled=True)
    smat = lax.psum(jnp.dot(rhs_t, rhs_t.T, precision=lax.Precision.HIGHEST), ("blk", "row"))
    sinv = inverse_of(smat, 0.0)
    quad = jnp.sum(jnp.dot(sinv, rhs_t, precision=lax.Precision.HIGHEST) * rhs_t, axis=0)
    lev_own = ((row_total / rank_width) * quad).astype(BF16)
    leverage = lax.all_gather(lev_own, "blk", axis=0, tiled=True)
    return (factor, leverage)


def solution(mesh):
    placed = (
        P(("blk", "row"), None),
        P("blk", None),
        P(),
        P(("blk", "row")),
        P(("blk", "row")),
        P(("blk", "row")),
        P(("blk", "row")),
    )
    return jax.shard_map(
        local, mesh=mesh, in_specs=placed, out_specs=(P("row", None), P("row")), check_vma=False
    )
```

```python
import jax
import jax.numpy as jnp
from jax import lax
from jax.experimental import pallas as pl
from jax.experimental.pallas import tpu as pltpu
from jax.sharding import PartitionSpec as P

ridge_share = 0.05
MESH = pl.DeviceIdType.MESH
F32 = jnp.float32
BF16 = jnp.bfloat16

ORDER = ((0, 1, 2), (1, 2, 0), (2, 0, 1))
R0 = (0, 96, 176)
RC = (96, 80, 80)
STEPS = (2, 1, 3, 0)
SUB = 512


def block_order():
    seen, order, marks = set(), [], []

    def add(color, d1, d2):
        for d3 in range(4):
            off = [0, 0, 0]
            off[ORDER[color][0]], off[ORDER[color][1]], off[ORDER[color][2]] = d1, d2, d3
            if tuple(off) not in seen:
                seen.add(tuple(off))
                order.append(tuple(off))

    for d2 in STEPS:
        for group in ((2,), (1, 3), (0,)):
            for d1 in group:
                for color in range(3):
                    add(color, d1, d2)
            marks.append(len(order))
    return order, marks


BLOCKS, MARKS = block_order()
PACK = 5


def block_at(t, me):
    code = jnp.int32(0)
    for g in range(0, 64, PACK):
        word = 0
        for j, (dx, dy, dz) in enumerate(BLOCKS[g:g + PACK]):
            word += (dx + 4 * dy + 16 * dz) << (6 * j)
        code = jnp.where(t // PACK == g // PACK, jnp.int32(word), code)
    code = lax.shift_right_logical(code, 6 * (t % PACK)) % 64
    return ((me[0] + code % 4) % 4, (me[1] + code // 4 % 4) % 4, (me[2] + code // 16) % 4)


def position():
    b, r = lax.axis_index("blk"), lax.axis_index("row")
    return (b // 2, r % 4, r // 4), b % 2


def device(coord, core):
    return {"blk": 2 * coord[0] + core, "row": 4 * coord[2] + coord[1]}


def shifted(me, axis, by):
    out = list(me)
    out[axis] = (me[axis] + by) % 4
    return tuple(out)


def all_reduce_phases(part, res, near, rx, ry, rz, far_s, far_v, snd, rcv, me, core):
    half = core * 128
    row_x = half + 32 * me[0]
    row_y = row_x + 8 * me[1]
    partner = device(me, 1 - core)

    def rows(at, n):
        return pl.ds(pl.multiple_of(at, 8), n)

    def spread(phase, axis, src_of, dst_of):
        copies = []
        for by in (1, 2, 3):
            to = shifted(me, axis, by)
            copies.append(pltpu.make_async_remote_copy(
                src_of(to[axis]), dst_of(by), snd.at[phase, by - 1], rcv.at[phase, by - 1],
                device_id=device(to, core), device_id_type=MESH))
        return copies

    def pair(slot, src, dst):
        return pltpu.make_async_remote_copy(
            src, dst, far_s.at[slot], far_v.at[slot], device_id=partner, device_id_type=MESH)

    def begin(copies):
        for copy in copies:
            copy.start()

    def arrive(copies):
        for copy in copies:
            copy.wait_recv()

    first = [pair(0, part.at[rows((1 - core) * 128, 128)], near)]
    over_x = spread(0, 0, lambda i: part.at[rows(half + 32 * i, 32)], lambda by: rx.at[by - 1])
    over_y = spread(1, 1, lambda i: part.at[rows(row_x + 8 * i, 8)], lambda by: ry.at[by - 1])
    over_z = spread(2, 2, lambda i: part.at[rows(row_y, 8)], lambda by: rz.at[me[2]])
    back_y = spread(3, 1, lambda i: res.at[rows(row_y, 8)], lambda by: res.at[rows(row_y, 8)])
    back_x = spread(4, 0, lambda i: res.at[rows(row_x, 32)], lambda by: res.at[rows(row_x, 32)])
    last = [pair(1, res.at[rows(half, 128)], res.at[rows(half, 128)])]

    def end_core():
        arrive(first)
        part[rows(half, 128)] += near[...]

    def end_x():
        arrive(over_x)
        part[rows(row_x, 32)] += rx[0] + rx[1] + rx[2]

    def end_y():
        arrive(over_y)
        part[rows(row_y, 8)] += ry[0] + ry[1] + ry[2]

    def end_z():
        arrive(over_z)
        rz[me[2]] = part[rows(row_y, 8)]
        res[rows(row_y, 8)] = (rz[0] + rz[1]) + (rz[2] + rz[3])

    stages = [(first, end_core), (over_x, end_x), (over_y, end_y), (over_z, end_z),
              (back_y, lambda: arrive(back_y)), (back_x, lambda: arrive(back_x)), (last, lambda: arrive(last))]

    def drain():
        for copies, _ in stages:
            for copy in copies:
                copy.wait_send()

    return [(lambda c=copies: begin(c), end) for copies, end in stages], drain


def all_reduce_scratch():
    dma = pltpu.SemaphoreType.DMA
    return [pltpu.VMEM((256, 256), F32), pltpu.VMEM((128, 256), F32), pltpu.VMEM((3, 32, 256), F32),
            pltpu.VMEM((3, 8, 256), F32), pltpu.VMEM((4, 8, 256), F32),
            dma((2,)), dma((2,)), dma((5, 3)), dma((5, 3))]


def greet(peers):
    barrier = pltpu.get_barrier_semaphore()
    for p in peers:
        pl.semaphore_signal(barrier, inc=1, device_id=p, device_id_type=MESH)
    pl.semaphore_wait(barrier, len(peers))


def all_peers(me, core):
    return [device(shifted(me, a, s), core) for a in range(3) for s in (1, 2, 3)] + [device(me, 1 - core)]


def reduce_kernel(fib, wt_own, kr, out, gram, fo, fp, wt_far, part, r1, r2, r3, tot,
                  fo_sem, fs_sem, fr_sem, w_sem, s1, v1, s2, v2, s3, v3, *gram_scratch):
    me, core = position()
    partner = device(me, 1 - core)
    greet(all_peers(me, core))
    gram_phases, gram_drain = all_reduce_phases(gram_scratch[0], gram, *gram_scratch[1:], me, core)

    def gram_step(p):
        gram_phases[p][1]()
        if p < 6:
            gram_phases[p + 1][0]()

    def column(t, k):
        x, y, z = block_at(t, me)
        return pl.multiple_of((4 * z + y) * 4096 + (2 * x + k) * SUB, SUB)

    def local_copy(t):
        return pltpu.make_async_copy(fib.at[:, pl.ds(column(t, core), SUB)], fo.at[t], fo_sem.at[t])

    def far_copy(t):
        return pltpu.make_async_remote_copy(
            fib.at[:, pl.ds(column(t, 1 - core), SUB)], fp.at[t], fs_sem.at[t], fr_sem.at[t],
            device_id=partner, device_id_type=MESH)

    wt_copy = pltpu.make_async_remote_copy(
        wt_own, wt_far, w_sem.at[0], w_sem.at[1], device_id=partner, device_id_type=MESH)
    wt_copy.start()

    @pl.loop(0, 64)
    def _(t):
        local_copy(t).start()
        far_copy(t).start()

    wt_copy.wait()

    def compute(lo, hi):
        @pl.loop(lo, hi)
        def _(t):
            local_copy(t).wait()
            far_copy(t).wait_recv()
            x, y, z = block_at(t, me)
            acc = jnp.dot(wt_own[...], fo[t], preferred_element_type=F32)
            acc += jnp.dot(wt_far[...], fp[t], preferred_element_type=F32)
            part[x, y, z] = acc.astype(BF16)

    def rank(c):
        return pl.ds(R0[c], RC[c])

    def place(c, i1, i2, i3):
        at = [None] * 3
        at[ORDER[c][0]], at[ORDER[c][1]], at[ORDER[c][2]] = i1, i2, i3
        return tuple(at)

    def half_of(kind, d):
        return d if kind < 2 else 1 - d

    def dest_step(kind, d):
        return 2 if kind == 0 else (1, 3)[d]

    def slab1(c, d1, e, h):
        i1 = (me[ORDER[c][0]] + d1) % 4
        i2 = (me[ORDER[c][1]] + e) % 4
        return place(c, i1, i2, pl.ds(2 * h, 2)) + (rank(c), slice(None))

    def msg1(kind, d, i, c):
        if kind == 1:
            src = r1.at[0, d, i, :, rank(c)]
        else:
            src = part.at[slab1(c, dest_step(kind, d), STEPS[i], half_of(kind, d))]
        return pltpu.make_async_remote_copy(
            src, r1.at[kind, d, i, :, rank(c)], s1.at[kind, d, i, c], v1.at[kind, d, i, c],
            device_id=device(shifted(me, ORDER[c][0], (1, 3)[d]), core), device_id_type=MESH)

    def slab2(c, e, h):
        return slab1(c, 0, e, h)

    def msg2(kind, d, c):
        if kind == 1:
            src = r2.at[0, d, :, rank(c)]
        else:
            src = part.at[slab2(c, dest_step(kind, d), half_of(kind, d))]
        return pltpu.make_async_remote_copy(
            src, r2.at[kind, d, :, rank(c)], s2.at[kind, d, c], v2.at[kind, d, c],
            device_id=device(shifted(me, ORDER[c][1], (1, 3)[d]), core), device_id_type=MESH)

    def lanes(h):
        return pl.ds(h * (SUB // 2), SUB // 2)

    def msg3(kind, d, c):
        if kind == 1:
            src = r3.at[0, d, rank(c)]
        else:
            f = (me[ORDER[c][2]] + dest_step(kind, d)) % 4
            src = tot.at[f, rank(c), lanes(half_of(kind, d))]
        return pltpu.make_async_remote_copy(
            src, r3.at[kind, d, rank(c)], s3.at[kind, d, c], v3.at[kind, d, c],
            device_id=device(shifted(me, ORDER[c][2], (1, 3)[d]), core), device_id_type=MESH)

    def rows16(c, body):
        @pl.loop(0, RC[c] // 16)
        def _(j):
            body(pl.ds(pl.multiple_of(R0[c] + 16 * j, 16), 16))

    def forward1(d, i, c):
        msg1(0, d, i, c).wait_recv()
        at = slab1(c, (1, 3)[d], STEPS[i], d)

        def body(rows):
            mine = part[at[:3] + (rows, slice(None))].astype(F32)
            r1[0, d, i, :, rows] = (r1[0, d, i, :, rows].astype(F32) + mine).astype(BF16)

        rows16(c, body)
        msg1(1, d, i, c).start()

    def finish1(i, c):
        for d in range(2):
            msg1(2, d, i, c).wait_recv()
        for d in range(2):
            msg1(1, d, i, c).wait_recv()
        for h in range(2):
            at = slab1(c, 0, STEPS[i], h)

            def body(rows):
                total = (r1[1, h, i, :, rows].astype(F32) + r1[2, 1 - h, i, :, rows].astype(F32)
                         + part[at[:3] + (rows, slice(None))].astype(F32))
                if STEPS[i] == 0:
                    tot[pl.ds(2 * h, 2), rows] = total
                else:
                    part[at[:3] + (rows, slice(None))] = total.astype(BF16)

            rows16(c, body)

    def forward2(d, c):
        msg2(0, d, c).wait_recv()
        at = slab2(c, (1, 3)[d], d)

        def body(rows):
            mine = part[at[:3] + (rows, slice(None))].astype(F32)
            r2[0, d, :, rows] = (r2[0, d, :, rows].astype(F32) + mine).astype(BF16)

        rows16(c, body)
        msg2(1, d, c).start()

    gram_scratch[0][...] = jnp.dot(wt_own[...], kr[...], preferred_element_type=F32)
    gram_phases[0][0]()

    compute(0, MARKS[0])
    for c in range(3):
        for d in range(2):
            msg1(0, d, 0, c).start()
    compute(MARKS[0], MARKS[1])
    for c in range(3):
        for d in range(2):
            msg1(2, d, 0, c).start()
    gram_step(0)
    compute(MARKS[1], 64)

    for i in range(4):
        for c in range(3):
            for d in range(2):
                forward1(d, i, c)
        if i < 3:
            for kind in (0, 2):
                for c in range(3):
                    for d in range(2):
                        msg1(kind, d, i + 1, c).start()
            gram_step(2 * i + 1)
        for c in range(3):
            finish1(i, c)
            if i == 0:
                for d in range(2):
                    msg2(0, d, c).start()
            elif i < 3:
                d = i - 1
                msg2(2, d, c).start()
                forward2(d, c)
        if i < 3:
            gram_step(2 * i + 2)

    for c in range(3):
        for d in range(2):
            msg2(2, d, c).wait_recv()
            msg2(1, d, c).wait_recv()
        for h in range(2):
            def body(rows):
                tot[pl.ds(2 * h, 2), rows] += r2[1, h, :, rows].astype(F32) + r2[2, 1 - h, :, rows].astype(F32)

            rows16(c, body)
        for kind in (0, 2):
            for d in range(2):
                msg3(kind, d, c).start()
    for c in range(3):
        for d in range(2):
            msg3(0, d, c).wait_recv()
            f = (me[ORDER[c][2]] + (1, 3)[d]) % 4

            def body(rows):
                r3[0, d, rows] += tot[f, rows, lanes(d)]

            rows16(c, body)
            msg3(1, d, c).start()
    for c in range(3):
        for d in range(2):
            msg3(2, d, c).wait_recv()
            msg3(1, d, c).wait_recv()
        own = me[ORDER[c][2]]
        for h in range(2):
            def body(rows):
                out[rows, lanes(h)] = tot[own, rows, lanes(h)] + r3[1, h, rows] + r3[2, 1 - h, rows]

            rows16(c, body)

    for c in range(3):
        for kind in range(3):
            for d in range(2):
                for i in range(4):
                    msg1(kind, d, i, c).wait_send()
                msg2(kind, d, c).wait_send()
                msg3(kind, d, c).wait_send()

    @pl.loop(0, 64)
    def _(t):
        far_copy(t).wait_send()

    gram_drain()


def reduce_rhs(fibers, weighted_t, kr_rows):
    cap = fibers.shape[0]
    dma = pltpu.SemaphoreType.DMA
    vmem = pltpu.VMEM
    return pl.pallas_call(
        reduce_kernel,
        name="reduce_rhs",
        out_shape=(jax.ShapeDtypeStruct((256, SUB), F32), jax.ShapeDtypeStruct((256, 256), F32)),
        in_specs=[pl.BlockSpec(memory_space=pl.ANY)] + [pl.BlockSpec(memory_space=pltpu.VMEM)] * 2,
        out_specs=[pl.BlockSpec(memory_space=pltpu.VMEM)] * 2,
        scratch_shapes=[
            vmem((64, cap, SUB), BF16), vmem((64, cap, SUB), BF16), vmem((256, cap), BF16),
            vmem((4, 4, 4, 256, SUB), BF16),
            vmem((3, 2, 4, 2, 256, SUB), BF16), vmem((3, 2, 2, 256, SUB), BF16),
            vmem((3, 2, 256, SUB // 2), F32), vmem((4, 256, SUB), F32),
            dma((64,)), dma((64,)), dma((64,)), dma((2,)),
            dma((3, 2, 4, 3)), dma((3, 2, 4, 3)), dma((3, 2, 3)), dma((3, 2, 3)), dma((3, 2, 3)), dma((3, 2, 3)),
        ] + all_reduce_scratch(),
        compiler_params=pltpu.CompilerParams(
            collective_id=0, has_side_effects=True, vmem_limit_bytes=60 * 1024 * 1024),
    )(fibers, weighted_t, kr_rows)


def build_rows(factor_b, factor_c, row_b, mode3_idx, sample_wt, live):
    product = factor_b[row_b].astype(F32) * factor_c[mode3_idx].astype(F32)
    kr_rows = lax.optimization_barrier(product.astype(BF16))
    scale = jnp.where(live, sample_wt.astype(F32), F32(0.0))
    weighted = (scale[:, None] * kr_rows.astype(F32)).astype(BF16)
    return (kr_rows, weighted)


def dot32(a, b):
    return jnp.dot(a, b, precision=lax.Precision.HIGHEST, preferred_element_type=F32)


def dot16(a, b):
    return jnp.dot(a.astype(BF16), b.astype(BF16), preferred_element_type=F32)


def invert(a_ref, x_ref, r_ref):
    n = a_ref.shape[0]
    row = lax.broadcasted_iota(jnp.int32, (n, n), 0)
    col = lax.broadcasted_iota(jnp.int32, (n, n), 1)
    eye = jnp.where(row == col, F32(1), F32(0))
    a = a_ref[...]
    diag = jnp.where(row == col, a, F32(0))
    s_col = lax.rsqrt(jnp.sum(diag, axis=1, keepdims=True))
    s_row = lax.rsqrt(jnp.sum(diag, axis=0, keepdims=True))
    a_ref[...] = a * s_col * s_row
    bound = jnp.max(jnp.sum(jnp.abs(a_ref[...]), axis=0, keepdims=True))
    alpha = 1.9 / bound
    x_ref[...] = alpha * eye
    r_ref[...] = eye - alpha * a_ref[...]

    def coarse(carry):
        it, _ = carry
        r = r_ref[...]
        x = x_ref[...]
        x_ref[...] = x + dot16(x, r)
        r = dot16(r, r)
        r_ref[...] = r
        return it + 1, jnp.sum(r * r)

    lax.while_loop(lambda c: (c[0] < 24) & (c[1] > 1e-3), coarse, (jnp.int32(0), F32(1e9)))

    def fine(carry):
        it, last, _ = carry
        x = x_ref[...]
        e = (row == col).astype(F32) - dot32(a_ref[...], x)
        size = jnp.sum(e * e)
        reset = (it == 0) & jnp.logical_not(size < 0.25)
        stop = (size < 1e-8) | ((size < 1e-3) & (size > 0.25 * last))

        @pl.when(reset)
        def _():
            x_ref[...] = alpha * (row == col).astype(F32)

        @pl.when(jnp.logical_not(reset))
        def _():
            x_ref[...] = x + dot32(x, e)

        return it + 1, jnp.where(reset, F32(1e30), size), stop.astype(jnp.int32)

    lax.while_loop(lambda c: (c[0] < 80) & (c[2] == 0), fine, (jnp.int32(0), F32(1e30), jnp.int32(0)))
    x_ref[...] = x_ref[...] * s_col * s_row


def solve_kernel(gram, rhs_t, factor, smat, shifted_m, work, inv, res):
    n = gram.shape[0]
    row = lax.broadcasted_iota(jnp.int32, (n, n), 0)
    col = lax.broadcasted_iota(jnp.int32, (n, n), 1)
    g = gram[...]
    mean = jnp.sum(jnp.where(row == col, g, F32(0))) / n
    a = g + jnp.where(row == col, ridge_share * mean, F32(0))
    shifted_m[...] = a
    work[...] = a
    invert(work, inv, res)
    r = rhs_t[...]
    factor[...] = lax.dot_general(
        r, inv[...], (((0,), (0,)), ((), ())), precision=lax.Precision.HIGHEST,
        preferred_element_type=F32).astype(BF16)
    smat[...] = lax.dot_general(
        r, r, (((1,), (1,)), ((), ())), precision=lax.Precision.HIGHEST, preferred_element_type=F32)


def solve_factor(gram, rhs_t):
    square = jax.ShapeDtypeStruct((256, 256), F32)
    return pl.pallas_call(
        solve_kernel, name="solve_factor",
        out_shape=(jax.ShapeDtypeStruct((SUB, 256), BF16), square, square),
        scratch_shapes=[pltpu.VMEM((256, 256), F32)] * 3,
    )(gram, rhs_t)


def gather_kernel(own, smat, factor, ssum, x_s, x_v, c_s, c_v, *scratch):
    me, core = position()
    partner = device(me, 1 - core)
    greet(all_peers(me, core))
    work = scratch[0]
    work[...] = smat[...]
    phases, drain = all_reduce_phases(work, ssum, *scratch[1:], me, core)
    phases[0][0]()

    def block(x, k):
        return factor.at[pl.ds(pl.multiple_of((2 * x + k) * SUB, SUB), SUB)]

    over_x = [pltpu.make_async_remote_copy(
        own, block(me[0], core), x_s.at[by - 1], x_v.at[by - 1],
        device_id=device(shifted(me, 0, by), core), device_id_type=MESH) for by in (1, 2, 3)]
    over_core = [pltpu.make_async_remote_copy(
        own if by == 0 else block((me[0] + 4 - by) % 4, core), block((me[0] + 4 - by) % 4, core),
        c_s.at[by], c_v.at[by], device_id=partner, device_id_type=MESH) for by in range(4)]
    over_core[0].start()
    phases[0][1]()
    phases[1][0]()
    for copy in over_x:
        copy.start()
    factor[pl.ds(pl.multiple_of((2 * me[0] + core) * SUB, SUB), SUB)] = own[...]
    phases[1][1]()
    for p in range(2, 5):
        phases[p][0]()
        phases[p][1]()
    phases[5][0]()
    for by in (1, 3, 2):
        over_x[by - 1].wait_recv()
        over_core[by].start()
    phases[5][1]()
    phases[6][0]()
    phases[6][1]()
    for by in range(4):
        over_core[by].wait_recv()
    for copy in over_x + over_core:
        copy.wait_send()
    drain()


def gather_factor(own, smat):
    dma = pltpu.SemaphoreType.DMA
    vm = pl.BlockSpec(memory_space=pltpu.VMEM)
    return pl.pallas_call(
        gather_kernel, name="gather_factor",
        out_shape=(jax.ShapeDtypeStruct((8 * SUB, 256), BF16), jax.ShapeDtypeStruct((256, 256), F32)),
        in_specs=[vm, vm], out_specs=[vm, vm],
        scratch_shapes=[dma((3,)), dma((3,)), dma((4,)), dma((4,))] + all_reduce_scratch(),
        compiler_params=pltpu.CompilerParams(collective_id=1, has_side_effects=True),
    )(own, smat)


def leverage_kernel(scale, factor, smat, shifted_m, out, lev, work, inv, res):
    work[...] = smat[...]
    invert(work, inv, res)
    a = shifted_m[...]
    hinv = dot32(a, dot32(inv[...], a))
    high = hinv.astype(BF16)
    low = (hinv - high.astype(F32)).astype(BF16)
    ones = jnp.full((8, 256), 1.0, BF16)
    over = (((1,), (1,)), ((), ()))

    @pl.loop(0, 8)
    def _(j):
        at = pl.ds(pl.multiple_of(j * SUB, SUB), SUB)
        f = factor[at]
        out[at] = f
        quad = (jnp.dot(f, high, preferred_element_type=F32) + jnp.dot(f, low, preferred_element_type=F32)) * f.astype(F32)
        q_high = quad.astype(BF16)
        rest = quad - q_high.astype(F32)
        q_mid = rest.astype(BF16)
        q_low = (rest - q_mid.astype(F32)).astype(BF16)
        total = (lax.dot_general(ones, q_high, over, preferred_element_type=F32)
                 + lax.dot_general(ones, q_mid, over, preferred_element_type=F32)
                 + lax.dot_general(ones, q_low, over, preferred_element_type=F32))
        lev[j] = scale * total


def leverage_of(factor, smat, shifted_m, scale):
    rows = factor.shape[0]
    out, lev = pl.pallas_call(
        lambda *refs: leverage_kernel(scale, *refs), name="leverage",
        out_shape=(jax.ShapeDtypeStruct((rows, 256), BF16), jax.ShapeDtypeStruct((rows // SUB, 8, SUB), F32)),
        scratch_shapes=[pltpu.VMEM((256, 256), F32)] * 3,
    )(factor, smat, shifted_m)
    return out, lev[:, 0].reshape(rows).astype(BF16)


def local(fibers, factor_b, factor_c, mode2_idx, mode3_idx, sample_wt, counts):
    slot_cap, row_total = fibers.shape
    rank_width = factor_c.shape[1]
    own_live = jnp.arange(slot_cap, dtype=jnp.int32) < counts[0]
    kr_rows, weighted = build_rows(factor_b, factor_c, mode2_idx, mode3_idx, sample_wt, own_live)
    rhs_t, gram = reduce_rhs(fibers, weighted.T, kr_rows)
    factor_own, smat, shifted_m = solve_factor(gram, rhs_t)
    factor, ssum = gather_factor(factor_own, smat)
    return leverage_of(factor, ssum, shifted_m, row_total / rank_width)


def solution(mesh):
    placed = (
        P(("blk", "row"), None),
        P("blk", None),
        P(),
        P(("blk", "row")),
        P(("blk", "row")),
        P(("blk", "row")),
        P(("blk", "row")),
    )
    return jax.shard_map(
        local, mesh=mesh, in_specs=placed, out_specs=(P("row", None), P("row")), check_vma=False
    )
```

```python
import jax
import jax.numpy as jnp
from jax import lax
from jax.experimental import pallas as pl
from jax.experimental.pallas import tpu as pltpu
from jax.sharding import PartitionSpec as P

ridge_share = 0.05
MESH = pl.DeviceIdType.MESH
F32 = jnp.float32
BF16 = jnp.bfloat16

ORDER = ((0, 1, 2), (1, 2, 0), (2, 0, 1))
R0 = (0, 96, 176)
RC = (96, 80, 80)
STEPS = (2, 1, 3, 0)
SUB = 512


def block_lines(kind, i, color):
    d2 = STEPS[i]
    lines = []
    for d1 in {"across": (2,), "near": (1, 3), "own": (0,)}[kind]:
        for d3 in range(4):
            off = [0, 0, 0]
            off[ORDER[color][0]], off[ORDER[color][1]], off[ORDER[color][2]] = d1, d2, d3
            lines.append(tuple(off))
    return lines


def block_order():
    order, ends = [], {}
    needs = [("across", 0), ("near", 0), ("across", 1), ("near", 1), ("own", 0)]
    for i in (2, 3):
        needs += [("across", i), ("near", i), ("own", i - 1)]
    needs += [("own", 3)]
    for kind, i in needs:
        for color in range(3):
            for off in block_lines(kind, i, color):
                if off not in order:
                    order.append(off)
            ends[kind, i, color] = len(order)
    return order, ends


BLOCKS, ENDS = block_order()
PACK = 5


def block_at(t, me):
    code = jnp.int32(0)
    for g in range(0, 64, PACK):
        word = 0
        for j, (dx, dy, dz) in enumerate(BLOCKS[g:g + PACK]):
            word += (dx + 4 * dy + 16 * dz) << (6 * j)
        code = jnp.where(t // PACK == g // PACK, jnp.int32(word), code)
    code = lax.shift_right_logical(code, 6 * (t % PACK)) % 64
    return ((me[0] + code % 4) % 4, (me[1] + code // 4 % 4) % 4, (me[2] + code // 16) % 4)


def position():
    b, r = lax.axis_index("blk"), lax.axis_index("row")
    return (b // 2, r % 4, r // 4), b % 2


def device(coord, core):
    return {"blk": 2 * coord[0] + core, "row": 4 * coord[2] + coord[1]}


def shifted(me, axis, by):
    out = list(me)
    out[axis] = (me[axis] + by) % 4
    return tuple(out)


def all_reduce_phases(part, res, near, rx, ry, rz, far_s, far_v, snd, rcv, me, core):
    half = core * 128
    row_x = half + 32 * me[0]
    row_y = row_x + 8 * me[1]
    partner = device(me, 1 - core)

    def rows(at, n):
        return pl.ds(pl.multiple_of(at, 8), n)

    def spread(phase, axis, src_of, dst_of):
        copies = []
        for by in (1, 2, 3):
            to = shifted(me, axis, by)
            copies.append(pltpu.make_async_remote_copy(
                src_of(to[axis]), dst_of(by), snd.at[phase, by - 1], rcv.at[phase, by - 1],
                device_id=device(to, core), device_id_type=MESH))
        return copies

    def pair(slot, src, dst):
        return pltpu.make_async_remote_copy(
            src, dst, far_s.at[slot], far_v.at[slot], device_id=partner, device_id_type=MESH)

    def begin(copies):
        for copy in copies:
            copy.start()

    def arrive(copies):
        for copy in copies:
            copy.wait_recv()

    first = [pair(0, part.at[rows((1 - core) * 128, 128)], near)]
    over_x = spread(0, 0, lambda i: part.at[rows(half + 32 * i, 32)], lambda by: rx.at[by - 1])
    over_y = spread(1, 1, lambda i: part.at[rows(row_x + 8 * i, 8)], lambda by: ry.at[by - 1])
    over_z = spread(2, 2, lambda i: part.at[rows(row_y, 8)], lambda by: rz.at[me[2]])
    back_y = spread(3, 1, lambda i: res.at[rows(row_y, 8)], lambda by: res.at[rows(row_y, 8)])
    back_x = spread(4, 0, lambda i: res.at[rows(row_x, 32)], lambda by: res.at[rows(row_x, 32)])
    last = [pair(1, res.at[rows(half, 128)], res.at[rows(half, 128)])]

    def end_core():
        arrive(first)
        part[rows(half, 128)] += near[...]

    def end_x():
        arrive(over_x)
        part[rows(row_x, 32)] += rx[0] + rx[1] + rx[2]

    def end_y():
        arrive(over_y)
        part[rows(row_y, 8)] += ry[0] + ry[1] + ry[2]

    def end_z():
        arrive(over_z)
        rz[me[2]] = part[rows(row_y, 8)]
        res[rows(row_y, 8)] = (rz[0] + rz[1]) + (rz[2] + rz[3])

    stages = [(first, end_core), (over_x, end_x), (over_y, end_y), (over_z, end_z),
              (back_y, lambda: arrive(back_y)), (back_x, lambda: arrive(back_x)), (last, lambda: arrive(last))]

    def drain():
        for copies, _ in stages:
            for copy in copies:
                copy.wait_send()

    return [(lambda c=copies: begin(c), end) for copies, end in stages], drain


def all_reduce_scratch():
    dma = pltpu.SemaphoreType.DMA
    return [pltpu.VMEM((256, 256), F32), pltpu.VMEM((128, 256), F32), pltpu.VMEM((3, 32, 256), F32),
            pltpu.VMEM((3, 8, 256), F32), pltpu.VMEM((4, 8, 256), F32),
            dma((2,)), dma((2,)), dma((5, 3)), dma((5, 3))]


def greet(peers):
    barrier = pltpu.get_barrier_semaphore()
    for p in peers:
        pl.semaphore_signal(barrier, inc=1, device_id=p, device_id_type=MESH)
    pl.semaphore_wait(barrier, len(peers))


def all_peers(me, core):
    return [device(shifted(me, a, s), core) for a in range(3) for s in (1, 2, 3)] + [device(me, 1 - core)]


def reduce_kernel(fib, rows_b, rows_c, scale, out, gram, fo, fp, wt_own, wt_far, part, r1, r2, r3, tot,
                  fo_sem, fs_sem, fr_sem, w_sem, s1, v1, s2, v2, s3, v3, *gram_scratch):
    me, core = position()
    partner = device(me, 1 - core)

    near = [[(me[a] + by) % 4 for by in range(4)] for a in range(3)]
    bases = [near[1][by] * 4096 for by in range(4)], [near[2][by] * 16384 for by in range(4)]

    def column(t, k):
        dx, dy, dz = BLOCKS[t]
        return pl.multiple_of(bases[1][dz] + bases[0][dy] + near[0][dx] * 1024 + k * SUB, SUB)

    def local_copy(t, at):
        return pltpu.make_async_copy(fib.at[:, pl.ds(at, SUB)], fo.at[t], fo_sem.at[t])

    def far_copy(t, at):
        return pltpu.make_async_remote_copy(
            fib.at[:, pl.ds(at, SUB)], fp.at[t], fs_sem.at[t], fr_sem.at[t],
            device_id=partner, device_id_type=MESH)

    wt_copy = pltpu.make_async_remote_copy(
        wt_own, wt_far, w_sem.at[0], w_sem.at[1], device_id=partner, device_id_type=MESH)
    gram_phases, gram_drain = all_reduce_phases(gram_scratch[0], gram, *gram_scratch[1:], me, core)

    def gram_step(p):
        gram_phases[p][1]()
        if p < 6:
            gram_phases[p + 1][0]()

    for t in range(64):
        local_copy(t, column(t, core)).start()

    kr = (rows_b[...].astype(F32) * rows_c[...].astype(F32)).astype(BF16)
    weighted = (scale[...] * kr.astype(F32)).astype(BF16)
    wt_own[...] = weighted.T
    gram_scratch[0][...] = jnp.dot(wt_own[...], kr, preferred_element_type=F32)

    greet(all_peers(me, core))
    wt_copy.start()
    gram_phases[0][0]()

    for t in range(64):
        far_copy(t, column(t, 1 - core)).start()

    wt_copy.wait()

    done = [0]

    def need(kind, i, c):
        lo, hi = done[0], ENDS[kind, i, c]
        if hi <= lo:
            return
        done[0] = hi

        @pl.loop(lo, hi)
        def _(t):
            local_copy(t, 0).wait()
            far_copy(t, 0).wait_recv()
            x, y, z = block_at(t, me)
            acc = jnp.dot(wt_own[...], fo[t], preferred_element_type=F32)
            acc += jnp.dot(wt_far[...], fp[t], preferred_element_type=F32)
            part[x, y, z] = acc.astype(BF16)

    def rank(c):
        return pl.ds(R0[c], RC[c])

    def place(c, i1, i2, i3):
        at = [None] * 3
        at[ORDER[c][0]], at[ORDER[c][1]], at[ORDER[c][2]] = i1, i2, i3
        return tuple(at)

    def half_of(kind, d):
        return d if kind < 2 else 1 - d

    def dest_step(kind, d):
        return 2 if kind == 0 else (1, 3)[d]

    def slab1(c, d1, e, h):
        i1 = (me[ORDER[c][0]] + d1) % 4
        i2 = (me[ORDER[c][1]] + e) % 4
        return place(c, i1, i2, pl.ds(2 * h, 2)) + (rank(c), slice(None))

    def msg1(kind, d, i, c):
        if kind == 1:
            src = r1.at[0, d, i, :, rank(c)]
        else:
            src = part.at[slab1(c, dest_step(kind, d), STEPS[i], half_of(kind, d))]
        return pltpu.make_async_remote_copy(
            src, r1.at[kind, d, i, :, rank(c)], s1.at[kind, d, i, c], v1.at[kind, d, i, c],
            device_id=device(shifted(me, ORDER[c][0], (1, 3)[d]), core), device_id_type=MESH)

    def slab2(c, e, h):
        return slab1(c, 0, e, h)

    def msg2(kind, d, c):
        if kind == 1:
            src = r2.at[0, d, :, rank(c)]
        else:
            src = part.at[slab2(c, dest_step(kind, d), half_of(kind, d))]
        return pltpu.make_async_remote_copy(
            src, r2.at[kind, d, :, rank(c)], s2.at[kind, d, c], v2.at[kind, d, c],
            device_id=device(shifted(me, ORDER[c][1], (1, 3)[d]), core), device_id_type=MESH)

    def lanes(h):
        return pl.ds(h * (SUB // 2), SUB // 2)

    def msg3(kind, d, c):
        if kind == 1:
            src = r3.at[0, d, rank(c)]
        else:
            f = (me[ORDER[c][2]] + dest_step(kind, d)) % 4
            src = tot.at[f, rank(c), lanes(half_of(kind, d))]
        return pltpu.make_async_remote_copy(
            src, r3.at[kind, d, rank(c)], s3.at[kind, d, c], v3.at[kind, d, c],
            device_id=device(shifted(me, ORDER[c][2], (1, 3)[d]), core), device_id_type=MESH)

    def rows16(c, body):
        @pl.loop(0, RC[c] // 16)
        def _(j):
            body(pl.ds(pl.multiple_of(R0[c] + 16 * j, 16), 16))

    def forward1(d, i, c):
        msg1(0, d, i, c).wait_recv()
        at = slab1(c, (1, 3)[d], STEPS[i], d)

        def body(rows):
            mine = part[at[:3] + (rows, slice(None))].astype(F32)
            r1[0, d, i, :, rows] = (r1[0, d, i, :, rows].astype(F32) + mine).astype(BF16)

        rows16(c, body)
        msg1(1, d, i, c).start()

    def finish1(i, c):
        for d in range(2):
            msg1(2, d, i, c).wait_recv()
        for d in range(2):
            msg1(1, d, i, c).wait_recv()
        for h in range(2):
            at = slab1(c, 0, STEPS[i], h)

            def body(rows):
                total = (r1[1, h, i, :, rows].astype(F32) + r1[2, 1 - h, i, :, rows].astype(F32)
                         + part[at[:3] + (rows, slice(None))].astype(F32))
                if STEPS[i] == 0:
                    tot[pl.ds(2 * h, 2), rows] = total
                else:
                    part[at[:3] + (rows, slice(None))] = total.astype(BF16)

            rows16(c, body)

    def forward2(d, c):
        msg2(0, d, c).wait_recv()
        at = slab2(c, (1, 3)[d], d)

        def body(rows):
            mine = part[at[:3] + (rows, slice(None))].astype(F32)
            r2[0, d, :, rows] = (r2[0, d, :, rows].astype(F32) + mine).astype(BF16)

        rows16(c, body)
        msg2(1, d, c).start()

    def send1(kind, i, c):
        need(("across", None, "near")[kind], i, c)
        for d in range(2):
            msg1(kind, d, i, c).start()

    for kind in (0, 2):
        for c in range(3):
            send1(kind, 0, c)
    gram_step(0)

    for i in range(4):
        for c in range(3):
            for d in range(2):
                forward1(d, i, c)
        if i < 3:
            for kind in (0, 2):
                for c in range(3):
                    send1(kind, i + 1, c)
            gram_step(2 * i + 1)
        for c in range(3):
            need("own", i, c)
        for c in range(3):
            finish1(i, c)
            if i == 0:
                for d in range(2):
                    msg2(0, d, c).start()
            elif i < 3:
                d = i - 1
                msg2(2, d, c).start()
                forward2(d, c)
        if i < 3:
            gram_step(2 * i + 2)

    for c in range(3):
        for d in range(2):
            msg2(2, d, c).wait_recv()
            msg2(1, d, c).wait_recv()
        for h in range(2):
            def body(rows):
                tot[pl.ds(2 * h, 2), rows] += r2[1, h, :, rows].astype(F32) + r2[2, 1 - h, :, rows].astype(F32)

            rows16(c, body)
        for kind in (0, 2):
            for d in range(2):
                msg3(kind, d, c).start()
    for c in range(3):
        for d in range(2):
            msg3(0, d, c).wait_recv()
            f = (me[ORDER[c][2]] + (1, 3)[d]) % 4

            def body(rows):
                r3[0, d, rows] += tot[f, rows, lanes(d)]

            rows16(c, body)
            msg3(1, d, c).start()
    for c in range(3):
        for d in range(2):
            msg3(2, d, c).wait_recv()
            msg3(1, d, c).wait_recv()
        own = me[ORDER[c][2]]
        for h in range(2):
            def body(rows):
                out[rows, lanes(h)] = tot[own, rows, lanes(h)] + r3[1, h, rows] + r3[2, 1 - h, rows]

            rows16(c, body)

    for c in range(3):
        for kind in range(3):
            for d in range(2):
                for i in range(4):
                    msg1(kind, d, i, c).wait_send()
                msg2(kind, d, c).wait_send()
                msg3(kind, d, c).wait_send()

    @pl.loop(0, 64)
    def _(t):
        far_copy(t, 0).wait_send()

    gram_drain()


def reduce_rhs(fibers, rows_b, rows_c, scale):
    cap = fibers.shape[0]
    dma = pltpu.SemaphoreType.DMA
    vmem = pltpu.VMEM
    return pl.pallas_call(
        reduce_kernel,
        name="reduce_rhs",
        out_shape=(jax.ShapeDtypeStruct((256, SUB), F32), jax.ShapeDtypeStruct((256, 256), F32)),
        in_specs=[pl.BlockSpec(memory_space=pl.ANY)] + [pl.BlockSpec(memory_space=pltpu.VMEM)] * 3,
        out_specs=[pl.BlockSpec(memory_space=pltpu.VMEM)] * 2,
        scratch_shapes=[
            vmem((64, cap, SUB), BF16), vmem((64, cap, SUB), BF16), vmem((256, cap), BF16), vmem((256, cap), BF16),
            vmem((4, 4, 4, 256, SUB), BF16),
            vmem((3, 2, 4, 2, 256, SUB), BF16), vmem((3, 2, 2, 256, SUB), BF16),
            vmem((3, 2, 256, SUB // 2), F32), vmem((4, 256, SUB), F32),
            dma((64,)), dma((64,)), dma((64,)), dma((2,)),
            dma((3, 2, 4, 3)), dma((3, 2, 4, 3)), dma((3, 2, 3)), dma((3, 2, 3)), dma((3, 2, 3)), dma((3, 2, 3)),
        ] + all_reduce_scratch(),
        compiler_params=pltpu.CompilerParams(
            collective_id=0, has_side_effects=True, vmem_limit_bytes=60 * 1024 * 1024),
    )(fibers, rows_b, rows_c, scale)


def dot32(a, b):
    return jnp.dot(a, b, precision=lax.Precision.HIGHEST, preferred_element_type=F32)


def dot16(a, b):
    return jnp.dot(a.astype(BF16), b.astype(BF16), preferred_element_type=F32)


def invert(a_ref, x_ref, r_ref):
    n = a_ref.shape[0]
    row = lax.broadcasted_iota(jnp.int32, (n, n), 0)
    col = lax.broadcasted_iota(jnp.int32, (n, n), 1)
    eye = jnp.where(row == col, F32(1), F32(0))
    a = a_ref[...]
    diag = jnp.where(row == col, a, F32(0))
    s_col = lax.rsqrt(jnp.sum(diag, axis=1, keepdims=True))
    s_row = lax.rsqrt(jnp.sum(diag, axis=0, keepdims=True))
    a_ref[...] = a * s_col * s_row
    bound = jnp.max(jnp.sum(jnp.abs(a_ref[...]), axis=0, keepdims=True))
    alpha = 1.9 / bound
    x_ref[...] = alpha * eye
    r_ref[...] = eye - alpha * a_ref[...]

    def coarse(carry):
        it, _ = carry
        r = r_ref[...]
        x = x_ref[...]
        x_ref[...] = x + dot16(x, r)
        r = dot16(r, r)
        r_ref[...] = r
        return it + 1, jnp.sum(r * r)

    lax.while_loop(lambda c: (c[0] < 24) & (c[1] > 1e-3), coarse, (jnp.int32(0), F32(1e9)))

    def fine(carry):
        it, last, _ = carry
        x = x_ref[...]
        e = (row == col).astype(F32) - dot32(a_ref[...], x)
        size = jnp.sum(e * e)
        reset = (it == 0) & jnp.logical_not(size < 0.25)
        stop = (size < 1e-8) | ((size < 1e-3) & (size > 0.25 * last))

        @pl.when(reset)
        def _():
            x_ref[...] = alpha * (row == col).astype(F32)

        @pl.when(jnp.logical_not(reset))
        def _():
            x_ref[...] = x + dot32(x, e)

        return it + 1, jnp.where(reset, F32(1e30), size), stop.astype(jnp.int32)

    lax.while_loop(lambda c: (c[0] < 80) & (c[2] == 0), fine, (jnp.int32(0), F32(1e30), jnp.int32(0)))
    x_ref[...] = x_ref[...] * s_col * s_row


def solve_kernel(gram, rhs_t, factor, smat, shifted_m, work, inv, res):
    n = gram.shape[0]
    row = lax.broadcasted_iota(jnp.int32, (n, n), 0)
    col = lax.broadcasted_iota(jnp.int32, (n, n), 1)
    g = gram[...]
    mean = jnp.sum(jnp.where(row == col, g, F32(0))) / n
    a = g + jnp.where(row == col, ridge_share * mean, F32(0))
    shifted_m[...] = a
    work[...] = a
    invert(work, inv, res)
    r = rhs_t[...]
    factor[...] = lax.dot_general(
        r, inv[...], (((0,), (0,)), ((), ())), precision=lax.Precision.HIGHEST,
        preferred_element_type=F32).astype(BF16)
    smat[...] = lax.dot_general(
        r, r, (((1,), (1,)), ((), ())), precision=lax.Precision.HIGHEST, preferred_element_type=F32)


def solve_factor(gram, rhs_t):
    square = jax.ShapeDtypeStruct((256, 256), F32)
    return pl.pallas_call(
        solve_kernel, name="solve_factor",
        out_shape=(jax.ShapeDtypeStruct((SUB, 256), BF16), square, square),
        scratch_shapes=[pltpu.VMEM((256, 256), F32)] * 3,
    )(gram, rhs_t)


def gather_kernel(own, smat, factor, ssum, x_s, x_v, c_s, c_v, *scratch):
    me, core = position()
    partner = device(me, 1 - core)
    greet(all_peers(me, core))
    work = scratch[0]
    work[...] = smat[...]
    phases, drain = all_reduce_phases(work, ssum, *scratch[1:], me, core)
    phases[0][0]()

    def block(x, k):
        return factor.at[pl.ds(pl.multiple_of((2 * x + k) * SUB, SUB), SUB)]

    over_x = [pltpu.make_async_remote_copy(
        own, block(me[0], core), x_s.at[by - 1], x_v.at[by - 1],
        device_id=device(shifted(me, 0, by), core), device_id_type=MESH) for by in (1, 2, 3)]
    over_core = [pltpu.make_async_remote_copy(
        own if by == 0 else block((me[0] + 4 - by) % 4, core), block((me[0] + 4 - by) % 4, core),
        c_s.at[by], c_v.at[by], device_id=partner, device_id_type=MESH) for by in range(4)]
    over_core[0].start()
    phases[0][1]()
    phases[1][0]()
    for copy in over_x:
        copy.start()
    factor[pl.ds(pl.multiple_of((2 * me[0] + core) * SUB, SUB), SUB)] = own[...]
    phases[1][1]()
    for p in range(2, 5):
        phases[p][0]()
        phases[p][1]()
    phases[5][0]()
    for by in (1, 3, 2):
        over_x[by - 1].wait_recv()
        over_core[by].start()
    phases[5][1]()
    phases[6][0]()
    phases[6][1]()
    for by in range(4):
        over_core[by].wait_recv()
    for copy in over_x + over_core:
        copy.wait_send()
    drain()


def gather_factor(own, smat):
    dma = pltpu.SemaphoreType.DMA
    vm = pl.BlockSpec(memory_space=pltpu.VMEM)
    return pl.pallas_call(
        gather_kernel, name="gather_factor",
        out_shape=(jax.ShapeDtypeStruct((8 * SUB, 256), BF16), jax.ShapeDtypeStruct((256, 256), F32)),
        in_specs=[vm, vm], out_specs=[vm, vm],
        scratch_shapes=[dma((3,)), dma((3,)), dma((4,)), dma((4,))] + all_reduce_scratch(),
        compiler_params=pltpu.CompilerParams(collective_id=1, has_side_effects=True),
    )(own, smat)


def leverage_kernel(scale, factor, smat, shifted_m, out, lev, work, inv, res):
    work[...] = smat[...]
    invert(work, inv, res)
    a = shifted_m[...]
    hinv = dot32(a, dot32(inv[...], a))
    high = hinv.astype(BF16)
    low = (hinv - high.astype(F32)).astype(BF16)
    ones = jnp.full((8, 256), 1.0, BF16)
    over = (((1,), (1,)), ((), ()))

    @pl.loop(0, 8)
    def _(j):
        at = pl.ds(pl.multiple_of(j * SUB, SUB), SUB)
        f = factor[at]
        out[at] = f
        quad = (jnp.dot(f, high, preferred_element_type=F32) + jnp.dot(f, low, preferred_element_type=F32)) * f.astype(F32)
        quad = quad[:, :128] + quad[:, 128:]
        q_high = quad.astype(BF16)
        q_low = (quad - q_high.astype(F32)).astype(BF16)
        total = lax.dot_general(ones, jnp.concatenate([q_high, q_low], axis=1), over, preferred_element_type=F32)
        lev[j] = scale * total


def leverage_of(factor, smat, shifted_m, scale):
    rows = factor.shape[0]
    out, lev = pl.pallas_call(
        lambda *refs: leverage_kernel(scale, *refs), name="leverage",
        out_shape=(jax.ShapeDtypeStruct((rows, 256), BF16), jax.ShapeDtypeStruct((rows // SUB, 8, SUB), F32)),
        scratch_shapes=[pltpu.VMEM((256, 256), F32)] * 3,
    )(factor, smat, shifted_m)
    return out, lev[:, 0].reshape(rows).astype(BF16)


def local(fibers, factor_b, factor_c, mode2_idx, mode3_idx, sample_wt, counts):
    slot_cap, row_total = fibers.shape
    rank_width = factor_c.shape[1]
    own_live = jnp.arange(slot_cap, dtype=jnp.int32) < counts[0]
    scale = jnp.where(own_live, sample_wt.astype(F32), F32(0.0))[:, None]
    rows_b = factor_b.at[mode2_idx].get(mode="promise_in_bounds")
    rows_c = factor_c.at[mode3_idx].get(mode="promise_in_bounds")
    rhs_t, gram = reduce_rhs(fibers, rows_b, rows_c, scale)
    factor_own, smat, shifted_m = solve_factor(gram, rhs_t)
    factor, ssum = gather_factor(factor_own, smat)
    return leverage_of(factor, ssum, shifted_m, row_total / rank_width)


def solution(mesh):
    placed = (
        P(("blk", "row"), None),
        P("blk", None),
        P(),
        P(("blk", "row")),
        P(("blk", "row")),
        P(("blk", "row")),
        P(("blk", "row")),
    )
    return jax.shard_map(
        local, mesh=mesh, in_specs=placed, out_specs=(P("row", None), P("row")), check_vma=False
    )
```

```python
import jax
import jax.numpy as jnp
from jax import lax
from jax.experimental import pallas as pl
from jax.experimental.pallas import tpu as pltpu
from jax.sharding import PartitionSpec as P

ridge_share = 0.05
MESH = pl.DeviceIdType.MESH
F32 = jnp.float32
BF16 = jnp.bfloat16

ORDER = ((0, 1, 2), (1, 2, 0), (2, 0, 1))
R0 = (0, 96, 176)
RC = (96, 80, 80)
STEPS = (2, 1, 3, 0)
SUB = 512


def block_lines(kind, i, color):
    d2 = STEPS[i]
    lines = []
    for d1 in {"across": (2,), "near": (1, 3), "own": (0,)}[kind]:
        for d3 in range(4):
            off = [0, 0, 0]
            off[ORDER[color][0]], off[ORDER[color][1]], off[ORDER[color][2]] = d1, d2, d3
            lines.append(tuple(off))
    return lines


def block_order():
    order, ends = [], {}
    needs = [("across", 0), ("near", 0), ("across", 1), ("near", 1), ("own", 0)]
    for i in (2, 3):
        needs += [("across", i), ("near", i), ("own", i - 1)]
    needs += [("own", 3)]
    for kind, i in needs:
        for color in range(3):
            for off in block_lines(kind, i, color):
                if off not in order:
                    order.append(off)
            ends[kind, i, color] = len(order)
    return order, ends


BLOCKS, ENDS = block_order()
PACK = 5


def block_at(t, me):
    code = jnp.int32(0)
    for g in range(0, 64, PACK):
        word = 0
        for j, (dx, dy, dz) in enumerate(BLOCKS[g:g + PACK]):
            word += (dx + 4 * dy + 16 * dz) << (6 * j)
        code = jnp.where(t // PACK == g // PACK, jnp.int32(word), code)
    code = lax.shift_right_logical(code, 6 * (t % PACK)) % 64
    return ((me[0] + code % 4) % 4, (me[1] + code // 4 % 4) % 4, (me[2] + code // 16) % 4)


def position():
    b, r = lax.axis_index("blk"), lax.axis_index("row")
    return (b // 2, r % 4, r // 4), b % 2


def device(coord, core):
    return {"blk": 2 * coord[0] + core, "row": 4 * coord[2] + coord[1]}


def shifted(me, axis, by):
    out = list(me)
    out[axis] = (me[axis] + by) % 4
    return tuple(out)


def all_reduce_phases(part, res, near, rx, ry, rz, far_s, far_v, snd, rcv, me, core):
    half = core * 128
    row_x = half + 32 * me[0]
    row_y = row_x + 8 * me[1]
    partner = device(me, 1 - core)

    def rows(at, n):
        return pl.ds(pl.multiple_of(at, 8), n)

    def spread(phase, axis, src_of, dst_of):
        copies = []
        for by in (1, 2, 3):
            to = shifted(me, axis, by)
            copies.append(pltpu.make_async_remote_copy(
                src_of(to[axis]), dst_of(by), snd.at[phase, by - 1], rcv.at[phase, by - 1],
                device_id=device(to, core), device_id_type=MESH))
        return copies

    def pair(slot, src, dst):
        return pltpu.make_async_remote_copy(
            src, dst, far_s.at[slot], far_v.at[slot], device_id=partner, device_id_type=MESH)

    def begin(copies):
        for copy in copies:
            copy.start()

    def arrive(copies):
        for copy in copies:
            copy.wait_recv()

    first = [pair(0, part.at[rows((1 - core) * 128, 128)], near)]
    over_x = spread(0, 0, lambda i: part.at[rows(half + 32 * i, 32)], lambda by: rx.at[by - 1])
    over_y = spread(1, 1, lambda i: part.at[rows(row_x + 8 * i, 8)], lambda by: ry.at[by - 1])
    over_z = spread(2, 2, lambda i: part.at[rows(row_y, 8)], lambda by: rz.at[me[2]])
    back_y = spread(3, 1, lambda i: res.at[rows(row_y, 8)], lambda by: res.at[rows(row_y, 8)])
    back_x = spread(4, 0, lambda i: res.at[rows(row_x, 32)], lambda by: res.at[rows(row_x, 32)])
    last = [pair(1, res.at[rows(half, 128)], res.at[rows(half, 128)])]

    def end_core():
        arrive(first)
        part[rows(half, 128)] += near[...]

    def end_x():
        arrive(over_x)
        part[rows(row_x, 32)] += rx[0] + rx[1] + rx[2]

    def end_y():
        arrive(over_y)
        part[rows(row_y, 8)] += ry[0] + ry[1] + ry[2]

    def end_z():
        arrive(over_z)
        rz[me[2]] = part[rows(row_y, 8)]
        res[rows(row_y, 8)] = (rz[0] + rz[1]) + (rz[2] + rz[3])

    stages = [(first, end_core), (over_x, end_x), (over_y, end_y), (over_z, end_z),
              (back_y, lambda: arrive(back_y)), (back_x, lambda: arrive(back_x)), (last, lambda: arrive(last))]

    def drain():
        for copies, _ in stages:
            for copy in copies:
                copy.wait_send()

    return [(lambda c=copies: begin(c), end) for copies, end in stages], drain


def all_reduce_scratch():
    dma = pltpu.SemaphoreType.DMA
    return [pltpu.VMEM((256, 256), F32), pltpu.VMEM((128, 256), F32), pltpu.VMEM((3, 32, 256), F32),
            pltpu.VMEM((3, 8, 256), F32), pltpu.VMEM((4, 8, 256), F32),
            dma((2,)), dma((2,)), dma((5, 3)), dma((5, 3))]


def greet(peers):
    barrier = pltpu.get_barrier_semaphore()
    for p in peers:
        pl.semaphore_signal(barrier, inc=1, device_id=p, device_id_type=MESH)
    pl.semaphore_wait(barrier, len(peers))


def all_peers(me, core):
    return [device(shifted(me, a, s), core) for a in range(3) for s in (1, 2, 3)] + [device(me, 1 - core)]


def dot32(a, b):
    return jnp.dot(a, b, precision=lax.Precision.HIGHEST, preferred_element_type=F32)


def ridge_inverse_steps(gram, shifted_m, x, r):
    n = gram.shape[0]
    low = ridge_share / n / (1 + ridge_share)
    bound = (1 - low) / (1 + low)
    first = 2 / (1 + low)

    def eye():
        row = lax.broadcasted_iota(jnp.int32, (n, n), 0)
        col = lax.broadcasted_iota(jnp.int32, (n, n), 1)
        return jnp.where(row == col, F32(1), F32(0))

    def inverse_trace():
        return 1.0 / jnp.sum(jnp.sum(shifted_m[...] * eye(), axis=0, keepdims=True), axis=1, keepdims=True)

    def begin():
        g = gram[...]
        one = eye()
        g = 0.5 * (g + g.T)
        trace = jnp.sum(jnp.sum(g * one, axis=0, keepdims=True), axis=1, keepdims=True)
        shifted_m[...] = g + one * (trace * (ridge_share / n))
        x[...] = first * one
        r[...] = one - shifted_m[...] * (inverse_trace() * first)

    def square(scale):
        def step():
            res = r[...]
            x[...] = scale * (x[...] + dot32(x[...], res))
            r[...] = (1 - scale) * eye() + scale * dot32(res, res)

        return step

    def correct(last):
        def step():
            scale = inverse_trace()
            err = eye() - dot32(shifted_m[...] * scale, x[...])
            new = x[...] + dot32(x[...], err)
            x[...] = new * scale if last else new

        return step

    steps = [begin]
    while bound > 1e-2:
        scale = 2 / (2 - bound * bound)
        steps.append(square(scale))
        bound = bound * bound / (2 - bound * bound)
    return steps + [correct(False), correct(False), correct(True)]


def reduce_kernel(fib, rows_b, rows_c, weight, count, factor, ssum, shifted_m,
                  fo, fp, wt_own, wt_far, part, r1, r2, r3, tot, out, gram, inv, res, own,
                  fo_sem, fs_sem, fr_sem, w_sem, s1, v1, s2, v2, s3, v3, own_sem, x_s, x_v, c_s, c_v, *sums):
    gram_scratch, s_scratch = sums[:9], sums[9:]
    me, core = position()
    partner = device(me, 1 - core)

    near = [[(me[a] + by) % 4 for by in range(4)] for a in range(3)]
    bases = [near[1][by] * 4096 for by in range(4)], [near[2][by] * 16384 for by in range(4)]

    def column(t, k):
        dx, dy, dz = BLOCKS[t]
        return pl.multiple_of(bases[1][dz] + bases[0][dy] + near[0][dx] * 1024 + k * SUB, SUB)

    def local_copy(t, at):
        return pltpu.make_async_copy(fib.at[:, pl.ds(at, SUB)], fo.at[t], fo_sem.at[t])

    def far_copy(t, at):
        return pltpu.make_async_remote_copy(
            fib.at[:, pl.ds(at, SUB)], fp.at[t], fs_sem.at[t], fr_sem.at[t],
            device_id=partner, device_id_type=MESH)

    wt_copy = pltpu.make_async_remote_copy(
        wt_own, wt_far, w_sem.at[0], w_sem.at[1], device_id=partner, device_id_type=MESH)
    gram_phases, gram_drain = all_reduce_phases(gram_scratch[0], gram, *gram_scratch[1:], me, core)

    s_phases, s_drain = all_reduce_phases(s_scratch[0], ssum, *s_scratch[1:], me, core)
    inverse_steps = ridge_inverse_steps(gram, shifted_m, inv, res)

    def inverse_step(count):
        for _ in range(min(count, len(inverse_steps))):
            inverse_steps.pop(0)()

    def gram_step(p):
        gram_phases[p][1]()
        if p < 6:
            gram_phases[p + 1][0]()

    for t in range(64):
        local_copy(t, column(t, core)).start()

    kr = (rows_b[...].astype(F32) * rows_c[...].astype(F32)).astype(BF16)
    slot = lax.broadcasted_iota(jnp.int32, (1, kr.shape[0]), 1)
    scale = jnp.where(slot < count[0], weight[...].astype(F32), F32(0))
    wt_own[...] = (scale * kr.T.astype(F32)).astype(BF16)
    gram_scratch[0][...] = jnp.dot(wt_own[...], kr, preferred_element_type=F32)

    greet(all_peers(me, core))
    wt_copy.start()
    gram_phases[0][0]()

    for t in range(64):
        far_copy(t, column(t, 1 - core)).start()

    wt_copy.wait()

    done = [0]

    def need(kind, i, c):
        lo, hi = done[0], ENDS[kind, i, c]
        if hi <= lo:
            return
        done[0] = hi

        @pl.loop(lo, hi)
        def _(t):
            local_copy(t, 0).wait()
            far_copy(t, 0).wait_recv()
            x, y, z = block_at(t, me)
            acc = jnp.dot(wt_own[...], fo[t], preferred_element_type=F32)
            acc += jnp.dot(wt_far[...], fp[t], preferred_element_type=F32)
            part[x, y, z] = acc.astype(BF16)

    def rank(c):
        return pl.ds(R0[c], RC[c])

    def place(c, i1, i2, i3):
        at = [None] * 3
        at[ORDER[c][0]], at[ORDER[c][1]], at[ORDER[c][2]] = i1, i2, i3
        return tuple(at)

    def half_of(kind, d):
        return d if kind < 2 else 1 - d

    def dest_step(kind, d):
        return 2 if kind == 0 else (1, 3)[d]

    def slab1(c, d1, e, h):
        i1 = (me[ORDER[c][0]] + d1) % 4
        i2 = (me[ORDER[c][1]] + e) % 4
        return place(c, i1, i2, pl.ds(2 * h, 2)) + (rank(c), slice(None))

    def msg1(kind, d, i, c):
        if kind == 1:
            src = r1.at[0, d, i, :, rank(c)]
        else:
            src = part.at[slab1(c, dest_step(kind, d), STEPS[i], half_of(kind, d))]
        return pltpu.make_async_remote_copy(
            src, r1.at[kind, d, i, :, rank(c)], s1.at[kind, d, i, c], v1.at[kind, d, i, c],
            device_id=device(shifted(me, ORDER[c][0], (1, 3)[d]), core), device_id_type=MESH)

    def slab2(c, e, h):
        return slab1(c, 0, e, h)

    def msg2(kind, d, c):
        if kind == 1:
            src = r2.at[0, d, :, rank(c)]
        else:
            src = part.at[slab2(c, dest_step(kind, d), half_of(kind, d))]
        return pltpu.make_async_remote_copy(
            src, r2.at[kind, d, :, rank(c)], s2.at[kind, d, c], v2.at[kind, d, c],
            device_id=device(shifted(me, ORDER[c][1], (1, 3)[d]), core), device_id_type=MESH)

    def lanes(h):
        return pl.ds(h * (SUB // 2), SUB // 2)

    def msg3(kind, d, c):
        if kind == 1:
            src = r3.at[0, d, rank(c)]
        else:
            f = (me[ORDER[c][2]] + dest_step(kind, d)) % 4
            src = tot.at[f, rank(c), lanes(half_of(kind, d))]
        return pltpu.make_async_remote_copy(
            src, r3.at[kind, d, rank(c)], s3.at[kind, d, c], v3.at[kind, d, c],
            device_id=device(shifted(me, ORDER[c][2], (1, 3)[d]), core), device_id_type=MESH)

    def rows16(c, body):
        @pl.loop(0, RC[c] // 16)
        def _(j):
            body(pl.ds(pl.multiple_of(R0[c] + 16 * j, 16), 16))

    def forward1(d, i, c):
        msg1(0, d, i, c).wait_recv()
        at = slab1(c, (1, 3)[d], STEPS[i], d)

        def body(rows):
            mine = part[at[:3] + (rows, slice(None))].astype(F32)
            r1[0, d, i, :, rows] = (r1[0, d, i, :, rows].astype(F32) + mine).astype(BF16)

        rows16(c, body)
        msg1(1, d, i, c).start()

    def finish1(i, c):
        for d in range(2):
            msg1(2, d, i, c).wait_recv()
        for d in range(2):
            msg1(1, d, i, c).wait_recv()
        for h in range(2):
            at = slab1(c, 0, STEPS[i], h)

            def body(rows):
                total = (r1[1, h, i, :, rows].astype(F32) + r1[2, 1 - h, i, :, rows].astype(F32)
                         + part[at[:3] + (rows, slice(None))].astype(F32))
                if STEPS[i] == 0:
                    tot[pl.ds(2 * h, 2), rows] = total
                else:
                    part[at[:3] + (rows, slice(None))] = total.astype(BF16)

            rows16(c, body)

    def forward2(d, c):
        msg2(0, d, c).wait_recv()
        at = slab2(c, (1, 3)[d], d)

        def body(rows):
            mine = part[at[:3] + (rows, slice(None))].astype(F32)
            r2[0, d, :, rows] = (r2[0, d, :, rows].astype(F32) + mine).astype(BF16)

        rows16(c, body)
        msg2(1, d, c).start()

    def send1(kind, i, c):
        need(("across", None, "near")[kind], i, c)
        for d in range(2):
            msg1(kind, d, i, c).start()

    for c in range(3):
        send1(0, 0, c)
    gram_step(0)
    for c in range(3):
        send1(2, 0, c)
    gram_step(1)

    for i in range(4):
        for c in range(3):
            for d in range(2):
                forward1(d, i, c)
        if i < 2:
            gram_step((2, 5)[i])
        else:
            inverse_step(2)
        if i < 3:
            for kind in (0, 2):
                for c in range(3):
                    send1(kind, i + 1, c)
        if i < 2:
            gram_step((3, 6)[i])
        if i > 0:
            inverse_step(2 if i < 3 else 99)
        for c in range(3):
            need("own", i, c)
        for c in range(3):
            finish1(i, c)
            if i == 0:
                for d in range(2):
                    msg2(0, d, c).start()
            elif i < 3:
                d = i - 1
                msg2(2, d, c).start()
                forward2(d, c)
        if i == 0:
            gram_step(4)
        elif i < 3:
            inverse_step(2)

    for c in range(3):
        for d in range(2):
            msg2(2, d, c).wait_recv()
            msg2(1, d, c).wait_recv()
        for h in range(2):
            def body(rows):
                tot[pl.ds(2 * h, 2), rows] += r2[1, h, :, rows].astype(F32) + r2[2, 1 - h, :, rows].astype(F32)

            rows16(c, body)
        for kind in (0, 2):
            for d in range(2):
                msg3(kind, d, c).start()
    for c in range(3):
        for d in range(2):
            msg3(0, d, c).wait_recv()
            f = (me[ORDER[c][2]] + (1, 3)[d]) % 4

            def body(rows):
                r3[0, d, rows] += tot[f, rows, lanes(d)]

            rows16(c, body)
            msg3(1, d, c).start()
    for c in range(3):
        for d in range(2):
            msg3(2, d, c).wait_recv()
            msg3(1, d, c).wait_recv()
        mine = me[ORDER[c][2]]
        for h in range(2):
            def body(rows):
                out[rows, lanes(h)] = tot[mine, rows, lanes(h)] + r3[1, h, rows] + r3[2, 1 - h, rows]

            rows16(c, body)

    s_scratch[0][...] = lax.dot_general(
        out[...], out[...], (((1,), (1,)), ((), ())), precision=lax.Precision.HIGHEST, preferred_element_type=F32)
    s_phases[0][0]()
    own[...] = lax.dot_general(
        out[...], inv[...], (((0,), (0,)), ((), ())), precision=lax.Precision.HIGHEST,
        preferred_element_type=F32).astype(BF16)

    def block(by, k):
        return factor.at[pl.ds(pl.multiple_of((2 * ((me[0] + 4 - by) % 4) + k) * SUB, SUB), SUB)]

    over_x = [pltpu.make_async_remote_copy(
        own, block(0, core), x_s.at[by - 1], x_v.at[by - 1],
        device_id=device(shifted(me, 0, by), core), device_id_type=MESH) for by in (1, 2, 3)]
    over_core = [pltpu.make_async_remote_copy(
        own if by == 0 else block(by, core), block(by, core),
        c_s.at[by], c_v.at[by], device_id=partner, device_id_type=MESH) for by in range(4)]
    own_copy = pltpu.make_async_copy(own, block(0, core), own_sem.at[0])
    s_phases[0][1]()
    s_phases[1][0]()
    for copy in over_x:
        copy.start()
    over_core[0].start()
    own_copy.start()
    s_phases[1][1]()
    for p in range(2, 5):
        s_phases[p][0]()
        s_phases[p][1]()
    s_phases[5][0]()
    for by in (1, 3, 2):
        over_x[by - 1].wait_recv()
        over_core[by].start()
    s_phases[5][1]()
    s_phases[6][0]()
    s_phases[6][1]()
    for by in range(4):
        over_core[by].wait_recv()

    own_copy.wait()
    for copy in over_x + over_core:
        copy.wait_send()
    s_drain()
    for c in range(3):
        for kind in range(3):
            for d in range(2):
                for i in range(4):
                    msg1(kind, d, i, c).wait_send()
                msg2(kind, d, c).wait_send()
                msg3(kind, d, c).wait_send()

    @pl.loop(0, 64)
    def _(t):
        far_copy(t, 0).wait_send()

    gram_drain()


def update_factor(fibers, rows_b, rows_c, weight, count):
    cap = fibers.shape[0]
    dma = pltpu.SemaphoreType.DMA
    vmem = pltpu.VMEM
    square = jax.ShapeDtypeStruct((256, 256), F32)
    return pl.pallas_call(
        reduce_kernel,
        name="update_factor",
        out_shape=(jax.ShapeDtypeStruct((8 * SUB, 256), BF16), square, square),
        in_specs=[pl.BlockSpec(memory_space=pl.ANY)] + [pl.BlockSpec(memory_space=pltpu.VMEM)] * 3
        + [pl.BlockSpec(memory_space=pltpu.SMEM)],
        out_specs=[pl.BlockSpec(memory_space=pl.ANY)] + [pl.BlockSpec(memory_space=pltpu.VMEM)] * 2,
        scratch_shapes=[
            vmem((64, cap, SUB), BF16), vmem((64, cap, SUB), BF16), vmem((256, cap), BF16), vmem((256, cap), BF16),
            vmem((4, 4, 4, 256, SUB), BF16),
            vmem((3, 2, 4, 2, 256, SUB), BF16), vmem((3, 2, 2, 256, SUB), BF16),
            vmem((3, 2, 256, SUB // 2), F32), vmem((4, 256, SUB), F32),
            vmem((256, SUB), F32), vmem((256, 256), F32), vmem((256, 256), F32), vmem((256, 256), F32),
            vmem((SUB, 256), BF16),
            dma((64,)), dma((64,)), dma((64,)), dma((2,)),
            dma((3, 2, 4, 3)), dma((3, 2, 4, 3)), dma((3, 2, 3)), dma((3, 2, 3)), dma((3, 2, 3)), dma((3, 2, 3)),
            dma((1,)), dma((3,)), dma((3,)), dma((4,)), dma((4,)),
        ] + all_reduce_scratch() * 2,
        compiler_params=pltpu.CompilerParams(
            collective_id=0, has_side_effects=True, vmem_limit_bytes=63 * 1024 * 1024),
    )(fibers, rows_b, rows_c, weight, count)


def dot16(a, b):
    return jnp.dot(a.astype(BF16), b.astype(BF16), preferred_element_type=F32)


def invert(a_ref, x_ref, r_ref):
    n = a_ref.shape[0]
    row = lax.broadcasted_iota(jnp.int32, (n, n), 0)
    col = lax.broadcasted_iota(jnp.int32, (n, n), 1)
    eye = jnp.where(row == col, F32(1), F32(0))
    a = a_ref[...]
    diag = jnp.where(row == col, a, F32(0))
    s_col = lax.rsqrt(jnp.sum(diag, axis=1, keepdims=True))
    s_row = lax.rsqrt(jnp.sum(diag, axis=0, keepdims=True))
    a_ref[...] = a * s_col * s_row
    bound = jnp.max(jnp.sum(jnp.abs(a_ref[...]), axis=0, keepdims=True))
    alpha = 1.9 / bound
    x_ref[...] = alpha * eye
    r_ref[...] = eye - alpha * a_ref[...]

    def coarse(carry):
        it, _ = carry
        r = r_ref[...]
        x = x_ref[...]
        x_ref[...] = x + dot16(x, r)
        r = dot16(r, r)
        r_ref[...] = r
        return it + 1, jnp.sum(r * r)

    lax.while_loop(lambda c: (c[0] < 24) & (c[1] > 1e-3), coarse, (jnp.int32(0), F32(1e9)))

    def fine(carry):
        it, last, _ = carry
        x = x_ref[...]
        e = (row == col).astype(F32) - dot32(a_ref[...], x)
        size = jnp.sum(e * e)
        reset = (it == 0) & jnp.logical_not(size < 0.25)
        stop = (size < 1e-8) | ((size < 1e-3) & (size > 0.25 * last))

        @pl.when(reset)
        def _():
            x_ref[...] = alpha * (row == col).astype(F32)

        @pl.when(jnp.logical_not(reset))
        def _():
            x_ref[...] = x + dot32(x, e)

        return it + 1, jnp.where(reset, F32(1e30), size), stop.astype(jnp.int32)

    lax.while_loop(lambda c: (c[0] < 80) & (c[2] == 0), fine, (jnp.int32(0), F32(1e30), jnp.int32(0)))
    x_ref[...] = x_ref[...] * s_col * s_row


def leverage_kernel(scale, factor, smat, shifted_m, out, lev, work, inv, res, rows):
    work[...] = smat[...]
    invert(work, inv, res)
    a = shifted_m[...]
    hinv = dot32(a, dot32(inv[...], a))
    high = hinv.astype(BF16)
    low = (hinv - high.astype(F32)).astype(BF16)
    ones = jnp.full((8, 256), 1.0, BF16)
    over = (((1,), (1,)), ((), ()))

    @pl.loop(0, 8)
    def _(j):
        at = pl.ds(pl.multiple_of(j * SUB, SUB), SUB)
        f = factor[at]
        out[at] = f
        quad = (jnp.dot(f, high, preferred_element_type=F32) + jnp.dot(f, low, preferred_element_type=F32)) * f.astype(F32)
        quad = quad[:, :128] + quad[:, 128:]
        q_high = quad.astype(BF16)
        q_low = (quad - q_high.astype(F32)).astype(BF16)
        total = lax.dot_general(ones, jnp.concatenate([q_high, q_low], axis=1), over, preferred_element_type=F32)
        for k in range(SUB // 128):
            rows[pl.ds(j * (SUB // 128) + k, 1)] = total[0:1, 128 * k:128 * (k + 1)]

    lev[...] = (scale * rows[...]).astype(BF16)


def leverage_of(factor, smat, shifted_m, scale):
    rows = factor.shape[0]
    out, lev = pl.pallas_call(
        lambda *refs: leverage_kernel(scale, *refs), name="leverage",
        out_shape=(jax.ShapeDtypeStruct((rows, 256), BF16), jax.ShapeDtypeStruct((rows // 128, 128), BF16)),
        scratch_shapes=[pltpu.VMEM((256, 256), F32)] * 3 + [pltpu.VMEM((rows // 128, 128), F32)],
    )(factor, smat, shifted_m)
    return out, lev.reshape(rows)


def local(fibers, factor_b, factor_c, mode2_idx, mode3_idx, sample_wt, counts):
    slot_cap, row_total = fibers.shape
    rank_width = factor_c.shape[1]
    rows_b = factor_b.at[mode2_idx].get(mode="promise_in_bounds", wrap_negative_indices=False)
    rows_c = factor_c.at[mode3_idx].get(mode="promise_in_bounds", wrap_negative_indices=False)
    factor, ssum, shifted_m = update_factor(fibers, rows_b, rows_c, sample_wt.reshape(1, slot_cap), counts)
    return leverage_of(factor, ssum, shifted_m, row_total / rank_width)


def solution(mesh):
    placed = (
        P(("blk", "row"), None),
        P("blk", None),
        P(),
        P(("blk", "row")),
        P(("blk", "row")),
        P(("blk", "row")),
        P(("blk", "row")),
    )
    return jax.shard_map(
        local, mesh=mesh, in_specs=placed, out_specs=(P("row", None), P("row")), check_vma=False
    )
```

```python
import jax
import jax.numpy as jnp
from jax import lax
from jax.experimental import pallas as pl
from jax.experimental.pallas import tpu as pltpu
from jax.sharding import PartitionSpec as P

ridge_share = 0.05
MESH = pl.DeviceIdType.MESH
F32 = jnp.float32
BF16 = jnp.bfloat16

ORDER = ((0, 1, 2), (1, 2, 0), (2, 0, 1))
R0 = (0, 96, 176)
RC = (96, 80, 80)
STEPS = (2, 1, 3, 0)
SUB = 512


def block_lines(kind, i, color):
    d2 = STEPS[i]
    lines = []
    for d1 in {"across": (2,), "near": (1, 3), "own": (0,)}[kind]:
        for d3 in range(4):
            off = [0, 0, 0]
            off[ORDER[color][0]], off[ORDER[color][1]], off[ORDER[color][2]] = d1, d2, d3
            lines.append(tuple(off))
    return lines


def block_order():
    order, ends = [], {}
    needs = [("across", 0), ("near", 0), ("across", 1), ("near", 1), ("own", 0)]
    for i in (2, 3):
        needs += [("across", i), ("near", i), ("own", i - 1)]
    needs += [("own", 3)]
    for kind, i in needs:
        for color in range(3):
            for off in block_lines(kind, i, color):
                if off not in order:
                    order.append(off)
            ends[kind, i, color] = len(order)
    return order, ends


BLOCKS, ENDS = block_order()
PACK = 5


def block_at(t, me):
    code = jnp.int32(0)
    for g in range(0, 64, PACK):
        word = 0
        for j, (dx, dy, dz) in enumerate(BLOCKS[g:g + PACK]):
            word += (dx + 4 * dy + 16 * dz) << (6 * j)
        code = jnp.where(t // PACK == g // PACK, jnp.int32(word), code)
    code = lax.shift_right_logical(code, 6 * (t % PACK)) % 64
    return ((me[0] + code % 4) % 4, (me[1] + code // 4 % 4) % 4, (me[2] + code // 16) % 4)


def position():
    b, r = lax.axis_index("blk"), lax.axis_index("row")
    return (b // 2, r % 4, r // 4), b % 2


def device(coord, core):
    return {"blk": 2 * coord[0] + core, "row": 4 * coord[2] + coord[1]}


def shifted(me, axis, by):
    out = list(me)
    out[axis] = (me[axis] + by) % 4
    return tuple(out)


def all_reduce_phases(part, res, near, rx, ry, rz, far_s, far_v, snd, rcv, me, core):
    half = core * 128
    row_x = half + 32 * me[0]
    row_y = row_x + 8 * me[1]
    partner = device(me, 1 - core)

    def rows(at, n):
        return pl.ds(pl.multiple_of(at, 8), n)

    def spread(phase, axis, src_of, dst_of):
        copies = []
        for by in (1, 2, 3):
            to = shifted(me, axis, by)
            copies.append(pltpu.make_async_remote_copy(
                src_of(to[axis]), dst_of(by), snd.at[phase, by - 1], rcv.at[phase, by - 1],
                device_id=device(to, core), device_id_type=MESH))
        return copies

    def pair(slot, src, dst):
        return pltpu.make_async_remote_copy(
            src, dst, far_s.at[slot], far_v.at[slot], device_id=partner, device_id_type=MESH)

    def begin(copies):
        for copy in copies:
            copy.start()

    def arrive(copies):
        for copy in copies:
            copy.wait_recv()

    first = [pair(0, part.at[rows((1 - core) * 128, 128)], near)]
    over_x = spread(0, 0, lambda i: part.at[rows(half + 32 * i, 32)], lambda by: rx.at[by - 1])
    over_y = spread(1, 1, lambda i: part.at[rows(row_x + 8 * i, 8)], lambda by: ry.at[by - 1])
    over_z = spread(2, 2, lambda i: part.at[rows(row_y, 8)], lambda by: rz.at[me[2]])
    back_y = spread(3, 1, lambda i: res.at[rows(row_y, 8)], lambda by: res.at[rows(row_y, 8)])
    back_x = spread(4, 0, lambda i: res.at[rows(row_x, 32)], lambda by: res.at[rows(row_x, 32)])
    last = [pair(1, res.at[rows(half, 128)], res.at[rows(half, 128)])]

    def end_core():
        arrive(first)
        part[rows(half, 128)] += near[...]

    def end_x():
        arrive(over_x)
        part[rows(row_x, 32)] += rx[0] + rx[1] + rx[2]

    def end_y():
        arrive(over_y)
        part[rows(row_y, 8)] += ry[0] + ry[1] + ry[2]

    def end_z():
        arrive(over_z)
        rz[me[2]] = part[rows(row_y, 8)]
        res[rows(row_y, 8)] = (rz[0] + rz[1]) + (rz[2] + rz[3])

    stages = [(first, end_core), (over_x, end_x), (over_y, end_y), (over_z, end_z),
              (back_y, lambda: arrive(back_y)), (back_x, lambda: arrive(back_x)), (last, lambda: arrive(last))]

    def drain():
        for copies, _ in stages:
            for copy in copies:
                copy.wait_send()

    return [(lambda c=copies: begin(c), end) for copies, end in stages], drain


def all_reduce_scratch():
    dma = pltpu.SemaphoreType.DMA
    return [pltpu.VMEM((256, 256), F32), pltpu.VMEM((128, 256), F32), pltpu.VMEM((3, 32, 256), F32),
            pltpu.VMEM((3, 8, 256), F32), pltpu.VMEM((4, 8, 256), F32),
            dma((2,)), dma((2,)), dma((5, 3)), dma((5, 3))]


def greet(peers):
    barrier = pltpu.get_barrier_semaphore()
    for p in peers:
        pl.semaphore_signal(barrier, inc=1, device_id=p, device_id_type=MESH)
    return lambda: pl.semaphore_wait(barrier, len(peers))


def split(value):
    high = value.astype(BF16)
    return high, (value - high.astype(F32)).astype(BF16)


def all_peers(me, core):
    return [device(shifted(me, a, s), core) for a in range(3) for s in (1, 2, 3)] + [device(me, 1 - core)]


def dot32(a, b):
    return jnp.dot(a, b, precision=lax.Precision.HIGHEST, preferred_element_type=F32)


def ridge_inverse_steps(gram, shifted_m, x, r):
    n = gram.shape[0]
    low = ridge_share / n / (1 + ridge_share)
    bound = (1 - low) / (1 + low)
    first = 2 / (1 + low)

    def eye():
        row = lax.broadcasted_iota(jnp.int32, (n, n), 0)
        col = lax.broadcasted_iota(jnp.int32, (n, n), 1)
        return jnp.where(row == col, F32(1), F32(0))

    def inverse_trace():
        return 1.0 / jnp.sum(jnp.sum(shifted_m[...] * eye(), axis=0, keepdims=True), axis=1, keepdims=True)

    def begin():
        g = gram[...]
        one = eye()
        g = 0.5 * (g + g.T)
        trace = jnp.sum(jnp.sum(g * one, axis=0, keepdims=True), axis=1, keepdims=True)
        shifted_m[...] = g + one * (trace * (ridge_share / n))
        x[...] = first * one
        r[...] = one - shifted_m[...] * (inverse_trace() * first)

    def square(scale):
        def step():
            res = r[...]
            x[...] = scale * (x[...] + dot32(x[...], res))
            r[...] = (1 - scale) * eye() + scale * dot32(res, res)

        return step

    def correct(last):
        def step():
            scale = inverse_trace()
            err = eye() - dot32(shifted_m[...] * scale, x[...])
            new = x[...] + dot32(x[...], err)
            x[...] = new * scale if last else new

        return step

    steps = [begin]
    while bound > 1e-2:
        scale = 2 / (2 - bound * bound)
        steps.append(square(scale))
        bound = bound * bound / (2 - bound * bound)
    return steps + [correct(False), correct(False), correct(True)]


def reduce_kernel(fib, table_b, table_c, idx_b, idx_c, weight, count, factor, ssum, shifted_m,
                  fo, fp, wt_own, wt_far, part, r1, r2, r3, tot, out, gram, inv, res, own,
                  fo_sem, fs_sem, fr_sem, w_sem, s1, v1, s2, v2, s3, v3, own_sem, x_s, x_v, c_s, c_v, t_sem, *sums):
    gram_scratch, s_scratch = sums[:9], sums[9:]
    me, core = position()
    all_entered = greet(all_peers(me, core))
    chunks_b, chunks_c = table_b.shape[0] // 256, table_c.shape[0] // 256

    def chunk_slot(i):
        return (i // 16, i // 4 % 4, i % 4, slice(None), pl.ds(0, 256))

    def load_chunk(table, i, first):
        rows = pl.ds(pl.multiple_of(256 * i, 256), 256)
        return pltpu.make_async_copy(table.at[rows], part.at[chunk_slot(first + i)], t_sem.at[first + i])

    for table, count_of, first in ((table_b, chunks_b, 0), (table_c, chunks_c, chunks_b)):
        @pl.loop(0, count_of)
        def _(i):
            load_chunk(table, i, first).start()
    partner = device(me, 1 - core)

    near = [[(me[a] + by) % 4 for by in range(4)] for a in range(3)]
    bases = [near[1][by] * 4096 for by in range(4)], [near[2][by] * 16384 for by in range(4)]

    def column(t, k):
        dx, dy, dz = BLOCKS[t]
        return pl.multiple_of(bases[1][dz] + bases[0][dy] + near[0][dx] * 1024 + k * SUB, SUB)

    def local_copy(t, at):
        return pltpu.make_async_copy(fib.at[:, pl.ds(at, SUB)], fo.at[t], fo_sem.at[t])

    def far_copy(t, at):
        return pltpu.make_async_remote_copy(
            fib.at[:, pl.ds(at, SUB)], fp.at[t], fs_sem.at[t], fr_sem.at[t],
            device_id=partner, device_id_type=MESH)

    wt_copy = pltpu.make_async_remote_copy(
        wt_own, wt_far, w_sem.at[0], w_sem.at[1], device_id=partner, device_id_type=MESH)
    gram_phases, gram_drain = all_reduce_phases(gram_scratch[0], gram, *gram_scratch[1:], me, core)

    s_phases, s_drain = all_reduce_phases(s_scratch[0], ssum, *s_scratch[1:], me, core)
    inverse_steps = ridge_inverse_steps(gram, shifted_m, inv, res)

    def inverse_step(count):
        for _ in range(min(count, len(inverse_steps))):
            inverse_steps.pop(0)()

    def gram_step(p):
        gram_phases[p][1]()
        if p < 6:
            gram_phases[p + 1][0]()

    for t in range(64):
        local_copy(t, column(t, core)).start()

    cap = weight.shape[1]
    lane = lax.broadcasted_iota(jnp.int32, (cap, 256), 1).astype(F32)
    diagonal = lax.broadcasted_iota(jnp.int32, (cap, cap), 0) == lax.broadcasted_iota(jnp.int32, (cap, cap), 1)

    def gather_rows(table, idx, chunks, first):
        at = jnp.sum(jnp.where(diagonal, idx[...].astype(F32), F32(0)), axis=1, keepdims=True)

        def body(i, total):
            load_chunk(table, i, first).wait()
            hot = jnp.where(at == lane + (256 * i).astype(F32), F32(1), F32(0)).astype(BF16)
            return total + jnp.dot(hot, part[chunk_slot(first + i)], preferred_element_type=F32)

        return lax.fori_loop(0, chunks, body, jnp.zeros((cap, 256), F32))

    kr = (gather_rows(table_b, idx_b, chunks_b, 0) * gather_rows(table_c, idx_c, chunks_c, chunks_b)).astype(BF16)
    slot = lax.broadcasted_iota(jnp.int32, (1, cap), 1)
    scale = jnp.where(slot < count[0], weight[...].astype(F32), F32(0))
    wt_own[...] = (scale * kr.T.astype(F32)).astype(BF16)
    gram_scratch[0][...] = jnp.dot(wt_own[...], kr, preferred_element_type=F32)

    all_entered()
    wt_copy.start()
    gram_phases[0][0]()

    for t in range(64):
        far_copy(t, column(t, 1 - core)).start()

    wt_copy.wait()

    done = [0]

    def need(kind, i, c):
        lo, hi = done[0], ENDS[kind, i, c]
        if hi <= lo:
            return
        done[0] = hi

        @pl.loop(lo, hi)
        def _(t):
            local_copy(t, 0).wait()
            far_copy(t, 0).wait_recv()
            x, y, z = block_at(t, me)
            acc = jnp.dot(wt_own[...], fo[t], preferred_element_type=F32)
            acc += jnp.dot(wt_far[...], fp[t], preferred_element_type=F32)
            part[x, y, z] = acc.astype(BF16)

    def rank(c):
        return pl.ds(R0[c], RC[c])

    def place(c, i1, i2, i3):
        at = [None] * 3
        at[ORDER[c][0]], at[ORDER[c][1]], at[ORDER[c][2]] = i1, i2, i3
        return tuple(at)

    def half_of(kind, d):
        return d if kind < 2 else 1 - d

    def dest_step(kind, d):
        return 2 if kind == 0 else (1, 3)[d]

    def slab1(c, d1, e, h):
        i1 = (me[ORDER[c][0]] + d1) % 4
        i2 = (me[ORDER[c][1]] + e) % 4
        return place(c, i1, i2, pl.ds(2 * h, 2)) + (rank(c), slice(None))

    def msg1(kind, d, i, c):
        if kind == 1:
            src = r1.at[0, d, i, :, rank(c)]
        else:
            src = part.at[slab1(c, dest_step(kind, d), STEPS[i], half_of(kind, d))]
        return pltpu.make_async_remote_copy(
            src, r1.at[kind, d, i, :, rank(c)], s1.at[kind, d, i, c], v1.at[kind, d, i, c],
            device_id=device(shifted(me, ORDER[c][0], (1, 3)[d]), core), device_id_type=MESH)

    def slab2(c, e, h):
        return slab1(c, 0, e, h)

    def msg2(kind, d, c):
        if kind == 1:
            src = r2.at[0, d, :, rank(c)]
        else:
            src = part.at[slab2(c, dest_step(kind, d), half_of(kind, d))]
        return pltpu.make_async_remote_copy(
            src, r2.at[kind, d, :, rank(c)], s2.at[kind, d, c], v2.at[kind, d, c],
            device_id=device(shifted(me, ORDER[c][1], (1, 3)[d]), core), device_id_type=MESH)

    def lanes(h):
        return pl.ds(h * (SUB // 2), SUB // 2)

    def msg3(kind, d, c):
        if kind == 1:
            src = r3.at[0, d, rank(c)]
        else:
            f = (me[ORDER[c][2]] + dest_step(kind, d)) % 4
            src = tot.at[f, rank(c), lanes(half_of(kind, d))]
        return pltpu.make_async_remote_copy(
            src, r3.at[kind, d, rank(c)], s3.at[kind, d, c], v3.at[kind, d, c],
            device_id=device(shifted(me, ORDER[c][2], (1, 3)[d]), core), device_id_type=MESH)

    def rows16(c, body):
        @pl.loop(0, RC[c] // 16)
        def _(j):
            body(pl.ds(pl.multiple_of(R0[c] + 16 * j, 16), 16))

    def forward1(d, i, c):
        msg1(0, d, i, c).wait_recv()
        at = slab1(c, (1, 3)[d], STEPS[i], d)

        def body(rows):
            mine = part[at[:3] + (rows, slice(None))].astype(F32)
            r1[0, d, i, :, rows] = (r1[0, d, i, :, rows].astype(F32) + mine).astype(BF16)

        rows16(c, body)
        msg1(1, d, i, c).start()

    def finish1(i, c):
        for d in range(2):
            msg1(2, d, i, c).wait_recv()
        for d in range(2):
            msg1(1, d, i, c).wait_recv()
        for h in range(2):
            at = slab1(c, 0, STEPS[i], h)

            def body(rows):
                total = (r1[1, h, i, :, rows].astype(F32) + r1[2, 1 - h, i, :, rows].astype(F32)
                         + part[at[:3] + (rows, slice(None))].astype(F32))
                if STEPS[i] == 0:
                    tot[pl.ds(2 * h, 2), rows] = total
                else:
                    part[at[:3] + (rows, slice(None))] = total.astype(BF16)

            rows16(c, body)

    def forward2(d, c):
        msg2(0, d, c).wait_recv()
        at = slab2(c, (1, 3)[d], d)

        def body(rows):
            mine = part[at[:3] + (rows, slice(None))].astype(F32)
            r2[0, d, :, rows] = (r2[0, d, :, rows].astype(F32) + mine).astype(BF16)

        rows16(c, body)
        msg2(1, d, c).start()

    def send1(kind, i, c):
        need(("across", None, "near")[kind], i, c)
        for d in range(2):
            msg1(kind, d, i, c).start()

    for c in range(3):
        send1(0, 0, c)
    gram_step(0)
    for c in range(3):
        send1(2, 0, c)
    gram_step(1)

    for i in range(4):
        for c in range(3):
            for d in range(2):
                forward1(d, i, c)
        if i < 2:
            gram_step((2, 5)[i])
        else:
            inverse_step(2)
        if i < 3:
            for kind in (0, 2):
                for c in range(3):
                    send1(kind, i + 1, c)
        if i < 2:
            gram_step((3, 6)[i])
        if i > 0:
            inverse_step(2 if i < 3 else 99)
        for c in range(3):
            need("own", i, c)
        for c in range(3):
            finish1(i, c)
            if i == 0:
                for d in range(2):
                    msg2(0, d, c).start()
            elif i < 3:
                d = i - 1
                msg2(2, d, c).start()
                forward2(d, c)
        if i == 0:
            gram_step(4)
        elif i < 3:
            inverse_step(2)

    for c in range(3):
        for d in range(2):
            msg2(2, d, c).wait_recv()
            msg2(1, d, c).wait_recv()
        for h in range(2):
            def body(rows):
                tot[pl.ds(2 * h, 2), rows] += r2[1, h, :, rows].astype(F32) + r2[2, 1 - h, :, rows].astype(F32)

            rows16(c, body)
        for kind in (0, 2):
            for d in range(2):
                msg3(kind, d, c).start()
    for c in range(3):
        for d in range(2):
            msg3(0, d, c).wait_recv()
            f = (me[ORDER[c][2]] + (1, 3)[d]) % 4

            def body(rows):
                r3[0, d, rows] += tot[f, rows, lanes(d)]

            rows16(c, body)
            msg3(1, d, c).start()
    for c in range(3):
        for d in range(2):
            msg3(2, d, c).wait_recv()
            msg3(1, d, c).wait_recv()
        mine = me[ORDER[c][2]]
        for h in range(2):
            def body(rows):
                out[rows, lanes(h)] = tot[mine, rows, lanes(h)] + r3[1, h, rows] + r3[2, 1 - h, rows]

            rows16(c, body)

    high, low = split(out[...])
    cross = lax.dot_general(high, low, (((1,), (1,)), ((), ())), preferred_element_type=F32)
    s_scratch[0][...] = lax.dot_general(
        high, high, (((1,), (1,)), ((), ())), preferred_element_type=F32) + (cross + cross.T)
    s_phases[0][0]()
    inv_high, inv_low = split(inv[...])
    first_dims = (((0,), (0,)), ((), ()))
    own[...] = (lax.dot_general(high, inv_high, first_dims, preferred_element_type=F32)
                + (lax.dot_general(high, inv_low, first_dims, preferred_element_type=F32)
                   + lax.dot_general(low, inv_high, first_dims, preferred_element_type=F32))).astype(BF16)

    def block(by, k):
        return factor.at[pl.ds(pl.multiple_of((2 * ((me[0] + 4 - by) % 4) + k) * SUB, SUB), SUB)]

    over_x = [pltpu.make_async_remote_copy(
        own, block(0, core), x_s.at[by - 1], x_v.at[by - 1],
        device_id=device(shifted(me, 0, by), core), device_id_type=MESH) for by in (1, 2, 3)]
    over_core = [pltpu.make_async_remote_copy(
        own if by == 0 else block(by, core), block(by, core),
        c_s.at[by], c_v.at[by], device_id=partner, device_id_type=MESH) for by in range(4)]
    own_copy = pltpu.make_async_copy(own, block(0, core), own_sem.at[0])
    s_phases[0][1]()
    s_phases[1][0]()
    for copy in over_x:
        copy.start()
    over_core[0].start()
    own_copy.start()
    s_phases[1][1]()
    for p in range(2, 5):
        s_phases[p][0]()
        s_phases[p][1]()
    s_phases[5][0]()
    for by in (1, 3, 2):
        over_x[by - 1].wait_recv()
        over_core[by].start()
    s_phases[5][1]()
    s_phases[6][0]()
    s_phases[6][1]()
    for by in range(4):
        over_core[by].wait_recv()

    own_copy.wait()
    for copy in over_x + over_core:
        copy.wait_send()
    s_drain()
    for c in range(3):
        for kind in range(3):
            for d in range(2):
                for i in range(4):
                    msg1(kind, d, i, c).wait_send()
                msg2(kind, d, c).wait_send()
                msg3(kind, d, c).wait_send()

    @pl.loop(0, 64)
    def _(t):
        far_copy(t, 0).wait_send()

    gram_drain()


def update_factor(fibers, table_b, table_c, idx_b, idx_c, weight, count):
    cap = fibers.shape[0]
    dma = pltpu.SemaphoreType.DMA
    vmem = pltpu.VMEM
    square = jax.ShapeDtypeStruct((256, 256), F32)
    return pl.pallas_call(
        reduce_kernel,
        name="update_factor",
        out_shape=(jax.ShapeDtypeStruct((8 * SUB, 256), BF16), square, square),
        in_specs=[pl.BlockSpec(memory_space=pl.ANY)] * 3 + [pl.BlockSpec(memory_space=pltpu.VMEM)] * 3
        + [pl.BlockSpec(memory_space=pltpu.SMEM)],
        out_specs=[pl.BlockSpec(memory_space=pl.ANY)] + [pl.BlockSpec(memory_space=pltpu.VMEM)] * 2,
        scratch_shapes=[
            vmem((64, cap, SUB), BF16), vmem((64, cap, SUB), BF16), vmem((256, cap), BF16), vmem((256, cap), BF16),
            vmem((4, 4, 4, 256, SUB), BF16),
            vmem((3, 2, 4, 2, 256, SUB), BF16), vmem((3, 2, 2, 256, SUB), BF16),
            vmem((3, 2, 256, SUB // 2), F32), vmem((4, 256, SUB), F32),
            vmem((256, SUB), F32), vmem((256, 256), F32), vmem((256, 256), F32), vmem((256, 256), F32),
            vmem((SUB, 256), BF16),
            dma((64,)), dma((64,)), dma((64,)), dma((2,)),
            dma((3, 2, 4, 3)), dma((3, 2, 4, 3)), dma((3, 2, 3)), dma((3, 2, 3)), dma((3, 2, 3)), dma((3, 2, 3)),
            dma((1,)), dma((3,)), dma((3,)), dma((4,)), dma((4,)), dma((48,)),
        ] + all_reduce_scratch() * 2,
        compiler_params=pltpu.CompilerParams(
            collective_id=0, has_side_effects=True, vmem_limit_bytes=63 * 1024 * 1024),
    )(fibers, table_b, table_c, idx_b, idx_c, weight, count)


def dot16(a, b):
    return jnp.dot(a.astype(BF16), b.astype(BF16), preferred_element_type=F32)


def invert(a_ref, x_ref, r_ref, between):
    n = a_ref.shape[0]
    row = lax.broadcasted_iota(jnp.int32, (n, n), 0)
    col = lax.broadcasted_iota(jnp.int32, (n, n), 1)
    eye = jnp.where(row == col, F32(1), F32(0))
    a = a_ref[...]
    diag = jnp.where(row == col, a, F32(0))
    s_col = lax.rsqrt(jnp.sum(diag, axis=1, keepdims=True))
    s_row = lax.rsqrt(jnp.sum(diag, axis=0, keepdims=True))
    a_ref[...] = a * s_col * s_row
    bound = jnp.max(jnp.sum(jnp.abs(a_ref[...]), axis=0, keepdims=True))
    alpha = 1.9 / bound
    x_ref[...] = alpha * eye
    r_ref[...] = eye - alpha * a_ref[...]

    def coarse(carry):
        it, _ = carry
        r = r_ref[...]
        x = x_ref[...]
        x_ref[...] = x + dot16(x, r)
        r = dot16(r, r)
        r_ref[...] = r
        return it + 1, jnp.sum(r * r)

    lax.while_loop(lambda c: (c[0] < 24) & (c[1] > 1e-3), coarse, (jnp.int32(0), F32(1e9)))

    between()

    def fine(carry):
        it, last, _ = carry
        x = x_ref[...]
        e = (row == col).astype(F32) - dot32(a_ref[...], x)
        size = jnp.sum(e * e)
        reset = (it == 0) & jnp.logical_not(size < 0.25)
        stop = (size < 1e-8) | ((size < 1e-3) & (size > 0.25 * last))

        @pl.when(reset)
        def _():
            x_ref[...] = alpha * (row == col).astype(F32)

        @pl.when(jnp.logical_not(reset))
        def _():
            x_ref[...] = x + dot32(x, e)

        return it + 1, jnp.where(reset, F32(1e30), size), stop.astype(jnp.int32)

    lax.while_loop(lambda c: (c[0] < 80) & (c[2] == 0), fine, (jnp.int32(0), F32(1e30), jnp.int32(0)))
    x_ref[...] = x_ref[...] * s_col * s_row


def leverage_kernel(scale, factor, smat, shifted_m, out, lev, work, inv, res, rows, held, sem):
    take = pltpu.make_async_copy(factor, held, sem.at[0])
    give = pltpu.make_async_copy(held, out, sem.at[1])
    take.start()

    def pass_on():
        take.wait()
        give.start()

    work[...] = smat[...]
    invert(work, inv, res, pass_on)
    a = shifted_m[...]
    hinv = dot32(a, dot32(inv[...], a))
    high = hinv.astype(BF16)
    low = (hinv - high.astype(F32)).astype(BF16)
    ones = jnp.full((8, 256), 1.0, BF16)
    over = (((1,), (1,)), ((), ()))

    @pl.loop(0, 8)
    def _(j):
        at = pl.ds(pl.multiple_of(j * SUB, SUB), SUB)
        f = held[at]
        quad = (jnp.dot(f, high, preferred_element_type=F32) + jnp.dot(f, low, preferred_element_type=F32)) * f.astype(F32)
        quad = quad[:, :128] + quad[:, 128:]
        q_high = quad.astype(BF16)
        q_low = (quad - q_high.astype(F32)).astype(BF16)
        total = lax.dot_general(ones, jnp.concatenate([q_high, q_low], axis=1), over, preferred_element_type=F32)
        for k in range(SUB // 128):
            rows[pl.ds(j * (SUB // 128) + k, 1)] = total[0:1, 128 * k:128 * (k + 1)]

    lev[...] = (scale * rows[...]).astype(BF16)
    give.wait()


def leverage_of(factor, smat, shifted_m, scale):
    rows = factor.shape[0]
    out, lev = pl.pallas_call(
        lambda *refs: leverage_kernel(scale, *refs), name="leverage",
        out_shape=(jax.ShapeDtypeStruct((rows, 256), BF16), jax.ShapeDtypeStruct((rows // 128, 128), BF16)),
        in_specs=[pl.BlockSpec(memory_space=pl.ANY)] + [pl.BlockSpec(memory_space=pltpu.VMEM)] * 2,
        out_specs=[pl.BlockSpec(memory_space=pl.ANY), pl.BlockSpec(memory_space=pltpu.VMEM)],
        scratch_shapes=[pltpu.VMEM((256, 256), F32)] * 3 + [
            pltpu.VMEM((rows // 128, 128), F32), pltpu.VMEM((rows, 256), BF16), pltpu.SemaphoreType.DMA((2,))],
    )(factor, smat, shifted_m)
    return out, lev.reshape(rows)


def local(fibers, factor_b, factor_c, mode2_idx, mode3_idx, sample_wt, counts):
    slot_cap, row_total = fibers.shape
    rank_width = factor_c.shape[1]
    row = (1, slot_cap)
    factor, ssum, shifted_m = update_factor(
        fibers, factor_b, factor_c, mode2_idx.reshape(row), mode3_idx.reshape(row), sample_wt.reshape(row), counts)
    return leverage_of(factor, ssum, shifted_m, row_total / rank_width)


def solution(mesh):
    placed = (
        P(("blk", "row"), None),
        P("blk", None),
        P(),
        P(("blk", "row")),
        P(("blk", "row")),
        P(("blk", "row")),
        P(("blk", "row")),
    )
    return jax.shard_map(
        local, mesh=mesh, in_specs=placed, out_specs=(P("row", None), P("row")), check_vma=False
    )
```

```python
import jax
import jax.numpy as jnp
from jax import lax
from jax.experimental import pallas as pl
from jax.experimental.pallas import tpu as pltpu
from jax.sharding import PartitionSpec as P

ridge_share = 0.05
MESH = pl.DeviceIdType.MESH
F32 = jnp.float32
BF16 = jnp.bfloat16

ORDER = ((0, 1, 2), (1, 2, 0), (2, 0, 1))
R0 = ((0, 96, 176), (0, 80, 176))
RC = ((96, 80, 80), (80, 96, 80))
STEPS = (2, 1, 3, 0)
SUB = 512


def block_lines(kind, i, color):
    d2 = STEPS[i]
    lines = []
    for d1 in {"across": (2,), "near": (1, 3), "own": (0,)}[kind]:
        for d3 in range(4):
            off = [0, 0, 0]
            off[ORDER[color][0]], off[ORDER[color][1]], off[ORDER[color][2]] = d1, d2, d3
            lines.append(tuple(off))
    return lines


def block_order():
    order, ends = [], {}
    needs = [("across", 0), ("near", 0), ("across", 1), ("near", 1), ("own", 0)]
    for i in (2, 3):
        needs += [("across", i), ("near", i), ("own", i - 1)]
    needs += [("own", 3)]
    for kind, i in needs:
        for color in range(3):
            for off in block_lines(kind, i, color):
                if off not in order:
                    order.append(off)
            ends[kind, i, color] = len(order)
    return order, ends


BLOCKS, ENDS = block_order()
PACK = 5
AHEAD = 8


def block_at(t, me):
    code = jnp.int32(0)
    for g in range(0, 64, PACK):
        word = 0
        for j, (dx, dy, dz) in enumerate(BLOCKS[g:g + PACK]):
            word += (dx + 4 * dy + 16 * dz) << (6 * j)
        code = jnp.where(t // PACK == g // PACK, jnp.int32(word), code)
    code = lax.shift_right_logical(code, 6 * (t % PACK)) % 64
    return ((me[0] + code % 4) % 4, (me[1] + code // 4 % 4) % 4, (me[2] + code // 16) % 4)


def position():
    b, r = lax.axis_index("blk"), lax.axis_index("row")
    return (b // 2, r % 4, r // 4), b % 2


def device(coord, core):
    return {"blk": 2 * coord[0] + core, "row": 4 * coord[2] + coord[1]}


def shifted(me, axis, by):
    out = list(me)
    out[axis] = (me[axis] + by) % 4
    return tuple(out)


def all_reduce_phases(part, res, near, rx, ry, rz, far_s, far_v, snd, rcv, me, core):
    half = core * 128
    row_x = half + 32 * me[0]
    row_y = row_x + 8 * me[1]
    partner = device(me, 1 - core)

    def rows(at, n):
        return pl.ds(pl.multiple_of(at, 8), n)

    def spread(phase, axis, src_of, dst_of):
        copies = []
        for by in (1, 2, 3):
            to = shifted(me, axis, by)
            copies.append(pltpu.make_async_remote_copy(
                src_of(to[axis]), dst_of(by), snd.at[phase, by - 1], rcv.at[phase, by - 1],
                device_id=device(to, core), device_id_type=MESH))
        return copies

    def pair(slot, src, dst):
        return pltpu.make_async_remote_copy(
            src, dst, far_s.at[slot], far_v.at[slot], device_id=partner, device_id_type=MESH)

    def begin(copies):
        for copy in copies:
            copy.start()

    def arrive(copies):
        for copy in copies:
            copy.wait_recv()

    first = [pair(0, part.at[rows((1 - core) * 128, 128)], near)]
    over_x = spread(0, 0, lambda i: part.at[rows(half + 32 * i, 32)], lambda by: rx.at[by - 1])
    over_y = spread(1, 1, lambda i: part.at[rows(row_x + 8 * i, 8)], lambda by: ry.at[by - 1])
    over_z = spread(2, 2, lambda i: part.at[rows(row_y, 8)], lambda by: rz.at[me[2]])
    back_y = spread(3, 1, lambda i: res.at[rows(row_y, 8)], lambda by: res.at[rows(row_y, 8)])
    back_x = spread(4, 0, lambda i: res.at[rows(row_x, 32)], lambda by: res.at[rows(row_x, 32)])
    last = [pair(1, res.at[rows(half, 128)], res.at[rows(half, 128)])]

    def end_core():
        arrive(first)
        part[rows(half, 128)] += near[...]

    def end_x():
        arrive(over_x)
        part[rows(row_x, 32)] += rx[0] + rx[1] + rx[2]

    def end_y():
        arrive(over_y)
        part[rows(row_y, 8)] += ry[0] + ry[1] + ry[2]

    def end_z():
        arrive(over_z)
        rz[me[2]] = part[rows(row_y, 8)]
        res[rows(row_y, 8)] = (rz[0] + rz[1]) + (rz[2] + rz[3])

    stages = [(first, end_core), (over_x, end_x), (over_y, end_y), (over_z, end_z),
              (back_y, lambda: arrive(back_y)), (back_x, lambda: arrive(back_x)), (last, lambda: arrive(last))]

    def drain():
        for copies, _ in stages:
            for copy in copies:
                copy.wait_send()

    return [(lambda c=copies: begin(c), end) for copies, end in stages], drain


def all_reduce_scratch():
    dma = pltpu.SemaphoreType.DMA
    return [pltpu.VMEM((256, 256), F32), pltpu.VMEM((128, 256), F32), pltpu.VMEM((3, 32, 256), F32),
            pltpu.VMEM((3, 8, 256), F32), pltpu.VMEM((4, 8, 256), F32),
            dma((2,)), dma((2,)), dma((5, 3)), dma((5, 3))]


def greet(peers):
    barrier = pltpu.get_barrier_semaphore()
    for p in peers:
        pl.semaphore_signal(barrier, inc=1, device_id=p, device_id_type=MESH)
    return lambda: pl.semaphore_wait(barrier, len(peers))


def split(value):
    high = value.astype(BF16)
    return high, (value - high.astype(F32)).astype(BF16)


def all_peers(me, core):
    return [device(shifted(me, a, s), core) for a in range(3) for s in (1, 2, 3)] + [device(me, 1 - core)]


def dot32(a, b):
    return jnp.dot(a, b, precision=lax.Precision.HIGHEST, preferred_element_type=F32)


def ridge_inverse_steps(gram, shifted_m, x, r):
    n = gram.shape[0]
    low = ridge_share / n / (1 + ridge_share)
    bound = (1 - low) / (1 + low)
    first = 2 / (1 + low)

    def eye():
        row = lax.broadcasted_iota(jnp.int32, (n, n), 0)
        col = lax.broadcasted_iota(jnp.int32, (n, n), 1)
        return jnp.where(row == col, F32(1), F32(0))

    def inverse_trace():
        return 1.0 / jnp.sum(jnp.sum(shifted_m[...] * eye(), axis=0, keepdims=True), axis=1, keepdims=True)

    def begin():
        g = gram[...]
        one = eye()
        g = 0.5 * (g + g.T)
        trace = jnp.sum(jnp.sum(g * one, axis=0, keepdims=True), axis=1, keepdims=True)
        shifted_m[...] = g + one * (trace * (ridge_share / n))
        x[...] = first * one
        r[...] = one - shifted_m[...] * (inverse_trace() * first)

    def square(scale):
        def step():
            res = r[...]
            x[...] = scale * (x[...] + dot32(x[...], res))
            r[...] = (1 - scale) * eye() + scale * dot32(res, res)

        return step

    def correct(last):
        def step():
            scale = inverse_trace()
            err = eye() - dot32(shifted_m[...] * scale, x[...])
            new = x[...] + dot32(x[...], err)
            x[...] = new * scale if last else new

        return step

    steps = [begin]
    while bound > 1e-2:
        scale = 2 / (2 - bound * bound)
        steps.append(square(scale))
        bound = bound * bound / (2 - bound * bound)
    return steps + [correct(False), correct(False), correct(True)]


def reduce_kernel(fib, table_b, table_c, idx_b, idx_c, weight, count, factor, ssum, shifted_m,
                  fo, fp, wt_own, wt_far, part, r1, r2, r3, tot, out, gram, inv, res, own,
                  fo_sem, fs_sem, fr_sem, w_sem, s1, v1, s2, v2, s3, v3, own_sem, x_s, x_v, c_s, c_v, t_sem, *sums):
    gram_scratch, s_scratch = sums[:9], sums[9:]
    me, core = position()
    all_entered = greet(all_peers(me, core))
    chunks_b, chunks_c = table_b.shape[0] // 256, table_c.shape[0] // 256

    def chunk_slot(i):
        return (i // 16, i // 4 % 4, i % 4, slice(None), pl.ds(0, 256))

    def load_chunk(table, i, first):
        rows = pl.ds(pl.multiple_of(256 * i, 256), 256)
        return pltpu.make_async_copy(table.at[rows], part.at[chunk_slot(first + i)], t_sem.at[first + i])

    for table, count_of, first in ((table_b, chunks_b, 0), (table_c, chunks_c, chunks_b)):
        @pl.loop(0, count_of)
        def _(i):
            load_chunk(table, i, first).start()
    partner = device(me, 1 - core)

    near = [[(me[a] + by) % 4 for by in range(4)] for a in range(3)]
    bases = [near[1][by] * 4096 for by in range(4)], [near[2][by] * 16384 for by in range(4)]

    def column(t, k):
        dx, dy, dz = BLOCKS[t]
        return pl.multiple_of(bases[1][dz] + bases[0][dy] + near[0][dx] * 1024 + k * SUB, SUB)

    def local_copy(t, at):
        return pltpu.make_async_copy(fib.at[:, pl.ds(at, SUB)], fo.at[t], fo_sem.at[t])

    def far_copy(t, at):
        return pltpu.make_async_remote_copy(
            fib.at[:, pl.ds(at, SUB)], fp.at[t], fs_sem.at[t], fr_sem.at[t],
            device_id=partner, device_id_type=MESH)

    wt_copy = pltpu.make_async_remote_copy(
        wt_own, wt_far, w_sem.at[0], w_sem.at[1], device_id=partner, device_id_type=MESH)
    gram_phases, gram_drain = all_reduce_phases(gram_scratch[0], gram, *gram_scratch[1:], me, core)

    s_phases, s_drain = all_reduce_phases(s_scratch[0], ssum, *s_scratch[1:], me, core)
    inverse_steps = ridge_inverse_steps(gram, shifted_m, inv, res)

    def inverse_step(count):
        for _ in range(min(count, len(inverse_steps))):
            inverse_steps.pop(0)()

    def gram_step(p):
        gram_phases[p][1]()
        if p < 6:
            gram_phases[p + 1][0]()

    for t in range(64):
        local_copy(t, column(t, core)).start()

    cap = weight.shape[1]
    lane = lax.broadcasted_iota(jnp.int32, (cap, 256), 1).astype(F32)
    diagonal = lax.broadcasted_iota(jnp.int32, (cap, cap), 0) == lax.broadcasted_iota(jnp.int32, (cap, cap), 1)

    def gather_rows(table, idx, chunks, first):
        at = jnp.sum(jnp.where(diagonal, idx[...].astype(F32), F32(0)), axis=1, keepdims=True)

        def body(i, total):
            load_chunk(table, i, first).wait()
            hot = jnp.where(at == lane + (256 * i).astype(F32), F32(1), F32(0)).astype(BF16)
            return total + jnp.dot(hot, part[chunk_slot(first + i)], preferred_element_type=F32)

        return lax.fori_loop(0, chunks, body, jnp.zeros((cap, 256), F32), unroll=4)

    kr = (gather_rows(table_b, idx_b, chunks_b, 0) * gather_rows(table_c, idx_c, chunks_c, chunks_b)).astype(BF16)
    slot = lax.broadcasted_iota(jnp.int32, (1, cap), 1)
    scale = jnp.where(slot < count[0], weight[...].astype(F32), F32(0))
    wt_own[...] = (scale * kr.T.astype(F32)).astype(BF16)
    gram_scratch[0][...] = jnp.dot(wt_own[...], kr, preferred_element_type=F32)

    all_entered()
    wt_copy.start()
    gram_phases[0][0]()

    far_started = [0]

    def start_far(upto):
        for t in range(far_started[0], min(upto, 64)):
            far_copy(t, column(t, 1 - core)).start()
        far_started[0] = max(far_started[0], min(upto, 64))

    start_far(ENDS["across", 0, 2])
    wt_copy.wait()

    done = [0]

    def need(kind, i, c):
        lo, hi = done[0], ENDS[kind, i, c]
        if hi <= lo:
            return
        done[0] = hi
        start_far(hi + AHEAD)

        @pl.loop(lo, hi)
        def _(t):
            local_copy(t, 0).wait()
            far_copy(t, 0).wait_recv()
            x, y, z = block_at(t, me)
            acc = jnp.dot(wt_own[...], fo[t], preferred_element_type=F32)
            acc += jnp.dot(wt_far[...], fp[t], preferred_element_type=F32)
            part[x, y, z] = acc.astype(BF16)

    def rank(c, h):
        return pl.ds(R0[h][c], RC[h][c])

    def lanes(h):
        return pl.ds(h * (SUB // 2), SUB // 2)

    def place(c, i1, i2, i3):
        at = [None] * 3
        at[ORDER[c][0]], at[ORDER[c][1]], at[ORDER[c][2]] = i1, i2, i3
        return tuple(at)

    def half_of(kind, d):
        return d if kind < 2 else 1 - d

    def dest_step(kind, d):
        return 2 if kind == 0 else (1, 3)[d]

    def slab1(c, d1, e, h):
        i1 = (me[ORDER[c][0]] + d1) % 4
        i2 = (me[ORDER[c][1]] + e) % 4
        return place(c, i1, i2, slice(None)) + (rank(c, h), lanes(h))

    def msg1(kind, d, i, c):
        h = half_of(kind, d)
        if kind == 1:
            src = r1.at[0, d, i, :, rank(c, h)]
        else:
            src = part.at[slab1(c, dest_step(kind, d), STEPS[i], h)]
        return pltpu.make_async_remote_copy(
            src, r1.at[kind, d, i, :, rank(c, h)], s1.at[kind, d, i, c], v1.at[kind, d, i, c],
            device_id=device(shifted(me, ORDER[c][0], (1, 3)[d]), core), device_id_type=MESH)

    def slab2(c, e, h):
        return slab1(c, 0, e, h)

    def msg2(kind, d, c):
        h = half_of(kind, d)
        if kind == 1:
            src = r2.at[0, d, :, rank(c, h)]
        else:
            src = part.at[slab2(c, dest_step(kind, d), h)]
        return pltpu.make_async_remote_copy(
            src, r2.at[kind, d, :, rank(c, h)], s2.at[kind, d, c], v2.at[kind, d, c],
            device_id=device(shifted(me, ORDER[c][1], (1, 3)[d]), core), device_id_type=MESH)

    def msg3(kind, d, c):
        h = half_of(kind, d)
        if kind == 1:
            src = r3.at[0, d, rank(c, h)]
        else:
            f = (me[ORDER[c][2]] + dest_step(kind, d)) % 4
            src = tot.at[f, rank(c, h), lanes(h)]
        return pltpu.make_async_remote_copy(
            src, r3.at[kind, d, rank(c, h)], s3.at[kind, d, c], v3.at[kind, d, c],
            device_id=device(shifted(me, ORDER[c][2], (1, 3)[d]), core), device_id_type=MESH)

    def rows16(c, h, body):
        @pl.loop(0, RC[h][c] // 16)
        def _(j):
            body(pl.ds(pl.multiple_of(R0[h][c] + 16 * j, 16), 16))

    def forward1(d, i, c):
        msg1(0, d, i, c).wait_recv()
        at = slab1(c, (1, 3)[d], STEPS[i], d)

        def body(rows):
            mine = part[at[:3] + (rows, lanes(d))].astype(F32)
            r1[0, d, i, :, rows] = (r1[0, d, i, :, rows].astype(F32) + mine).astype(BF16)

        rows16(c, d, body)
        msg1(1, d, i, c).start()

    def finish1(i, c):
        for d in range(2):
            msg1(2, d, i, c).wait_recv()
        for d in range(2):
            msg1(1, d, i, c).wait_recv()
        for h in range(2):
            at = slab1(c, 0, STEPS[i], h)

            def body(rows):
                total = (r1[1, h, i, :, rows].astype(F32) + r1[2, 1 - h, i, :, rows].astype(F32)
                         + part[at[:3] + (rows, lanes(h))].astype(F32))
                if STEPS[i] == 0:
                    tot[:, rows, lanes(h)] = total
                else:
                    part[at[:3] + (rows, lanes(h))] = total.astype(BF16)

            rows16(c, h, body)

    def forward2(d, c):
        msg2(0, d, c).wait_recv()
        at = slab2(c, (1, 3)[d], d)

        def body(rows):
            mine = part[at[:3] + (rows, lanes(d))].astype(F32)
            r2[0, d, :, rows] = (r2[0, d, :, rows].astype(F32) + mine).astype(BF16)

        rows16(c, d, body)
        msg2(1, d, c).start()

    def send1(kind, i, c):
        need(("across", None, "near")[kind], i, c)
        for d in range(2):
            msg1(kind, d, i, c).start()

    for c in range(3):
        send1(0, 0, c)
    gram_step(0)
    for c in range(3):
        send1(2, 0, c)
    gram_step(1)

    for i in range(4):
        for c in range(3):
            for d in range(2):
                forward1(d, i, c)
        if i < 3:
            for c in range(3):
                send1(0, i + 1, c)
            gram_step((2, 4, 6)[i])
            for c in range(3):
                send1(2, i + 1, c)
        if i > 1:
            inverse_step(3 if i == 2 else 99)
        for c in range(3):
            need("own", i, c)
        for c in range(3):
            finish1(i, c)
            if i == 0:
                for d in range(2):
                    msg2(0, d, c).start()
            elif i < 3:
                d = i - 1
                msg2(2, d, c).start()
                forward2(d, c)
        if i < 2:
            gram_step((3, 5)[i])
        elif i == 2:
            inverse_step(4)

    for c in range(3):
        for d in range(2):
            msg2(2, d, c).wait_recv()
            msg2(1, d, c).wait_recv()
        for h in range(2):
            def body(rows):
                tot[:, rows, lanes(h)] += r2[1, h, :, rows].astype(F32) + r2[2, 1 - h, :, rows].astype(F32)

            rows16(c, h, body)
        for kind in (0, 2):
            for d in range(2):
                msg3(kind, d, c).start()
    for c in range(3):
        for d in range(2):
            msg3(0, d, c).wait_recv()
            f = (me[ORDER[c][2]] + (1, 3)[d]) % 4

            def body(rows):
                r3[0, d, rows] += tot[f, rows, lanes(d)]

            rows16(c, d, body)
            msg3(1, d, c).start()
    for c in range(3):
        for d in range(2):
            msg3(2, d, c).wait_recv()
            msg3(1, d, c).wait_recv()
        mine = me[ORDER[c][2]]
        for h in range(2):
            def body(rows):
                out[rows, lanes(h)] = tot[mine, rows, lanes(h)] + r3[1, h, rows] + r3[2, 1 - h, rows]

            rows16(c, h, body)

    high, low = split(out[...])
    cross = lax.dot_general(high, low, (((1,), (1,)), ((), ())), preferred_element_type=F32)
    s_scratch[0][...] = lax.dot_general(
        high, high, (((1,), (1,)), ((), ())), preferred_element_type=F32) + (cross + cross.T)
    s_phases[0][0]()
    inv_high, inv_low = split(inv[...])
    first_dims = (((0,), (0,)), ((), ()))
    own[...] = (lax.dot_general(high, inv_high, first_dims, preferred_element_type=F32)
                + (lax.dot_general(high, inv_low, first_dims, preferred_element_type=F32)
                   + lax.dot_general(low, inv_high, first_dims, preferred_element_type=F32))).astype(BF16)

    def block(by, k):
        return factor.at[pl.ds(pl.multiple_of((2 * ((me[0] + 4 - by) % 4) + k) * SUB, SUB), SUB)]

    over_x = [pltpu.make_async_remote_copy(
        own, block(0, core), x_s.at[by - 1], x_v.at[by - 1],
        device_id=device(shifted(me, 0, by), core), device_id_type=MESH) for by in (1, 2, 3)]
    over_core = [pltpu.make_async_remote_copy(
        own if by == 0 else block(by, core), block(by, core),
        c_s.at[by], c_v.at[by], device_id=partner, device_id_type=MESH) for by in range(4)]
    own_copy = pltpu.make_async_copy(own, block(0, core), own_sem.at[0])
    s_phases[0][1]()
    s_phases[1][0]()
    for copy in over_x:
        copy.start()
    over_core[0].start()
    own_copy.start()
    s_phases[1][1]()
    for p in range(2, 5):
        s_phases[p][0]()
        s_phases[p][1]()
    s_phases[5][0]()
    for by in (1, 3, 2):
        over_x[by - 1].wait_recv()
        over_core[by].start()
    s_phases[5][1]()
    s_phases[6][0]()
    s_phases[6][1]()
    for by in range(4):
        over_core[by].wait_recv()

    own_copy.wait()
    for copy in over_x + over_core:
        copy.wait_send()
    s_drain()
    for c in range(3):
        for kind in range(3):
            for d in range(2):
                for i in range(4):
                    msg1(kind, d, i, c).wait_send()
                msg2(kind, d, c).wait_send()
                msg3(kind, d, c).wait_send()

    @pl.loop(0, 64)
    def _(t):
        far_copy(t, 0).wait_send()

    gram_drain()


def update_factor(fibers, table_b, table_c, idx_b, idx_c, weight, count):
    cap = fibers.shape[0]
    dma = pltpu.SemaphoreType.DMA
    vmem = pltpu.VMEM
    square = jax.ShapeDtypeStruct((256, 256), F32)
    return pl.pallas_call(
        reduce_kernel,
        name="update_factor",
        out_shape=(jax.ShapeDtypeStruct((8 * SUB, 256), BF16), square, square),
        in_specs=[pl.BlockSpec(memory_space=pl.ANY)] * 3 + [pl.BlockSpec(memory_space=pltpu.VMEM)] * 3
        + [pl.BlockSpec(memory_space=pltpu.SMEM)],
        out_specs=[pl.BlockSpec(memory_space=pl.ANY)] + [pl.BlockSpec(memory_space=pltpu.VMEM)] * 2,
        scratch_shapes=[
            vmem((64, cap, SUB), BF16), vmem((64, cap, SUB), BF16), vmem((256, cap), BF16), vmem((256, cap), BF16),
            vmem((4, 4, 4, 256, SUB), BF16),
            vmem((3, 2, 4, 4, 256, SUB // 2), BF16), vmem((3, 2, 4, 256, SUB // 2), BF16),
            vmem((3, 2, 256, SUB // 2), F32), vmem((4, 256, SUB), F32),
            vmem((256, SUB), F32), vmem((256, 256), F32), vmem((256, 256), F32), vmem((256, 256), F32),
            vmem((SUB, 256), BF16),
            dma((64,)), dma((64,)), dma((64,)), dma((2,)),
            dma((3, 2, 4, 3)), dma((3, 2, 4, 3)), dma((3, 2, 3)), dma((3, 2, 3)), dma((3, 2, 3)), dma((3, 2, 3)),
            dma((1,)), dma((3,)), dma((3,)), dma((4,)), dma((4,)), dma((48,)),
        ] + all_reduce_scratch() * 2,
        compiler_params=pltpu.CompilerParams(
            collective_id=0, has_side_effects=True, vmem_limit_bytes=63 * 1024 * 1024),
    )(fibers, table_b, table_c, idx_b, idx_c, weight, count)


def dot16(a, b):
    return jnp.dot(a.astype(BF16), b.astype(BF16), preferred_element_type=F32)


def invert(a_ref, x_ref, r_ref, between):
    n = a_ref.shape[0]
    row = lax.broadcasted_iota(jnp.int32, (n, n), 0)
    col = lax.broadcasted_iota(jnp.int32, (n, n), 1)
    eye = jnp.where(row == col, F32(1), F32(0))
    a = a_ref[...]
    diag = jnp.where(row == col, a, F32(0))
    s_col = lax.rsqrt(jnp.sum(diag, axis=1, keepdims=True))
    s_row = lax.rsqrt(jnp.sum(diag, axis=0, keepdims=True))
    a_ref[...] = a * s_col * s_row
    bound = jnp.max(jnp.sum(jnp.abs(a_ref[...]), axis=0, keepdims=True))
    alpha = 1.9 / bound
    x_ref[...] = alpha * eye
    r_ref[...] = eye - alpha * a_ref[...]

    def coarse(carry):
        it, _ = carry
        r = r_ref[...]
        x = x_ref[...]
        x_ref[...] = x + dot16(x, r)
        r = dot16(r, r)
        r_ref[...] = r
        return it + 1, jnp.sum(r * r)

    lax.while_loop(lambda c: (c[0] < 24) & (c[1] > 1e-3), coarse, (jnp.int32(0), F32(1e9)))

    between()

    def fine(carry):
        it, last, _ = carry
        x = x_ref[...]
        e = (row == col).astype(F32) - dot32(a_ref[...], x)
        size = jnp.sum(e * e)
        reset = (it == 0) & jnp.logical_not(size < 0.25)
        stop = (size < 1e-8) | ((size < 1e-3) & (size > 0.25 * last))

        @pl.when(reset)
        def _():
            x_ref[...] = alpha * (row == col).astype(F32)

        @pl.when(jnp.logical_not(reset))
        def _():
            x_ref[...] = x + dot32(x, e)

        return it + 1, jnp.where(reset, F32(1e30), size), stop.astype(jnp.int32)

    lax.while_loop(lambda c: (c[0] < 80) & (c[2] == 0), fine, (jnp.int32(0), F32(1e30), jnp.int32(0)))
    x_ref[...] = x_ref[...] * s_col * s_row


def leverage_kernel(scale, factor, smat, shifted_m, out, lev, work, inv, res, rows, held, sem):
    take = pltpu.make_async_copy(factor, held, sem.at[0])
    give = pltpu.make_async_copy(held, out, sem.at[1])
    take.start()

    def pass_on():
        take.wait()
        give.start()

    work[...] = smat[...]
    invert(work, inv, res, pass_on)
    a = shifted_m[...]
    hinv = dot32(a, dot32(inv[...], a))
    high = hinv.astype(BF16)
    low = (hinv - high.astype(F32)).astype(BF16)
    ones = jnp.full((8, 256), 1.0, BF16)
    over = (((1,), (1,)), ((), ()))

    @pl.loop(0, 8)
    def _(j):
        at = pl.ds(pl.multiple_of(j * SUB, SUB), SUB)
        f = held[at]
        quad = (jnp.dot(f, high, preferred_element_type=F32) + jnp.dot(f, low, preferred_element_type=F32)) * f.astype(F32)
        quad = quad[:, :128] + quad[:, 128:]
        q_high = quad.astype(BF16)
        q_low = (quad - q_high.astype(F32)).astype(BF16)
        total = lax.dot_general(ones, jnp.concatenate([q_high, q_low], axis=1), over, preferred_element_type=F32)
        for k in range(SUB // 128):
            rows[pl.ds(j * (SUB // 128) + k, 1)] = total[0:1, 128 * k:128 * (k + 1)]

    lev[...] = (scale * rows[...]).astype(BF16)
    give.wait()


def leverage_of(factor, smat, shifted_m, scale):
    rows = factor.shape[0]
    out, lev = pl.pallas_call(
        lambda *refs: leverage_kernel(scale, *refs), name="leverage",
        out_shape=(jax.ShapeDtypeStruct((rows, 256), BF16), jax.ShapeDtypeStruct((rows // 128, 128), BF16)),
        in_specs=[pl.BlockSpec(memory_space=pl.ANY)] + [pl.BlockSpec(memory_space=pltpu.VMEM)] * 2,
        out_specs=[pl.BlockSpec(memory_space=pl.ANY), pl.BlockSpec(memory_space=pltpu.VMEM)],
        scratch_shapes=[pltpu.VMEM((256, 256), F32)] * 3 + [
            pltpu.VMEM((rows // 128, 128), F32), pltpu.VMEM((rows, 256), BF16), pltpu.SemaphoreType.DMA((2,))],
    )(factor, smat, shifted_m)
    return out, lev.reshape(rows)


def local(fibers, factor_b, factor_c, mode2_idx, mode3_idx, sample_wt, counts):
    slot_cap, row_total = fibers.shape
    rank_width = factor_c.shape[1]
    row = (1, slot_cap)
    factor, ssum, shifted_m = update_factor(
        fibers, factor_b, factor_c, mode2_idx.reshape(row), mode3_idx.reshape(row), sample_wt.reshape(row), counts)
    return leverage_of(factor, ssum, shifted_m, row_total / rank_width)


def solution(mesh):
    placed = (
        P(("blk", "row"), None),
        P("blk", None),
        P(),
        P(("blk", "row")),
        P(("blk", "row")),
        P(("blk", "row")),
        P(("blk", "row")),
    )
    return jax.shard_map(
        local, mesh=mesh, in_specs=placed, out_specs=(P("row", None), P("row")), check_vma=False
    )
```

```python
import jax
import jax.numpy as jnp
from jax import lax
from jax.experimental import pallas as pl
from jax.experimental.pallas import tpu as pltpu
from jax.sharding import PartitionSpec as P

ridge_share = 0.05
MESH = pl.DeviceIdType.MESH
F32 = jnp.float32
BF16 = jnp.bfloat16

ORDER = ((0, 1, 2), (1, 2, 0), (2, 0, 1))
R0 = ((0, 96, 176), (0, 80, 176))
RC = ((96, 80, 80), (80, 96, 80))
STEPS = (2, 1, 3, 0)
SUB = 512


def block_lines(kind, i, color):
    d2 = STEPS[i]
    lines = []
    for d1 in {"across": (2,), "near": (1, 3), "own": (0,)}[kind]:
        for d3 in range(4):
            off = [0, 0, 0]
            off[ORDER[color][0]], off[ORDER[color][1]], off[ORDER[color][2]] = d1, d2, d3
            lines.append(tuple(off))
    return lines


def block_order():
    order, ends = [], {}
    needs = [("across", 0), ("near", 0), ("across", 1), ("near", 1), ("own", 0)]
    for i in (2, 3):
        needs += [("across", i), ("near", i), ("own", i - 1)]
    needs += [("own", 3)]
    for kind, i in needs:
        for color in range(3):
            for off in block_lines(kind, i, color):
                if off not in order:
                    order.append(off)
            ends[kind, i, color] = len(order)
    return order, ends


BLOCKS, ENDS = block_order()
PACK = 5
AHEAD = 8


def block_at(t, me):
    code = jnp.int32(0)
    for g in range(0, 64, PACK):
        word = 0
        for j, (dx, dy, dz) in enumerate(BLOCKS[g:g + PACK]):
            word += (dx + 4 * dy + 16 * dz) << (6 * j)
        code = jnp.where(t // PACK == g // PACK, jnp.int32(word), code)
    code = lax.shift_right_logical(code, 6 * (t % PACK)) % 64
    return ((me[0] + code % 4) % 4, (me[1] + code // 4 % 4) % 4, (me[2] + code // 16) % 4)


def position():
    b, r = lax.axis_index("blk"), lax.axis_index("row")
    return (b // 2, r % 4, r // 4), b % 2


def device(coord, core):
    return {"blk": 2 * coord[0] + core, "row": 4 * coord[2] + coord[1]}


def shifted(me, axis, by):
    out = list(me)
    out[axis] = (me[axis] + by) % 4
    return tuple(out)


def all_reduce_phases(part, res, near, rx, ry, mid, rz, far_s, far_v, snd, rcv, me, core):
    half = core * 128
    row_x = half + 32 * me[0]
    partner = device(me, 1 - core)

    def rows(at, n):
        return pl.ds(pl.multiple_of(at, 8), n)

    def spread(phase, axis, src_of, dst_of):
        copies = []
        for by in (1, 2, 3):
            to = shifted(me, axis, by)
            copies.append(pltpu.make_async_remote_copy(
                src_of(to[axis]), dst_of(by), snd.at[phase, by - 1], rcv.at[phase, by - 1],
                device_id=device(to, core), device_id_type=MESH))
        return copies

    def pair(slot, src, dst):
        return pltpu.make_async_remote_copy(
            src, dst, far_s.at[slot], far_v.at[slot], device_id=partner, device_id_type=MESH)

    def begin(copies):
        for copy in copies:
            copy.start()

    def arrive(copies):
        for copy in copies:
            copy.wait_recv()

    first = [pair(0, part.at[rows((1 - core) * 128, 128)], near)]
    over_x = spread(0, 0, lambda i: part.at[rows(half + 32 * i, 32)], lambda by: rx.at[by - 1])
    over_y = spread(1, 1, lambda i: part.at[rows(row_x, 32)], lambda by: ry.at[me[1]])
    over_z = spread(2, 2, lambda i: mid, lambda by: rz.at[me[2]])
    back_x = spread(3, 0, lambda i: res.at[rows(row_x, 32)], lambda by: res.at[rows(row_x, 32)])
    last = [pair(1, res.at[rows(half, 128)], res.at[rows(half, 128)])]

    def end_core():
        arrive(first)
        part[rows(half, 128)] += near[...]

    def end_x():
        arrive(over_x)
        part[rows(row_x, 32)] += rx[0] + rx[1] + rx[2]

    def end_y():
        arrive(over_y)
        ry[me[1]] = part[rows(row_x, 32)]
        mid[...] = (ry[0] + ry[1]) + (ry[2] + ry[3])

    def end_z():
        arrive(over_z)
        rz[me[2]] = mid[...]
        res[rows(row_x, 32)] = (rz[0] + rz[1]) + (rz[2] + rz[3])

    stages = [(first, end_core), (over_x, end_x), (over_y, end_y), (over_z, end_z),
              (back_x, lambda: arrive(back_x)), (last, lambda: arrive(last))]

    def drain():
        for copies, _ in stages:
            for copy in copies:
                copy.wait_send()

    return [(lambda c=copies: begin(c), end) for copies, end in stages], drain


def all_reduce_scratch():
    dma = pltpu.SemaphoreType.DMA
    return [pltpu.VMEM((256, 256), F32), pltpu.VMEM((128, 256), F32), pltpu.VMEM((3, 32, 256), F32),
            pltpu.VMEM((4, 32, 256), F32), pltpu.VMEM((32, 256), F32), pltpu.VMEM((4, 32, 256), F32),
            dma((2,)), dma((2,)), dma((4, 3)), dma((4, 3))]


def greet(peers):
    barrier = pltpu.get_barrier_semaphore()
    for p in peers:
        pl.semaphore_signal(barrier, inc=1, device_id=p, device_id_type=MESH)
    return lambda: pl.semaphore_wait(barrier, len(peers))


def split(value):
    high = value.astype(BF16)
    return high, (value - high.astype(F32)).astype(BF16)


def all_peers(me, core):
    return [device(shifted(me, a, s), core) for a in range(3) for s in (1, 2, 3)] + [device(me, 1 - core)]


def dot32(a, b):
    return jnp.dot(a, b, precision=lax.Precision.HIGHEST, preferred_element_type=F32)


def ridge_inverse_steps(gram, shifted_m, x, r):
    n = gram.shape[0]
    low = ridge_share / n / (1 + ridge_share)
    bound = (1 - low) / (1 + low)
    first = 2 / (1 + low)

    def eye():
        row = lax.broadcasted_iota(jnp.int32, (n, n), 0)
        col = lax.broadcasted_iota(jnp.int32, (n, n), 1)
        return jnp.where(row == col, F32(1), F32(0))

    def inverse_trace():
        return 1.0 / jnp.sum(jnp.sum(shifted_m[...] * eye(), axis=0, keepdims=True), axis=1, keepdims=True)

    def begin():
        g = gram[...]
        one = eye()
        g = 0.5 * (g + g.T)
        trace = jnp.sum(jnp.sum(g * one, axis=0, keepdims=True), axis=1, keepdims=True)
        shifted_m[...] = g + one * (trace * (ridge_share / n))
        x[...] = first * one
        r[...] = one - shifted_m[...] * (inverse_trace() * first)

    def square(scale):
        def step():
            res = r[...]
            x[...] = scale * (x[...] + dot32(x[...], res))
            r[...] = (1 - scale) * eye() + scale * dot32(res, res)

        return step

    def correct(last):
        def step():
            scale = inverse_trace()
            err = eye() - dot32(shifted_m[...] * scale, x[...])
            new = x[...] + dot32(x[...], err)
            x[...] = new * scale if last else new

        return step

    steps = [begin]
    while bound > 1e-2:
        scale = 2 / (2 - bound * bound)
        steps.append(square(scale))
        bound = bound * bound / (2 - bound * bound)
    return steps + [correct(False), correct(False), correct(True)]


def reduce_kernel(fib, table_b, table_c, idx_b, idx_c, weight, count, factor, ssum, shifted_m,
                  fo, fp, wt_own, wt_far, part, r1, r2, r3, tot, out, gram, inv, res, own,
                  fo_sem, fs_sem, fr_sem, w_sem, s1, v1, s2, v2, s3, v3, own_sem, x_s, x_v, c_s, c_v, t_sem, *sums):
    gram_scratch, s_scratch = sums[:10], sums[10:]
    me, core = position()
    all_entered = greet(all_peers(me, core))
    chunks_b, chunks_c = table_b.shape[0] // 256, table_c.shape[0] // 256

    def chunk_slot(i):
        return (i // 16, i // 4 % 4, i % 4, slice(None), pl.ds(0, 256))

    def load_chunk(table, i, first):
        rows = pl.ds(pl.multiple_of(256 * i, 256), 256)
        return pltpu.make_async_copy(table.at[rows], part.at[chunk_slot(first + i)], t_sem.at[first + i])

    for table, count_of, first in ((table_b, chunks_b, 0), (table_c, chunks_c, chunks_b)):
        @pl.loop(0, count_of)
        def _(i):
            load_chunk(table, i, first).start()
    partner = device(me, 1 - core)

    near = [[(me[a] + by) % 4 for by in range(4)] for a in range(3)]
    bases = [near[1][by] * 4096 for by in range(4)], [near[2][by] * 16384 for by in range(4)]

    def column(t, k):
        dx, dy, dz = BLOCKS[t]
        return pl.multiple_of(bases[1][dz] + bases[0][dy] + near[0][dx] * 1024 + k * SUB, SUB)

    def local_copy(t, at):
        return pltpu.make_async_copy(fib.at[:, pl.ds(at, SUB)], fo.at[t], fo_sem.at[t])

    def far_copy(t, at):
        return pltpu.make_async_remote_copy(
            fib.at[:, pl.ds(at, SUB)], fp.at[t], fs_sem.at[t], fr_sem.at[t],
            device_id=partner, device_id_type=MESH)

    wt_copy = pltpu.make_async_remote_copy(
        wt_own, wt_far, w_sem.at[0], w_sem.at[1], device_id=partner, device_id_type=MESH)
    gram_phases, gram_drain = all_reduce_phases(gram_scratch[0], gram, *gram_scratch[1:], me, core)

    s_phases, s_drain = all_reduce_phases(s_scratch[0], ssum, *s_scratch[1:], me, core)
    inverse_steps = ridge_inverse_steps(gram, shifted_m, inv, res)

    def inverse_step(count):
        for _ in range(min(count, len(inverse_steps))):
            inverse_steps.pop(0)()

    def gram_step(p):
        gram_phases[p][1]()
        if p < 5:
            gram_phases[p + 1][0]()

    for t in range(64):
        local_copy(t, column(t, core)).start()

    cap = weight.shape[1]
    lane = lax.broadcasted_iota(jnp.int32, (cap, 256), 1).astype(F32)
    diagonal = lax.broadcasted_iota(jnp.int32, (cap, cap), 0) == lax.broadcasted_iota(jnp.int32, (cap, cap), 1)

    def gather_rows(table, idx, chunks, first):
        at = jnp.sum(jnp.where(diagonal, idx[...].astype(F32), F32(0)), axis=1, keepdims=True)

        def body(i, total):
            load_chunk(table, i, first).wait()
            hot = jnp.where(at == lane + (256 * i).astype(F32), F32(1), F32(0)).astype(BF16)
            return total + jnp.dot(hot, part[chunk_slot(first + i)], preferred_element_type=F32)

        return lax.fori_loop(0, chunks, body, jnp.zeros((cap, 256), F32), unroll=4)

    kr = (gather_rows(table_b, idx_b, chunks_b, 0) * gather_rows(table_c, idx_c, chunks_c, chunks_b)).astype(BF16)
    slot = lax.broadcasted_iota(jnp.int32, (1, cap), 1)
    scale = jnp.where(slot < count[0], weight[...].astype(F32), F32(0))
    wt_own[...] = (scale * kr.T.astype(F32)).astype(BF16)
    gram_scratch[0][...] = jnp.dot(wt_own[...], kr, preferred_element_type=F32)

    all_entered()
    wt_copy.start()
    gram_phases[0][0]()

    far_started = [0]

    def start_far(upto):
        for t in range(far_started[0], min(upto, 64)):
            far_copy(t, column(t, 1 - core)).start()
        far_started[0] = max(far_started[0], min(upto, 64))

    start_far(ENDS["across", 0, 2])
    wt_copy.wait()

    done = [0]

    def need(kind, i, c):
        lo, hi = done[0], ENDS[kind, i, c]
        if hi <= lo:
            return
        done[0] = hi
        start_far(hi + AHEAD)

        @pl.loop(lo, hi)
        def _(t):
            local_copy(t, 0).wait()
            far_copy(t, 0).wait_recv()
            x, y, z = block_at(t, me)
            acc = jnp.dot(wt_own[...], fo[t], preferred_element_type=F32)
            acc += jnp.dot(wt_far[...], fp[t], preferred_element_type=F32)
            part[x, y, z] = acc.astype(BF16)

    def rank(c, h):
        return pl.ds(R0[h][c], RC[h][c])

    def lanes(h):
        return pl.ds(h * (SUB // 2), SUB // 2)

    def place(c, i1, i2, i3):
        at = [None] * 3
        at[ORDER[c][0]], at[ORDER[c][1]], at[ORDER[c][2]] = i1, i2, i3
        return tuple(at)

    def half_of(kind, d):
        return d if kind < 2 else 1 - d

    def dest_step(kind, d):
        return 2 if kind == 0 else (1, 3)[d]

    def slab1(c, d1, e, h):
        i1 = (me[ORDER[c][0]] + d1) % 4
        i2 = (me[ORDER[c][1]] + e) % 4
        return place(c, i1, i2, slice(None)) + (rank(c, h), lanes(h))

    def msg1(kind, d, i, c):
        h = half_of(kind, d)
        if kind == 1:
            src = r1.at[0, d, i, :, rank(c, h)]
        else:
            src = part.at[slab1(c, dest_step(kind, d), STEPS[i], h)]
        return pltpu.make_async_remote_copy(
            src, r1.at[kind, d, i, :, rank(c, h)], s1.at[kind, d, i, c], v1.at[kind, d, i, c],
            device_id=device(shifted(me, ORDER[c][0], (1, 3)[d]), core), device_id_type=MESH)

    def slab2(c, e, h):
        return slab1(c, 0, e, h)

    def msg2(kind, d, c):
        h = half_of(kind, d)
        if kind == 1:
            src = r2.at[0, d, :, rank(c, h)]
        else:
            src = part.at[slab2(c, dest_step(kind, d), h)]
        return pltpu.make_async_remote_copy(
            src, r2.at[kind, d, :, rank(c, h)], s2.at[kind, d, c], v2.at[kind, d, c],
            device_id=device(shifted(me, ORDER[c][1], (1, 3)[d]), core), device_id_type=MESH)

    def msg3(kind, d, c):
        h = half_of(kind, d)
        if kind == 1:
            src = r3.at[0, d, rank(c, h)]
        else:
            f = (me[ORDER[c][2]] + dest_step(kind, d)) % 4
            src = tot.at[f, rank(c, h), lanes(h)]
        return pltpu.make_async_remote_copy(
            src, r3.at[kind, d, rank(c, h)], s3.at[kind, d, c], v3.at[kind, d, c],
            device_id=device(shifted(me, ORDER[c][2], (1, 3)[d]), core), device_id_type=MESH)

    def rows16(c, h, body):
        @pl.loop(0, RC[h][c] // 16)
        def _(j):
            body(pl.ds(pl.multiple_of(R0[h][c] + 16 * j, 16), 16))

    def forward1(d, i, c):
        msg1(0, d, i, c).wait_recv()
        at = slab1(c, (1, 3)[d], STEPS[i], d)

        def body(rows):
            mine = part[at[:3] + (rows, lanes(d))].astype(F32)
            r1[0, d, i, :, rows] = (r1[0, d, i, :, rows].astype(F32) + mine).astype(BF16)

        rows16(c, d, body)
        msg1(1, d, i, c).start()

    def finish1(i, c):
        for d in range(2):
            msg1(2, d, i, c).wait_recv()
        for d in range(2):
            msg1(1, d, i, c).wait_recv()
        for h in range(2):
            at = slab1(c, 0, STEPS[i], h)

            def body(rows):
                total = (r1[1, h, i, :, rows].astype(F32) + r1[2, 1 - h, i, :, rows].astype(F32)
                         + part[at[:3] + (rows, lanes(h))].astype(F32))
                if STEPS[i] == 0:
                    tot[:, rows, lanes(h)] = total
                else:
                    part[at[:3] + (rows, lanes(h))] = total.astype(BF16)

            rows16(c, h, body)

    def forward2(d, c):
        msg2(0, d, c).wait_recv()
        at = slab2(c, (1, 3)[d], d)

        def body(rows):
            mine = part[at[:3] + (rows, lanes(d))].astype(F32)
            r2[0, d, :, rows] = (r2[0, d, :, rows].astype(F32) + mine).astype(BF16)

        rows16(c, d, body)
        msg2(1, d, c).start()

    def send1(kind, i, c):
        need(("across", None, "near")[kind], i, c)
        for d in range(2):
            msg1(kind, d, i, c).start()

    for c in range(3):
        send1(0, 0, c)
    gram_step(0)
    for c in range(3):
        send1(2, 0, c)
    gram_step(1)

    for i in range(4):
        for c in range(3):
            for d in range(2):
                forward1(d, i, c)
            if i < 3:
                send1(0, i + 1, c)
        if i < 3:
            if i < 2:
                gram_step((2, 4)[i])
            for c in range(3):
                send1(2, i + 1, c)
        if i > 1:
            inverse_step(3 if i == 2 else 99)
        for c in range(3):
            need("own", i, c)
        for c in range(3):
            finish1(i, c)
            if i == 0:
                for d in range(2):
                    msg2(0, d, c).start()
            elif i < 3:
                d = i - 1
                msg2(2, d, c).start()
                forward2(d, c)
        if i < 2:
            gram_step((3, 5)[i])
        elif i == 2:
            inverse_step(4)

    for c in range(3):
        for d in range(2):
            msg2(2, d, c).wait_recv()
            msg2(1, d, c).wait_recv()
        for h in range(2):
            def body(rows):
                tot[:, rows, lanes(h)] += r2[1, h, :, rows].astype(F32) + r2[2, 1 - h, :, rows].astype(F32)

            rows16(c, h, body)
        for kind in (0, 2):
            for d in range(2):
                msg3(kind, d, c).start()
    for c in range(3):
        for d in range(2):
            msg3(0, d, c).wait_recv()
            f = (me[ORDER[c][2]] + (1, 3)[d]) % 4

            def body(rows):
                r3[0, d, rows] += tot[f, rows, lanes(d)]

            rows16(c, d, body)
            msg3(1, d, c).start()
    for c in range(3):
        for d in range(2):
            msg3(2, d, c).wait_recv()
            msg3(1, d, c).wait_recv()
        mine = me[ORDER[c][2]]
        for h in range(2):
            def body(rows):
                out[rows, lanes(h)] = tot[mine, rows, lanes(h)] + r3[1, h, rows] + r3[2, 1 - h, rows]

            rows16(c, h, body)

    high, low = split(out[...])
    cross = lax.dot_general(high, low, (((1,), (1,)), ((), ())), preferred_element_type=F32)
    s_scratch[0][...] = lax.dot_general(
        high, high, (((1,), (1,)), ((), ())), preferred_element_type=F32) + (cross + cross.T)
    s_phases[0][0]()
    inv_high, inv_low = split(inv[...])
    first_dims = (((0,), (0,)), ((), ()))
    own[...] = (lax.dot_general(high, inv_high, first_dims, preferred_element_type=F32)
                + (lax.dot_general(high, inv_low, first_dims, preferred_element_type=F32)
                   + lax.dot_general(low, inv_high, first_dims, preferred_element_type=F32))).astype(BF16)

    def block(by, k):
        return factor.at[pl.ds(pl.multiple_of((2 * ((me[0] + 4 - by) % 4) + k) * SUB, SUB), SUB)]

    over_x = [pltpu.make_async_remote_copy(
        own, block(0, core), x_s.at[by - 1], x_v.at[by - 1],
        device_id=device(shifted(me, 0, by), core), device_id_type=MESH) for by in (1, 2, 3)]
    over_core = [pltpu.make_async_remote_copy(
        own if by == 0 else block(by, core), block(by, core),
        c_s.at[by], c_v.at[by], device_id=partner, device_id_type=MESH) for by in range(4)]
    own_copy = pltpu.make_async_copy(own, block(0, core), own_sem.at[0])
    s_phases[0][1]()
    s_phases[1][0]()
    for copy in over_x:
        copy.start()
    over_core[0].start()
    own_copy.start()
    s_phases[1][1]()
    for p in range(2, 4):
        s_phases[p][0]()
        s_phases[p][1]()
    s_phases[4][0]()
    for by in (1, 3, 2):
        over_x[by - 1].wait_recv()
        over_core[by].start()
    s_phases[4][1]()
    s_phases[5][0]()
    s_phases[5][1]()
    for by in range(4):
        over_core[by].wait_recv()

    own_copy.wait()
    for copy in over_x + over_core:
        copy.wait_send()
    s_drain()
    for c in range(3):
        for kind in range(3):
            for d in range(2):
                for i in range(4):
                    msg1(kind, d, i, c).wait_send()
                msg2(kind, d, c).wait_send()
                msg3(kind, d, c).wait_send()

    @pl.loop(0, 64)
    def _(t):
        far_copy(t, 0).wait_send()

    gram_drain()


def update_factor(fibers, table_b, table_c, idx_b, idx_c, weight, count):
    cap = fibers.shape[0]
    dma = pltpu.SemaphoreType.DMA
    vmem = pltpu.VMEM
    square = jax.ShapeDtypeStruct((256, 256), F32)
    return pl.pallas_call(
        reduce_kernel,
        name="update_factor",
        out_shape=(jax.ShapeDtypeStruct((8 * SUB, 256), BF16), square, square),
        in_specs=[pl.BlockSpec(memory_space=pl.ANY)] * 3 + [pl.BlockSpec(memory_space=pltpu.VMEM)] * 3
        + [pl.BlockSpec(memory_space=pltpu.SMEM)],
        out_specs=[pl.BlockSpec(memory_space=pl.ANY)] + [pl.BlockSpec(memory_space=pltpu.VMEM)] * 2,
        scratch_shapes=[
            vmem((64, cap, SUB), BF16), vmem((64, cap, SUB), BF16), vmem((256, cap), BF16), vmem((256, cap), BF16),
            vmem((4, 4, 4, 256, SUB), BF16),
            vmem((3, 2, 4, 4, 256, SUB // 2), BF16), vmem((3, 2, 4, 256, SUB // 2), BF16),
            vmem((3, 2, 256, SUB // 2), F32), vmem((4, 256, SUB), F32),
            vmem((256, SUB), F32), vmem((256, 256), F32), vmem((256, 256), F32), vmem((256, 256), F32),
            vmem((SUB, 256), BF16),
            dma((64,)), dma((64,)), dma((64,)), dma((2,)),
            dma((3, 2, 4, 3)), dma((3, 2, 4, 3)), dma((3, 2, 3)), dma((3, 2, 3)), dma((3, 2, 3)), dma((3, 2, 3)),
            dma((1,)), dma((3,)), dma((3,)), dma((4,)), dma((4,)), dma((48,)),
        ] + all_reduce_scratch() * 2,
        compiler_params=pltpu.CompilerParams(
            collective_id=0, has_side_effects=True, vmem_limit_bytes=63 * 1024 * 1024),
    )(fibers, table_b, table_c, idx_b, idx_c, weight, count)


def dot16(a, b):
    return jnp.dot(a.astype(BF16), b.astype(BF16), preferred_element_type=F32)


def invert(a_ref, x_ref, r_ref, between):
    n = a_ref.shape[0]
    row = lax.broadcasted_iota(jnp.int32, (n, n), 0)
    col = lax.broadcasted_iota(jnp.int32, (n, n), 1)
    eye = jnp.where(row == col, F32(1), F32(0))
    a = a_ref[...]
    diag = jnp.where(row == col, a, F32(0))
    s_col = lax.rsqrt(jnp.sum(diag, axis=1, keepdims=True))
    s_row = lax.rsqrt(jnp.sum(diag, axis=0, keepdims=True))
    a_ref[...] = a * s_col * s_row
    bound = jnp.max(jnp.sum(jnp.abs(a_ref[...]), axis=0, keepdims=True))
    alpha = 1.9 / bound
    x_ref[...] = alpha * eye
    r_ref[...] = eye - alpha * a_ref[...]

    def coarse(carry):
        it, _ = carry
        r = r_ref[...]
        x = x_ref[...]
        x_ref[...] = x + dot16(x, r)
        r = dot16(r, r)
        r_ref[...] = r
        return it + 1, jnp.sum(r * r)

    lax.while_loop(lambda c: (c[0] < 24) & (c[1] > 1e-3), coarse, (jnp.int32(0), F32(1e9)))

    between()

    def fine(carry):
        it, last, _ = carry
        x = x_ref[...]
        e = (row == col).astype(F32) - dot32(a_ref[...], x)
        size = jnp.sum(e * e)
        reset = (it == 0) & jnp.logical_not(size < 0.25)
        stop = (size < 1e-6) | ((size < 1e-3) & (size > 0.25 * last))

        @pl.when(reset)
        def _():
            x_ref[...] = alpha * (row == col).astype(F32)

        @pl.when(jnp.logical_not(reset))
        def _():
            x_ref[...] = x + dot32(x, e)

        return it + 1, jnp.where(reset, F32(1e30), size), stop.astype(jnp.int32)

    lax.while_loop(lambda c: (c[0] < 80) & (c[2] == 0), fine, (jnp.int32(0), F32(1e30), jnp.int32(0)))
    x_ref[...] = x_ref[...] * s_col * s_row


def leverage_kernel(scale, factor, smat, shifted_m, out, lev, work, inv, res, rows, held, sem):
    take = pltpu.make_async_copy(factor, held, sem.at[0])
    give = pltpu.make_async_copy(held, out, sem.at[1])
    take.start()

    def pass_on():
        take.wait()
        give.start()

    work[...] = smat[...]
    invert(work, inv, res, pass_on)
    a = shifted_m[...]
    hinv = dot32(a, dot32(inv[...], a))
    high = hinv.astype(BF16)
    low = (hinv - high.astype(F32)).astype(BF16)
    ones = jnp.full((8, 256), 1.0, BF16)
    over = (((1,), (1,)), ((), ()))

    @pl.loop(0, 8)
    def _(j):
        at = pl.ds(pl.multiple_of(j * SUB, SUB), SUB)
        f = held[at]
        quad = (jnp.dot(f, high, preferred_element_type=F32) + jnp.dot(f, low, preferred_element_type=F32)) * f.astype(F32)
        quad = quad[:, :128] + quad[:, 128:]
        q_high = quad.astype(BF16)
        q_low = (quad - q_high.astype(F32)).astype(BF16)
        total = lax.dot_general(ones, jnp.concatenate([q_high, q_low], axis=1), over, preferred_element_type=F32)
        for k in range(SUB // 128):
            rows[pl.ds(j * (SUB // 128) + k, 1)] = total[0:1, 128 * k:128 * (k + 1)]

    lev[...] = (scale * rows[...]).astype(BF16)
    give.wait()


def leverage_of(factor, smat, shifted_m, scale):
    rows = factor.shape[0]
    out, lev = pl.pallas_call(
        lambda *refs: leverage_kernel(scale, *refs), name="leverage",
        out_shape=(jax.ShapeDtypeStruct((rows, 256), BF16), jax.ShapeDtypeStruct((rows // 128, 128), BF16)),
        in_specs=[pl.BlockSpec(memory_space=pl.ANY)] + [pl.BlockSpec(memory_space=pltpu.VMEM)] * 2,
        out_specs=[pl.BlockSpec(memory_space=pl.ANY), pl.BlockSpec(memory_space=pltpu.VMEM)],
        scratch_shapes=[pltpu.VMEM((256, 256), F32)] * 3 + [
            pltpu.VMEM((rows // 128, 128), F32), pltpu.VMEM((rows, 256), BF16), pltpu.SemaphoreType.DMA((2,))],
    )(factor, smat, shifted_m)
    return out, lev.reshape(rows)


def local(fibers, factor_b, factor_c, mode2_idx, mode3_idx, sample_wt, counts):
    slot_cap, row_total = fibers.shape
    rank_width = factor_c.shape[1]
    row = (1, slot_cap)
    factor, ssum, shifted_m = update_factor(
        fibers, factor_b, factor_c, mode2_idx.reshape(row), mode3_idx.reshape(row), sample_wt.reshape(row), counts)
    return leverage_of(factor, ssum, shifted_m, row_total / rank_width)


def solution(mesh):
    placed = (
        P(("blk", "row"), None),
        P("blk", None),
        P(),
        P(("blk", "row")),
        P(("blk", "row")),
        P(("blk", "row")),
        P(("blk", "row")),
    )
    return jax.shard_map(
        local, mesh=mesh, in_specs=placed, out_specs=(P("row", None), P("row")), check_vma=False
    )
```

```python
import jax
import jax.numpy as jnp
from jax import lax
from jax.experimental import pallas as pl
from jax.experimental.pallas import tpu as pltpu
from jax.sharding import PartitionSpec as P

ridge_share = 0.05
MESH = pl.DeviceIdType.MESH
F32 = jnp.float32
BF16 = jnp.bfloat16

ORDER = ((0, 1, 2), (1, 2, 0), (2, 0, 1))
R0 = ((0, 96, 176), (0, 80, 176))
RC = ((96, 80, 80), (80, 96, 80))
STEPS = (2, 1, 3, 0)
SUB = 512


def block_lines(kind, i, color):
    d2 = STEPS[i]
    lines = []
    for d1 in {"across": (2,), "near": (1, 3), "own": (0,)}[kind]:
        for d3 in range(4):
            off = [0, 0, 0]
            off[ORDER[color][0]], off[ORDER[color][1]], off[ORDER[color][2]] = d1, d2, d3
            lines.append(tuple(off))
    return lines


def block_order():
    order, ends = [], {}
    needs = [("across", 0), ("near", 0), ("across", 1), ("near", 1), ("own", 0)]
    for i in (2, 3):
        needs += [("across", i), ("near", i), ("own", i - 1)]
    needs += [("own", 3)]
    for kind, i in needs:
        for color in range(3):
            for off in block_lines(kind, i, color):
                if off not in order:
                    order.append(off)
            ends[kind, i, color] = len(order)
    return order, ends


BLOCKS, ENDS = block_order()
PACK = 5
AHEAD = 8


def block_at(t, me):
    code = jnp.int32(0)
    for g in range(0, 64, PACK):
        word = 0
        for j, (dx, dy, dz) in enumerate(BLOCKS[g:g + PACK]):
            word += (dx + 4 * dy + 16 * dz) << (6 * j)
        code = jnp.where(t // PACK == g // PACK, jnp.int32(word), code)
    code = lax.shift_right_logical(code, 6 * (t % PACK)) % 64
    return ((me[0] + code % 4) % 4, (me[1] + code // 4 % 4) % 4, (me[2] + code // 16) % 4)


def position():
    b, r = lax.axis_index("blk"), lax.axis_index("row")
    return (b // 2, r % 4, r // 4), b % 2


def device(coord, core):
    return {"blk": 2 * coord[0] + core, "row": 4 * coord[2] + coord[1]}


def shifted(me, axis, by):
    out = list(me)
    out[axis] = (me[axis] + by) % 4
    return tuple(out)


def all_reduce_phases(part, res, near, rx, ry, mid, rz, far_s, far_v, snd, rcv, me, core):
    half = core * 128
    row_x = half + 32 * me[0]
    partner = device(me, 1 - core)

    def rows(at, n):
        return pl.ds(pl.multiple_of(at, 8), n)

    def spread(phase, axis, src_of, dst_of):
        copies = []
        for by in (1, 2, 3):
            to = shifted(me, axis, by)
            copies.append(pltpu.make_async_remote_copy(
                src_of(to[axis]), dst_of(by), snd.at[phase, by - 1], rcv.at[phase, by - 1],
                device_id=device(to, core), device_id_type=MESH))
        return copies

    def pair(slot, src, dst):
        return pltpu.make_async_remote_copy(
            src, dst, far_s.at[slot], far_v.at[slot], device_id=partner, device_id_type=MESH)

    def begin(copies):
        for copy in copies:
            copy.start()

    def arrive(copies):
        for copy in copies:
            copy.wait_recv()

    first = [pair(0, part.at[rows((1 - core) * 128, 128)], near)]
    over_x = spread(0, 0, lambda i: part.at[rows(half + 32 * i, 32)], lambda by: rx.at[by - 1])
    over_y = spread(1, 1, lambda i: part.at[rows(row_x, 32)], lambda by: ry.at[me[1]])
    over_z = spread(2, 2, lambda i: mid, lambda by: rz.at[me[2]])
    back_x = spread(3, 0, lambda i: res.at[rows(row_x, 32)], lambda by: res.at[rows(row_x, 32)])
    last = [pair(1, res.at[rows(half, 128)], res.at[rows(half, 128)])]

    def end_core():
        arrive(first)
        part[rows(half, 128)] += near[...]

    def end_x():
        arrive(over_x)
        part[rows(row_x, 32)] += rx[0] + rx[1] + rx[2]

    def end_y():
        arrive(over_y)
        ry[me[1]] = part[rows(row_x, 32)]
        mid[...] = (ry[0] + ry[1]) + (ry[2] + ry[3])

    def end_z():
        arrive(over_z)
        rz[me[2]] = mid[...]
        res[rows(row_x, 32)] = (rz[0] + rz[1]) + (rz[2] + rz[3])

    stages = [(first, end_core), (over_x, end_x), (over_y, end_y), (over_z, end_z),
              (back_x, lambda: arrive(back_x)), (last, lambda: arrive(last))]

    def drain():
        for copies, _ in stages:
            for copy in copies:
                copy.wait_send()

    return [(lambda c=copies: begin(c), end) for copies, end in stages], drain


def all_reduce_scratch():
    dma = pltpu.SemaphoreType.DMA
    return [pltpu.VMEM((256, 256), F32), pltpu.VMEM((128, 256), F32), pltpu.VMEM((3, 32, 256), F32),
            pltpu.VMEM((4, 32, 256), F32), pltpu.VMEM((32, 256), F32), pltpu.VMEM((4, 32, 256), F32),
            dma((2,)), dma((2,)), dma((4, 3)), dma((4, 3))]


def greet(peers):
    barrier = pltpu.get_barrier_semaphore()
    for p in peers:
        pl.semaphore_signal(barrier, inc=1, device_id=p, device_id_type=MESH)
    return lambda: pl.semaphore_wait(barrier, len(peers))


def split(value):
    high = value.astype(BF16)
    return high, (value - high.astype(F32)).astype(BF16)


def all_peers(me, core):
    return [device(shifted(me, a, s), core) for a in range(3) for s in (1, 2, 3)] + [device(me, 1 - core)]


def dot32(a, b):
    return jnp.dot(a, b, precision=lax.Precision.HIGHEST, preferred_element_type=F32)


def ridge_inverse_steps(gram, shifted_m, x, r):
    n = gram.shape[0]
    low = ridge_share / n / (1 + ridge_share)
    bound = (1 - low) / (1 + low)
    first = 2 / (1 + low)

    def eye():
        row = lax.broadcasted_iota(jnp.int32, (n, n), 0)
        col = lax.broadcasted_iota(jnp.int32, (n, n), 1)
        return jnp.where(row == col, F32(1), F32(0))

    def inverse_trace():
        return 1.0 / jnp.sum(jnp.sum(shifted_m[...] * eye(), axis=0, keepdims=True), axis=1, keepdims=True)

    def begin():
        g = gram[...]
        one = eye()
        g = 0.5 * (g + g.T)
        trace = jnp.sum(jnp.sum(g * one, axis=0, keepdims=True), axis=1, keepdims=True)
        shifted_m[...] = g + one * (trace * (ridge_share / n))
        x[...] = first * one
        r[...] = one - shifted_m[...] * (inverse_trace() * first)

    def square(scale):
        def step():
            res = r[...]
            x[...] = scale * (x[...] + dot32(x[...], res))
            r[...] = (1 - scale) * eye() + scale * dot32(res, res)

        return step

    def correct(last):
        def step():
            scale = inverse_trace()
            err = eye() - dot32(shifted_m[...] * scale, x[...])
            new = x[...] + dot32(x[...], err)
            x[...] = new * scale if last else new

        return step

    steps = [begin]
    while bound > 1e-2:
        scale = 2 / (2 - bound * bound)
        steps.append(square(scale))
        bound = bound * bound / (2 - bound * bound)
    return steps + [correct(False), correct(False), correct(True)]


def reduce_kernel(fib, table_b, table_c, idx_b, idx_c, weight, count, factor, ssum, shifted_m,
                  fo, fp, wt_own, wt_far, part, r1, r2, r3, tot, out, gram, inv, res, own,
                  fo_sem, fs_sem, fr_sem, w_sem, s1, v1, s2, v2, s3, v3, own_sem, x_s, x_v, c_s, c_v, t_sem, *sums):
    gram_scratch, s_scratch = sums[:10], sums[10:]
    me, core = position()
    all_entered = greet(all_peers(me, core))
    chunks_b, chunks_c = table_b.shape[0] // 256, table_c.shape[0] // 256

    def chunk_slot(i):
        return (i // 16, i // 4 % 4, i % 4, slice(None), pl.ds(0, 256))

    def load_chunk(table, i, first):
        rows = pl.ds(pl.multiple_of(256 * i, 256), 256)
        return pltpu.make_async_copy(table.at[rows], part.at[chunk_slot(first + i)], t_sem.at[first + i])

    for table, count_of, first in ((table_b, chunks_b, 0), (table_c, chunks_c, chunks_b)):
        @pl.loop(0, count_of)
        def _(i):
            load_chunk(table, i, first).start()
    partner = device(me, 1 - core)

    near = [[(me[a] + by) % 4 for by in range(4)] for a in range(3)]
    bases = [near[1][by] * 4096 for by in range(4)], [near[2][by] * 16384 for by in range(4)]

    def column(t, k):
        dx, dy, dz = BLOCKS[t]
        return pl.multiple_of(bases[1][dz] + bases[0][dy] + near[0][dx] * 1024 + k * SUB, SUB)

    def local_copy(t, at):
        return pltpu.make_async_copy(fib.at[:, pl.ds(at, SUB)], fo.at[t], fo_sem.at[t])

    def far_copy(t, at):
        return pltpu.make_async_remote_copy(
            fib.at[:, pl.ds(at, SUB)], fp.at[t], fs_sem.at[t], fr_sem.at[t],
            device_id=partner, device_id_type=MESH)

    wt_copy = pltpu.make_async_remote_copy(
        wt_own, wt_far, w_sem.at[0], w_sem.at[1], device_id=partner, device_id_type=MESH)
    gram_phases, gram_drain = all_reduce_phases(gram_scratch[0], gram, *gram_scratch[1:], me, core)

    s_phases, s_drain = all_reduce_phases(s_scratch[0], ssum, *s_scratch[1:], me, core)
    inverse_steps = ridge_inverse_steps(gram, shifted_m, inv, res)

    def inverse_step(count):
        for _ in range(min(count, len(inverse_steps))):
            inverse_steps.pop(0)()

    def gram_step(p):
        gram_phases[p][1]()
        if p < 5:
            gram_phases[p + 1][0]()

    for t in range(64):
        local_copy(t, column(t, core)).start()

    cap = weight.shape[1]
    lane = lax.broadcasted_iota(jnp.int32, (cap, 256), 1).astype(F32)
    diagonal = lax.broadcasted_iota(jnp.int32, (cap, cap), 0) == lax.broadcasted_iota(jnp.int32, (cap, cap), 1)

    def gather_rows(table, idx, chunks, first):
        at = jnp.sum(jnp.where(diagonal, idx[...].astype(F32), F32(0)), axis=1, keepdims=True)

        def body(i, total):
            load_chunk(table, i, first).wait()
            hot = jnp.where(at == lane + (256 * i).astype(F32), F32(1), F32(0)).astype(BF16)
            return total + jnp.dot(hot, part[chunk_slot(first + i)], preferred_element_type=F32)

        return lax.fori_loop(0, chunks, body, jnp.zeros((cap, 256), F32), unroll=8)

    kr = (gather_rows(table_b, idx_b, chunks_b, 0) * gather_rows(table_c, idx_c, chunks_c, chunks_b)).astype(BF16)
    slot = lax.broadcasted_iota(jnp.int32, (1, cap), 1)
    scale = jnp.where(slot < count[0], weight[...].astype(F32), F32(0))
    wt_own[...] = (scale * kr.T.astype(F32)).astype(BF16)
    gram_scratch[0][...] = jnp.dot(wt_own[...], kr, preferred_element_type=F32)

    all_entered()
    wt_copy.start()
    gram_phases[0][0]()

    far_started = [0]

    def start_far(upto):
        for t in range(far_started[0], min(upto, 64)):
            far_copy(t, column(t, 1 - core)).start()
        far_started[0] = max(far_started[0], min(upto, 64))

    start_far(ENDS["across", 0, 2])
    wt_copy.wait()

    done = [0]

    def need(kind, i, c):
        lo, hi = done[0], ENDS[kind, i, c]
        if hi <= lo:
            return
        done[0] = hi
        start_far(hi + AHEAD)

        @pl.loop(lo, hi)
        def _(t):
            local_copy(t, 0).wait()
            far_copy(t, 0).wait_recv()
            x, y, z = block_at(t, me)
            acc = jnp.dot(wt_own[...], fo[t], preferred_element_type=F32)
            acc += jnp.dot(wt_far[...], fp[t], preferred_element_type=F32)
            part[x, y, z] = acc.astype(BF16)

    def rank(c, h):
        return pl.ds(R0[h][c], RC[h][c])

    def lanes(h):
        return pl.ds(h * (SUB // 2), SUB // 2)

    def place(c, i1, i2, i3):
        at = [None] * 3
        at[ORDER[c][0]], at[ORDER[c][1]], at[ORDER[c][2]] = i1, i2, i3
        return tuple(at)

    def half_of(kind, d):
        return d if kind < 2 else 1 - d

    def dest_step(kind, d):
        return 2 if kind == 0 else (1, 3)[d]

    def slab1(c, d1, e, h):
        i1 = (me[ORDER[c][0]] + d1) % 4
        i2 = (me[ORDER[c][1]] + e) % 4
        return place(c, i1, i2, slice(None)) + (rank(c, h), lanes(h))

    def msg1(kind, d, i, c):
        h = half_of(kind, d)
        if kind == 1:
            src = r1.at[0, d, i, :, rank(c, h)]
        else:
            src = part.at[slab1(c, dest_step(kind, d), STEPS[i], h)]
        return pltpu.make_async_remote_copy(
            src, r1.at[kind, d, i, :, rank(c, h)], s1.at[kind, d, i, c], v1.at[kind, d, i, c],
            device_id=device(shifted(me, ORDER[c][0], (1, 3)[d]), core), device_id_type=MESH)

    def slab2(c, e, h):
        return slab1(c, 0, e, h)

    def msg2(kind, d, c):
        h = half_of(kind, d)
        if kind == 1:
            src = r2.at[0, d, :, rank(c, h)]
        else:
            src = part.at[slab2(c, dest_step(kind, d), h)]
        return pltpu.make_async_remote_copy(
            src, r2.at[kind, d, :, rank(c, h)], s2.at[kind, d, c], v2.at[kind, d, c],
            device_id=device(shifted(me, ORDER[c][1], (1, 3)[d]), core), device_id_type=MESH)

    def msg3(kind, d, c):
        h = half_of(kind, d)
        if kind == 1:
            src = r3.at[0, d, rank(c, h)]
        else:
            f = (me[ORDER[c][2]] + dest_step(kind, d)) % 4
            src = tot.at[f, rank(c, h), lanes(h)]
        return pltpu.make_async_remote_copy(
            src, r3.at[kind, d, rank(c, h)], s3.at[kind, d, c], v3.at[kind, d, c],
            device_id=device(shifted(me, ORDER[c][2], (1, 3)[d]), core), device_id_type=MESH)

    def rows16(c, h, body):
        @pl.loop(0, RC[h][c] // 16)
        def _(j):
            body(pl.ds(pl.multiple_of(R0[h][c] + 16 * j, 16), 16))

    def forward1(d, i, c):
        msg1(0, d, i, c).wait_recv()
        at = slab1(c, (1, 3)[d], STEPS[i], d)

        def body(rows):
            mine = part[at[:3] + (rows, lanes(d))].astype(F32)
            r1[0, d, i, :, rows] = (r1[0, d, i, :, rows].astype(F32) + mine).astype(BF16)

        rows16(c, d, body)
        msg1(1, d, i, c).start()

    def finish1(i, c):
        for d in range(2):
            msg1(2, d, i, c).wait_recv()
        for d in range(2):
            msg1(1, d, i, c).wait_recv()
        for h in range(2):
            at = slab1(c, 0, STEPS[i], h)

            def body(rows):
                total = (r1[1, h, i, :, rows].astype(F32) + r1[2, 1 - h, i, :, rows].astype(F32)
                         + part[at[:3] + (rows, lanes(h))].astype(F32))
                if STEPS[i] == 0:
                    tot[:, rows, lanes(h)] = total
                else:
                    part[at[:3] + (rows, lanes(h))] = total.astype(BF16)

            rows16(c, h, body)

    def forward2(d, c):
        msg2(0, d, c).wait_recv()
        at = slab2(c, (1, 3)[d], d)

        def body(rows):
            mine = part[at[:3] + (rows, lanes(d))].astype(F32)
            r2[0, d, :, rows] = (r2[0, d, :, rows].astype(F32) + mine).astype(BF16)

        rows16(c, d, body)
        msg2(1, d, c).start()

    def send1(kind, i, c):
        need(("across", None, "near")[kind], i, c)
        for d in range(2):
            msg1(kind, d, i, c).start()

    for c in range(3):
        send1(0, 0, c)
    gram_step(0)
    for c in range(3):
        send1(2, 0, c)
    gram_step(1)

    for i in range(4):
        for c in range(3):
            for d in range(2):
                forward1(d, i, c)
            if i < 3:
                send1(0, i + 1, c)
        if i < 3:
            if i < 2:
                gram_step((2, 4)[i])
            for c in range(3):
                send1(2, i + 1, c)
        if i > 1:
            inverse_step(3 if i == 2 else 99)
        for c in range(3):
            need("own", i, c)
        for c in range(3):
            finish1(i, c)
            if i == 0:
                for d in range(2):
                    msg2(0, d, c).start()
            elif i < 3:
                d = i - 1
                msg2(2, d, c).start()
                forward2(d, c)
        if i < 2:
            gram_step((3, 5)[i])
        elif i == 2:
            inverse_step(4)

    for c in range(3):
        for d in range(2):
            msg2(2, d, c).wait_recv()
            msg2(1, d, c).wait_recv()
        for h in range(2):
            def body(rows):
                tot[:, rows, lanes(h)] += r2[1, h, :, rows].astype(F32) + r2[2, 1 - h, :, rows].astype(F32)

            rows16(c, h, body)
        for kind in (0, 2):
            for d in range(2):
                msg3(kind, d, c).start()
    for c in range(3):
        for d in range(2):
            msg3(0, d, c).wait_recv()
            f = (me[ORDER[c][2]] + (1, 3)[d]) % 4

            def body(rows):
                r3[0, d, rows] += tot[f, rows, lanes(d)]

            rows16(c, d, body)
            msg3(1, d, c).start()
    for c in range(3):
        for d in range(2):
            msg3(2, d, c).wait_recv()
            msg3(1, d, c).wait_recv()
        mine = me[ORDER[c][2]]
        for h in range(2):
            def body(rows):
                out[rows, lanes(h)] = tot[mine, rows, lanes(h)] + r3[1, h, rows] + r3[2, 1 - h, rows]

            rows16(c, h, body)

    high, low = split(out[...])
    cross = lax.dot_general(high, low, (((1,), (1,)), ((), ())), preferred_element_type=F32)
    s_scratch[0][...] = lax.dot_general(
        high, high, (((1,), (1,)), ((), ())), preferred_element_type=F32) + (cross + cross.T)
    s_phases[0][0]()
    inv_high, inv_low = split(inv[...])
    first_dims = (((0,), (0,)), ((), ()))
    own[...] = (lax.dot_general(high, inv_high, first_dims, preferred_element_type=F32)
                + (lax.dot_general(high, inv_low, first_dims, preferred_element_type=F32)
                   + lax.dot_general(low, inv_high, first_dims, preferred_element_type=F32))).astype(BF16)

    def block(by, k):
        return factor.at[pl.ds(pl.multiple_of((2 * ((me[0] + 4 - by) % 4) + k) * SUB, SUB), SUB)]

    over_x = [pltpu.make_async_remote_copy(
        own, block(0, core), x_s.at[by - 1], x_v.at[by - 1],
        device_id=device(shifted(me, 0, by), core), device_id_type=MESH) for by in (1, 2, 3)]
    over_core = [pltpu.make_async_remote_copy(
        own if by == 0 else block(by, core), block(by, core),
        c_s.at[by], c_v.at[by], device_id=partner, device_id_type=MESH) for by in range(4)]
    own_copy = pltpu.make_async_copy(own, block(0, core), own_sem.at[0])
    s_phases[0][1]()
    s_phases[1][0]()
    for copy in over_x:
        copy.start()
    over_core[0].start()
    own_copy.start()
    s_phases[1][1]()
    for p in range(2, 4):
        s_phases[p][0]()
        s_phases[p][1]()
    s_phases[4][0]()
    for by in (1, 3, 2):
        over_x[by - 1].wait_recv()
        over_core[by].start()
    s_phases[4][1]()
    s_phases[5][0]()
    s_phases[5][1]()
    for by in range(4):
        over_core[by].wait_recv()

    own_copy.wait()
    for copy in over_x + over_core:
        copy.wait_send()
    s_drain()
    for c in range(3):
        for kind in range(3):
            for d in range(2):
                for i in range(4):
                    msg1(kind, d, i, c).wait_send()
                msg2(kind, d, c).wait_send()
                msg3(kind, d, c).wait_send()

    @pl.loop(0, 64)
    def _(t):
        far_copy(t, 0).wait_send()

    gram_drain()


def update_factor(fibers, table_b, table_c, idx_b, idx_c, weight, count):
    cap = fibers.shape[0]
    dma = pltpu.SemaphoreType.DMA
    vmem = pltpu.VMEM
    square = jax.ShapeDtypeStruct((256, 256), F32)
    return pl.pallas_call(
        reduce_kernel,
        name="update_factor",
        out_shape=(jax.ShapeDtypeStruct((8 * SUB, 256), BF16), square, square),
        in_specs=[pl.BlockSpec(memory_space=pl.ANY)] * 3 + [pl.BlockSpec(memory_space=pltpu.VMEM)] * 3
        + [pl.BlockSpec(memory_space=pltpu.SMEM)],
        out_specs=[pl.BlockSpec(memory_space=pl.ANY)] + [pl.BlockSpec(memory_space=pltpu.VMEM)] * 2,
        scratch_shapes=[
            vmem((64, cap, SUB), BF16), vmem((64, cap, SUB), BF16), vmem((256, cap), BF16), vmem((256, cap), BF16),
            vmem((4, 4, 4, 256, SUB), BF16),
            vmem((3, 2, 4, 4, 256, SUB // 2), BF16), vmem((3, 2, 4, 256, SUB // 2), BF16),
            vmem((3, 2, 256, SUB // 2), F32), vmem((4, 256, SUB), F32),
            vmem((256, SUB), F32), vmem((256, 256), F32), vmem((256, 256), F32), vmem((256, 256), F32),
            vmem((SUB, 256), BF16),
            dma((64,)), dma((64,)), dma((64,)), dma((2,)),
            dma((3, 2, 4, 3)), dma((3, 2, 4, 3)), dma((3, 2, 3)), dma((3, 2, 3)), dma((3, 2, 3)), dma((3, 2, 3)),
            dma((1,)), dma((3,)), dma((3,)), dma((4,)), dma((4,)), dma((48,)),
        ] + all_reduce_scratch() * 2,
        compiler_params=pltpu.CompilerParams(
            collective_id=0, has_side_effects=True, vmem_limit_bytes=63 * 1024 * 1024),
    )(fibers, table_b, table_c, idx_b, idx_c, weight, count)


def dot16(a, b):
    return jnp.dot(a.astype(BF16), b.astype(BF16), preferred_element_type=F32)


def invert(a_ref, x_ref, r_ref, between):
    n = a_ref.shape[0]
    row = lax.broadcasted_iota(jnp.int32, (n, n), 0)
    col = lax.broadcasted_iota(jnp.int32, (n, n), 1)
    eye = jnp.where(row == col, F32(1), F32(0))
    a = a_ref[...]
    diag = jnp.where(row == col, a, F32(0))
    s_col = lax.rsqrt(jnp.sum(diag, axis=1, keepdims=True))
    s_row = lax.rsqrt(jnp.sum(diag, axis=0, keepdims=True))
    a_ref[...] = a * s_col * s_row
    bound = jnp.max(jnp.sum(jnp.abs(a_ref[...]), axis=0, keepdims=True))
    alpha = 1.9 / bound
    x_ref[...] = alpha * eye
    r_ref[...] = eye - alpha * a_ref[...]

    def coarse(carry):
        it, _ = carry
        r = r_ref[...]
        x = x_ref[...]
        x_ref[...] = x + dot16(x, r)
        r = dot16(r, r)
        r_ref[...] = r
        return it + 1, jnp.sum(r * r)

    lax.while_loop(lambda c: (c[0] < 24) & (c[1] > 1e-3), coarse, (jnp.int32(0), F32(1e9)))

    between()

    def fine(carry):
        it, last, _ = carry
        x = x_ref[...]
        e = (row == col).astype(F32) - dot32(a_ref[...], x)
        size = jnp.sum(e * e)
        reset = (it == 0) & jnp.logical_not(size < 0.25)
        stop = (size < 1e-6) | ((size < 1e-3) & (size > 0.25 * last))

        @pl.when(reset)
        def _():
            x_ref[...] = alpha * (row == col).astype(F32)

        @pl.when(jnp.logical_not(reset))
        def _():
            x_ref[...] = x + dot32(x, e)

        return it + 1, jnp.where(reset, F32(1e30), size), stop.astype(jnp.int32)

    lax.while_loop(lambda c: (c[0] < 80) & (c[2] == 0), fine, (jnp.int32(0), F32(1e30), jnp.int32(0)))
    x_ref[...] = x_ref[...] * s_col * s_row


def leverage_kernel(scale, factor, smat, shifted_m, out, lev, work, inv, res, rows, held, sem):
    take = pltpu.make_async_copy(factor, held, sem.at[0])
    give = pltpu.make_async_copy(held, out, sem.at[1])
    take.start()

    def pass_on():
        take.wait()
        give.start()

    work[...] = smat[...]
    invert(work, inv, res, pass_on)
    a = shifted_m[...]
    hinv = dot32(a, dot32(inv[...], a))
    high = hinv.astype(BF16)
    low = (hinv - high.astype(F32)).astype(BF16)
    ones = jnp.full((8, 256), 1.0, BF16)
    over = (((1,), (1,)), ((), ()))

    @pl.loop(0, 8)
    def _(j):
        at = pl.ds(pl.multiple_of(j * SUB, SUB), SUB)
        f = held[at]
        quad = (jnp.dot(f, high, preferred_element_type=F32) + jnp.dot(f, low, preferred_element_type=F32)) * f.astype(F32)
        quad = quad[:, :128] + quad[:, 128:]
        q_high = quad.astype(BF16)
        q_low = (quad - q_high.astype(F32)).astype(BF16)
        total = lax.dot_general(ones, jnp.concatenate([q_high, q_low], axis=1), over, preferred_element_type=F32)
        for k in range(SUB // 128):
            rows[pl.ds(j * (SUB // 128) + k, 1)] = total[0:1, 128 * k:128 * (k + 1)]

    lev[...] = (scale * rows[...]).astype(BF16)
    give.wait()


def leverage_of(factor, smat, shifted_m, scale):
    rows = factor.shape[0]
    out, lev = pl.pallas_call(
        lambda *refs: leverage_kernel(scale, *refs), name="leverage",
        out_shape=(jax.ShapeDtypeStruct((rows, 256), BF16), jax.ShapeDtypeStruct((rows // 128, 128), BF16)),
        in_specs=[pl.BlockSpec(memory_space=pl.ANY)] + [pl.BlockSpec(memory_space=pltpu.VMEM)] * 2,
        out_specs=[pl.BlockSpec(memory_space=pl.ANY), pl.BlockSpec(memory_space=pltpu.VMEM)],
        scratch_shapes=[pltpu.VMEM((256, 256), F32)] * 3 + [
            pltpu.VMEM((rows // 128, 128), F32), pltpu.VMEM((rows, 256), BF16), pltpu.SemaphoreType.DMA((2,))],
    )(factor, smat, shifted_m)
    return out, lev.reshape(rows)


def local(fibers, factor_b, factor_c, mode2_idx, mode3_idx, sample_wt, counts):
    slot_cap, row_total = fibers.shape
    rank_width = factor_c.shape[1]
    row = (1, slot_cap)
    factor, ssum, shifted_m = update_factor(
        fibers, factor_b, factor_c, mode2_idx.reshape(row), mode3_idx.reshape(row), sample_wt.reshape(row), counts)
    return leverage_of(factor, ssum, shifted_m, row_total / rank_width)


def solution(mesh):
    placed = (
        P(("blk", "row"), None),
        P("blk", None),
        P(),
        P(("blk", "row")),
        P(("blk", "row")),
        P(("blk", "row")),
        P(("blk", "row")),
    )
    return jax.shard_map(
        local, mesh=mesh, in_specs=placed, out_specs=(P("row", None), P("row")), check_vma=False
    )
```
